32 devices in a mesh: fsdp: 2 (over y), ctx: 4 (over x, core), tp: 4 (over z).
Axes of the slice: x: 2, y: 2, z: 4, core: 2. Of those that a mesh axis runs over, the one named last changes fastest.
Arguments:
- inputs: bfloat16 [16, 1024, 768], P('fsdp', ('ctx', 'tp')), may hold values from -6 to 6
- norm1_gain: float32 [768], replicated, may hold values from 0.5 to 1.5
- norm1_bias: float32 [768], replicated, may hold values from -1.5 to 1.5
- qkv_weight: bfloat16 [768, 3, 768], P(('fsdp', 'ctx'), None, 'tp'), may hold values from -0.3125 to 0.3125
- qv_bias: float32 [2, 768], P(None, 'tp'), may hold values from -1.5 to 1.5
- score_weight: bfloat16 [768, 12], P(('fsdp', 'ctx'), 'tp'), may hold values from -0.21875 to 0.21875
- out_weight: bfloat16 [768, 768], P(('fsdp', 'ctx'), 'tp'), may hold values from -0.3125 to 0.3125
- out_bias: float32 [768], replicated, may hold values from -1.5 to 1.5
- norm2_gain: float32 [768], replicated, may hold values from 0.5 to 1.5
- norm2_bias: float32 [768], replicated, may hold values from -1.5 to 1.5
- fc1_weight: bfloat16 [768, 3072], P(('fsdp', 'ctx'), 'tp'), may hold values from -0.21875 to 0.21875
- fc1_bias: float32 [3072], P('tp'), may hold values from -1.5 to 1.5
- fc2_weight: bfloat16 [768, 3072], P(('fsdp', 'ctx'), 'tp'), may hold values from -0.15625 to 0.15625
- fc2_bias: float32 [768], replicated, may hold values from -1.5 to 1.5
- prefix: int32 [16], P('fsdp'), may hold values from 102 to 512
- selected: int32 [16, 16, 4], P('fsdp', 'ctx'), may hold values from 0 to 63, all different within a row
- cotangent: bfloat16 [16, 1024, 768], P('fsdp', ('ctx', 'tp')), may hold values from -6 to 6
Outputs:
- result: bfloat16 [16, 1024, 768], P('fsdp', ('ctx', 'tp'))
- input_grad: bfloat16 [16, 1024, 768], P('fsdp', ('ctx', 'tp'))
- norm1_gain_grad: float32 [768], replicated
- norm1_bias_grad: float32 [768], replicated
- qkv_weight_grad: float32 [768, 3, 768], P(('fsdp', 'ctx'), None, 'tp')
- qv_bias_grad: float32 [2, 768], P(None, 'tp')
- score_weight_grad: float32 [768, 12], P(('fsdp', 'ctx'), 'tp')
- out_weight_grad: float32 [768, 768], P(('fsdp', 'ctx'), 'tp')
- out_bias_grad: float32 [768], replicated
- norm2_gain_grad: float32 [768], replicated
- norm2_bias_grad: float32 [768], replicated
- fc1_weight_grad: float32 [768, 3072], P(('fsdp', 'ctx'), 'tp')
- fc1_bias_grad: float32 [3072], P('tp')
- fc2_weight_grad: float32 [768, 3072], P(('fsdp', 'ctx'), 'tp')
- fc2_bias_grad: float32 [768], replicated
The draws below stay inside these ranges and needn't reach their ends.
Inputs may be any that keep to these rules, and one draw needn't show every extreme that they name: `selected`: the 4 key blocks of each query block are distinct.
All inputs are finite; a program needn't handle non-finite values.
Results may differ from the reference program's by a relative error of at most 0.018.
Values may be sent and summed in bfloat16 or wider, within the bound.
A program may use at most 320 MiB of HBM per device.

```python
import jax
import jax.numpy as jnp
from jax import lax

D = 768
H = 12
HD = 64
FF = 3072
SEQ_LEN = 1024
QB = 64
KB = 16
SEL = 4
WIN = 64
SEQ_MB = 4
HH = 768
NQB = 16
NKB = 64
SEQS = 16


def touch_ends(drawn, key, least, top_value):
    place = [jax.random.randint(jax.random.fold_in(key, axis), (), 0, length) for axis, length in enumerate(drawn.shape)]
    main_axis = drawn.shape.index(max(drawn.shape))
    next_to = place[:main_axis] + [(place[main_axis] + 1) % drawn.shape[main_axis]] + place[main_axis + 1:]
    return drawn.at[tuple(place)].set(least).at[tuple(next_to)].set(top_value)


def block_scale(own_key, extent, cuts, low, top_value):
    loudness, own = 1.0, jax.random.fold_in(own_key, 6)
    for position, parts in cuts:
        draws = jnp.exp(jax.random.uniform(jax.random.fold_in(own, position), (parts,), jnp.float32, low / len(cuts), top_value / len(cuts)))
        loudness = loudness * jnp.repeat(draws, extent[position] // parts).reshape([-1 if axis == position else 1 for axis in range(len(extent))])
    return loudness


def picks_of(own_key, rows, count, top, lift):
    sequence = jax.random.permutation(jax.random.fold_in(own_key, 1), count)
    favour = sequence
    for power in range(3):
        favour = favour * favour // count
    favour = favour * lift // count
    chance = jax.random.randint(jax.random.fold_in(own_key, 2), (rows, count), 0, 4096) + favour
    holders = jax.random.permutation(jax.random.fold_in(own_key, 3), rows)[jnp.arange(count) % rows]
    chance = jnp.where(jnp.arange(rows)[:, None] == holders[None, :], 1 << 14, chance)
    priority = chance * count + jnp.arange(count)
    return lax.top_k(priority.astype(jnp.int32), top)[1].astype(jnp.int32)


def gaussian(rng, extent, scale, most, shards=(), kind=jnp.bfloat16):
    level = block_scale(rng, extent, shards, -0.22, 0.18) if shards else 1.0
    drawn = jax.random.normal(rng, extent, jnp.float32) * scale * level
    return jnp.minimum(jnp.maximum(drawn, -most), most).astype(kind)


def setup_inputs(seed: int = 0) -> dict:
    key_list = jax.random.split(jax.random.key(seed), 18)
    inputs = gaussian(key_list[0], (SEQS, SEQ_LEN, D), 1.0, 6.0, ((0, 2), (1, 16)))
    norm1_gain = jnp.clip(1.0 + 0.1 * jax.random.normal(key_list[1], (D,), jnp.float32), 0.5, 1.5)
    norm1_bias = gaussian(key_list[2], (D,), 0.3, 1.5, (), jnp.float32)
    qkv_weight = gaussian(key_list[3], (D, 3, HH), (D // 2) ** -0.5, 0.3125, ((0, 8), (2, 4)))
    qv_bias = gaussian(key_list[4], (2, HH), 0.3, 1.5, ((1, 4),), jnp.float32)
    score_weight = gaussian(key_list[5], (D, H), D ** -0.5, 0.21875, ((0, 8), (1, 4)))
    out_weight = gaussian(key_list[6], (D, HH), (HH // 2) ** -0.5, 0.3125, ((0, 8), (1, 4)))
    out_bias = gaussian(key_list[7], (D,), 0.3, 1.5, (), jnp.float32)
    norm2_gain = jnp.clip(1.0 + 0.1 * jax.random.normal(key_list[8], (D,), jnp.float32), 0.5, 1.5)
    norm2_bias = gaussian(key_list[9], (D,), 0.3, 1.5, (), jnp.float32)
    fc1_weight = gaussian(key_list[10], (D, FF), D ** -0.5, 0.21875, ((0, 8), (1, 4)))
    fc1_bias = gaussian(key_list[11], (FF,), 0.3, 1.5, ((0, 4),), jnp.float32)
    fc2_weight = gaussian(key_list[12], (D, FF), (FF // 2) ** -0.5, 0.15625, ((0, 8), (1, 4)))
    fc2_bias = gaussian(key_list[13], (D,), 0.3, 1.5, (), jnp.float32)
    prefix = touch_ends(jax.random.randint(key_list[14], (SEQS,), SEQ_LEN // 10, SEQ_LEN // 2 + 1), jax.random.fold_in(key_list[14], 1), SEQ_LEN // 10, (SEQ_LEN // 2 + 1) - 1).astype(jnp.int32)
    selected = picks_of(key_list[15], SEQS * NQB, NKB, SEL, 0).reshape((SEQS, NQB, SEL))
    cotangent = gaussian(key_list[16], (SEQS, SEQ_LEN, D), 1.0, 6.0, ((0, 2), (1, 16)))
    return dict(inputs=inputs, norm1_gain=norm1_gain, norm1_bias=norm1_bias, qkv_weight=qkv_weight, qv_bias=qv_bias, score_weight=score_weight, out_weight=out_weight, out_bias=out_bias, norm2_gain=norm2_gain, norm2_bias=norm2_bias, fc1_weight=fc1_weight, fc1_bias=fc1_bias, fc2_weight=fc2_weight, fc2_bias=fc2_bias, prefix=prefix, selected=selected, cotangent=cotangent)


@jax.custom_vjp
def low(v):
    return lax.optimization_barrier(v.astype(jnp.bfloat16)).astype(jnp.float32)

@jax.custom_vjp
def low_back(v):
    return v

def low_keep(v):
    return (low(v), None)

def low_pass(kept, grad):
    return (grad,)

def back_keep(v):
    return (v, None)

def back_low(kept, grad):
    return (low(grad),)
low.defvjp(low_keep, low_pass)
low_back.defvjp(back_keep, back_low)
epsilon = 1e-05
highest = lax.Precision.HIGHEST

def norm_rows(values, gain, shift):
    centred = values - lax.optimization_barrier(jnp.mean(values, axis=-1, keepdims=True))
    spread = lax.optimization_barrier(jnp.mean(centred * centred, axis=-1, keepdims=True))
    return centred * lax.rsqrt(spread + epsilon) * gain + shift

def allowed_keys(lengths, chosen):
    places = jnp.arange(SEQ_LEN, dtype=jnp.int32)
    query_pos = places[None, :, None]
    key_pos = places[None, None, :]
    prefix_end = lengths.astype(jnp.int32)[:, None, None]
    permitted = (key_pos <= query_pos) | (query_pos < prefix_end) & (key_pos < prefix_end)
    near_by = jnp.abs(query_pos - key_pos) < WIN
    block_hits = jnp.any(chosen.astype(jnp.int32)[:, :, :, None] == jnp.arange(NKB, dtype=jnp.int32), axis=2)
    member = jnp.repeat(jnp.repeat(block_hits, QB, axis=1), KB, axis=2)
    return permitted & (near_by | member)

def forward(inputs, norm1_gain, norm1_bias, qkv_weight, qv_bias, score_weight, out_weight, out_bias, norm2_gain, norm2_bias, fc1_weight, fc1_bias, fc2_weight, fc2_bias, prefix, selected):
    batch_seqs = inputs.shape[0]
    normed = low(norm_rows(inputs, norm1_gain, norm1_bias))
    mixed_rows = jnp.einsum('btd,dch->btch', normed, qkv_weight, precision=highest)
    offsets = jnp.stack([qv_bias[0], jnp.zeros_like(qv_bias[0]), qv_bias[1]])
    mixed_rows = low_back(low(mixed_rows + offsets))
    split_rows = mixed_rows.reshape(batch_seqs, SEQ_LEN, 3, H, HD)
    queries = split_rows[:, :, 0]
    keys_all = split_rows[:, :, 1]
    values_all = split_rows[:, :, 2]
    scoring = low_back(jnp.einsum('btd,dh->bth', normed, score_weight, precision=highest))
    gate_logs = low_back(low(jax.nn.log_sigmoid(scoring)))
    raw_scores = low_back(jnp.einsum('bqhd,bkhd->bhqk', queries, keys_all, precision=highest) * HD ** (-0.5))
    logits = raw_scores + jnp.transpose(gate_logs, (0, 2, 1))[:, :, None, :]
    logits = jnp.where(allowed_keys(prefix, selected)[:, None], logits, -1e+30)
    weights = low(jax.nn.softmax(logits, axis=-1))
    attended = jnp.einsum('bhqk,bkhd->bqhd', weights, values_all, precision=highest)
    attended = low_back(low(attended.reshape(batch_seqs, SEQ_LEN, H * HD)))
    middle = inputs + low_back(jnp.einsum('bte,de->btd', attended, out_weight, precision=highest)) + out_bias
    normed_two = low(norm_rows(middle, norm2_gain, norm2_bias))
    before = low_back(jnp.einsum('btd,df->btf', normed_two, fc1_weight, precision=highest) + fc1_bias)
    activated = low(jax.nn.gelu(before, approximate=True))
    return middle + low_back(jnp.einsum('btf,df->btd', activated, fc2_weight, precision=highest)) + fc2_bias

def reference(inputs, norm1_gain, norm1_bias, qkv_weight, qv_bias, score_weight, out_weight, out_bias, norm2_gain, norm2_bias, fc1_weight, fc1_bias, fc2_weight, fc2_bias, prefix, selected, cotangent):
    groups = inputs.shape[0] // SEQ_MB
    params = tuple((array_in.astype(jnp.float32) for array_in in (norm1_gain, norm1_bias, qkv_weight, qv_bias, score_weight, out_weight, out_bias, norm2_gain, norm2_bias, fc1_weight, fc1_bias, fc2_weight, fc2_bias)))
    group_rows = inputs.astype(jnp.float32).reshape(groups, SEQ_MB, SEQ_LEN, D)
    group_grads = cotangent.astype(jnp.float32).reshape(groups, SEQ_MB, SEQ_LEN, D)
    group_prefix = prefix.reshape(groups, SEQ_MB)
    group_chosen = selected.reshape(groups, SEQ_MB, NQB, SEL)

    def one_group(running, item):
        tok_rows, prefix_part, chosen_part, grad_rows = item

        def apply_layer(rows_in, *params_in):
            return forward(rows_in, *params_in, prefix_part, chosen_part)
        outputs, pullback = jax.vjp(apply_layer, tok_rows, *params)
        grads = pullback(grad_rows)
        running = tuple((total_in + update for total_in, update in zip(running, grads[1:])))
        return (running, (outputs, grads[0]))
    zeros_init = tuple((jnp.zeros_like(array_in) for array_in in params))
    sums, (outputs, input_grads) = lax.scan(one_group, zeros_init, (group_rows, group_prefix, group_chosen, group_grads))
    result = outputs.reshape(inputs.shape).astype(jnp.bfloat16)
    input_grad = input_grads.reshape(inputs.shape).astype(jnp.bfloat16)
    return (result, input_grad, sums[0], sums[1], sums[2], sums[3], sums[4], sums[5], sums[6], sums[7], sums[8], sums[9], sums[10], sums[11], sums[12])
```

```python
from functools import partial

import jax
import jax.numpy as jnp
from jax import lax
from jax.experimental import pallas as pl
from jax.experimental.pallas import tpu as pltpu
from jax.sharding import Mesh
from jax.sharding import PartitionSpec as P

HD = 64
QB = 64
KB = 16
SEL = 4
WIN = 64
SEQ_MB = 4
MICRO = 2


epsilon = 1e-05
negative_fill = -1e30


def contract(left, right, left_dim, right_dim):
    return lax.dot_general(
        left, right, (((left_dim,), (right_dim,)), ((), ())), preferred_element_type=jnp.float32
    )


def rounded(values):
    return values.astype(jnp.bfloat16)


def norm_rows(values, gain, shift):
    centred = values - jnp.mean(values, axis=-1, keepdims=True)
    inverse = lax.rsqrt(jnp.mean(centred * centred, axis=-1, keepdims=True) + epsilon)
    unit_rows = centred * inverse
    return (unit_rows * gain + shift, unit_rows, inverse)


def norm_back(upstream, unit_rows, inverse, gain):
    scaled = upstream * gain
    centred = scaled - jnp.mean(scaled, axis=-1, keepdims=True)
    return inverse * (centred - unit_rows * jnp.mean(scaled * unit_rows, axis=-1, keepdims=True))


def pick_rows(source, key_picks):
    return jax.vmap(lambda table_in, places: table_in[places])(source, key_picks)


def shards(
    inputs,
    norm1_gain,
    norm1_bias,
    qkv_weight,
    qv_bias,
    score_weight,
    out_weight,
    out_bias,
    norm2_gain,
    norm2_bias,
    fc1_weight,
    fc1_bias,
    fc2_weight,
    fc2_bias,
    prefix,
    selected,
    cotangent,
):
    all_seqs, own_tok, width_full = inputs.shape
    ctx_tok = own_tok * lax.axis_size("tp")
    heads_local = score_weight.shape[1]
    hidden_local = out_weight.shape[1]
    units_local = fc1_bias.shape[0]
    seq_full = ctx_tok * lax.axis_size("ctx")
    blocks_local = ctx_tok // QB
    near_span = QB + 2 * WIN
    chosen_span = SEL * KB
    key_count = chosen_span + near_span
    tokens = SEQ_MB * ctx_tok
    score_scale = HD ** (-0.5)
    own_start = lax.axis_index("tp") * own_tok
    block_ids = lax.axis_index("ctx") * blocks_local + jnp.arange(blocks_local, dtype=jnp.int32)
    query_pos = block_ids[:, None] * QB + jnp.arange(QB, dtype=jnp.int32)[None, :]
    near_picks = block_ids[:, None] * QB + jnp.arange(near_span, dtype=jnp.int32)[None, :]
    is_chosen = jnp.arange(key_count) < chosen_span
    qkv_offsets = jnp.stack([qv_bias[0], jnp.zeros_like(qv_bias[0]), qv_bias[1]])
    key_own = lax.axis_index("ctx") * ctx_tok + jnp.arange(ctx_tok, dtype=jnp.int32)
    every_query = jnp.arange(seq_full, dtype=jnp.int32)
    chosen_every = lax.all_gather(selected, "ctx", axis=1, tiled=True)

    def scores_of(queries, keys_near, gates_near, allowed):
        raw_scores = (
            jnp.einsum("sbqhd,sbkhd->sbhqk", queries, keys_near, preferred_element_type=jnp.float32)
            * score_scale
        )
        logits = raw_scores + jnp.transpose(gates_near, (0, 1, 3, 2))[:, :, :, None, :].astype(
            jnp.float32
        )
        return jnp.where(allowed[:, :, None], logits, negative_fill)

    def micro_step(micro_index, carried):
        big_sums, small_sums, out_buffer, grad_buffer = carried
        qkv_full, score_full, out_full, fc1_full, fc2_full = (
            lax.all_gather(qkv_weight, ("fsdp", "ctx"), axis=0, tiled=True),
            lax.all_gather(score_weight, ("fsdp", "ctx"), axis=0, tiled=True),
            lax.all_gather(out_weight, ("fsdp", "ctx"), axis=0, tiled=True),
            lax.all_gather(fc1_weight, ("fsdp", "ctx"), axis=0, tiled=True),
            lax.all_gather(fc2_weight, ("fsdp", "ctx"), axis=0, tiled=True),
        )
        seq_start = micro_index * SEQ_MB
        local_rows = lax.dynamic_slice_in_dim(inputs, seq_start, SEQ_MB, 0)
        full_rows = (
            lax.all_gather(local_rows, "tp", axis=1, tiled=True)
            .astype(jnp.float32)
            .reshape(tokens, width_full)
        )
        normed, unit_one, inverse_one = norm_rows(full_rows, norm1_gain, norm1_bias)
        normed_low = rounded(normed)
        qkv_flat = qkv_full.reshape(width_full, 3 * hidden_local)
        mixed_rows = contract(normed_low, qkv_flat, 1, 0).reshape(tokens, 3, hidden_local)
        mixed_low = rounded(mixed_rows + qkv_offsets)
        scoring = contract(normed_low, score_full, 1, 0)
        gate_low = rounded(jax.nn.log_sigmoid(scoring))
        kv_local = mixed_low[:, 1:].reshape(SEQ_MB, ctx_tok, 2 * hidden_local)
        kv_all, gate_all = (
            lax.all_gather(kv_local, "ctx", axis=1, tiled=True),
            lax.all_gather(
                gate_low.reshape(SEQ_MB, ctx_tok, heads_local), "ctx", axis=1, tiled=True
            ),
        )
        kv_padded = jnp.pad(kv_all, ((0, 0), (WIN, WIN), (0, 0)))
        gate_padded = jnp.pad(gate_all, ((0, 0), (WIN, WIN), (0, 0)))
        chosen = lax.dynamic_slice_in_dim(selected, seq_start, SEQ_MB, 0)
        chosen_picks = (chosen[..., None] * KB + jnp.arange(KB, dtype=jnp.int32) + WIN).reshape(
            SEQ_MB, blocks_local, chosen_span
        )
        key_picks = jnp.concatenate(
            [chosen_picks, jnp.broadcast_to(near_picks, (SEQ_MB, blocks_local, near_span))], axis=-1
        )
        key_pos = (key_picks - WIN)[:, :, None, :]
        query_at = query_pos[None, :, :, None]
        prefix_now = lax.dynamic_slice_in_dim(prefix, seq_start, SEQ_MB, 0)
        prefix_end = prefix_now[:, None, None, None]
        permitted = (key_pos <= query_at) | (query_at < prefix_end) & (key_pos < prefix_end)
        inside = (key_pos >= 0) & (key_pos < seq_full)
        near_by = jnp.abs(query_at - key_pos) < WIN
        allowed = inside & permitted & jnp.where(is_chosen, jnp.logical_not(near_by), near_by)
        kv_near = pick_rows(kv_padded, key_picks).reshape(
            SEQ_MB, blocks_local, key_count, 2, heads_local, HD
        )
        keys_near = kv_near[:, :, :, 0]
        values_near = kv_near[:, :, :, 1]
        gates_near = pick_rows(gate_padded, key_picks)
        queries = mixed_low[:, 0].reshape(SEQ_MB, blocks_local, QB, heads_local, HD)
        logits = scores_of(queries, keys_near, gates_near, allowed)
        row_max = jnp.max(logits, axis=-1, keepdims=True)
        log_total = row_max + jnp.log(jnp.sum(jnp.exp(logits - row_max), axis=-1, keepdims=True))
        probs_low = rounded(jnp.exp(logits - log_total))
        attended = jnp.einsum(
            "sbhqk,sbkhd->sbqhd", probs_low, values_near, preferred_element_type=jnp.float32
        )
        attended_low = rounded(attended).reshape(tokens, hidden_local)
        branch = contract(attended_low, out_full, 1, 1).reshape(SEQ_MB, ctx_tok, width_full)
        middle = (
            local_rows.astype(jnp.float32)
            + lax.psum_scatter(branch, "tp", scatter_dimension=1, tiled=True)
            + out_bias
        )
        middle_full = lax.all_gather(middle, "tp", axis=1, tiled=True).reshape(tokens, width_full)
        normed_two, unit_two, inverse_two = norm_rows(middle_full, norm2_gain, norm2_bias)
        normed_two_low = rounded(normed_two)
        before = contract(normed_two_low, fc1_full, 1, 0) + fc1_bias
        activated, gelu_back = jax.vjp(partial(jax.nn.gelu, approximate=True), before)
        activated_low = rounded(activated)
        mlp_terms = contract(activated_low, fc2_full, 1, 1).reshape(SEQ_MB, ctx_tok, width_full)
        outcome = (
            middle
            + lax.psum_scatter(
                mlp_terms.astype(jnp.bfloat16), "tp", scatter_dimension=1, tiled=True
            ).astype(jnp.float32)
            + fc2_bias
        )
        out_buffer = lax.dynamic_update_slice_in_dim(out_buffer, rounded(outcome), seq_start, 0)
        grad_local = lax.dynamic_slice_in_dim(cotangent, seq_start, SEQ_MB, 0)
        grad_low = lax.all_gather(grad_local, "tp", axis=1, tiled=True).reshape(tokens, width_full)
        grad_rows = grad_low.astype(jnp.float32)
        d_activated = contract(grad_low, fc2_full, 1, 0)
        d_before_low = rounded(gelu_back(d_activated)[0])
        fc2_step = contract(grad_low, activated_low, 0, 0)
        fc1_step = contract(normed_two_low, d_before_low, 0, 0)
        d_normed_two = lax.psum(contract(d_before_low, fc1_full, 1, 1), "tp")
        d_middle = grad_rows + norm_back(d_normed_two, unit_two, inverse_two, norm2_gain)
        d_middle_low = rounded(d_middle)
        out_step = contract(d_middle_low, attended_low, 0, 0)
        d_attended = rounded(contract(d_middle_low, out_full, 1, 0)).reshape(
            SEQ_MB, blocks_local, QB, heads_local, HD
        )
        probs_again = jnp.exp(scores_of(queries, keys_near, gates_near, allowed) - log_total)
        d_probs = jnp.einsum(
            "sbqhd,sbkhd->sbhqk", d_attended, values_near, preferred_element_type=jnp.float32
        )
        row_delta = jnp.sum(probs_again * d_probs, axis=-1, keepdims=True)
        d_logits = probs_again * (d_probs - row_delta)
        d_logits_low = rounded(d_logits)
        d_queries = (
            jnp.einsum(
                "sbhqk,sbkhd->sbqhd", d_logits_low, keys_near, preferred_element_type=jnp.float32
            )
            * score_scale
        )
        stats_local = (
            jnp.transpose(log_total, (0, 1, 3, 2, 4)).reshape(SEQ_MB, ctx_tok, heads_local),
            jnp.transpose(row_delta, (0, 1, 3, 2, 4)).reshape(SEQ_MB, ctx_tok, heads_local),
        )
        queries_flat = mixed_low[:, 0].reshape(SEQ_MB, ctx_tok, hidden_local)
        d_att_flat = d_attended.reshape(SEQ_MB, ctx_tok, hidden_local)
        queries_every, d_att_every = (
            lax.all_gather(queries_flat, "ctx", axis=1, tiled=True),
            lax.all_gather(d_att_flat, "ctx", axis=1, tiled=True),
        )
        log_every, delta_every = (
            lax.all_gather(stats_local[0], "ctx", axis=1, tiled=True),
            lax.all_gather(stats_local[1], "ctx", axis=1, tiled=True),
        )
        chosen_now = lax.dynamic_slice_in_dim(chosen_every, seq_start, SEQ_MB, 0)
        query_all = every_query[None, :, None]
        key_all = key_own[None, None, :]
        end_all = prefix_now[:, None, None]
        permitted_all = (key_all <= query_all) | (query_all < end_all) & (key_all < end_all)
        near_all = jnp.abs(query_all - key_all) < WIN
        block_hits = jnp.any(
            chosen_now[:, :, :, None] == (key_own // KB)[None, None, None, :], axis=2
        )
        member = jnp.repeat(block_hits, QB, axis=1)
        allowed_all = permitted_all & (near_all | member)
        queries_four = queries_every.reshape(SEQ_MB, seq_full, heads_local, HD)
        d_att_four = d_att_every.reshape(SEQ_MB, seq_full, heads_local, HD)
        keys_own = mixed_low[:, 1].reshape(SEQ_MB, ctx_tok, heads_local, HD)
        values_own = mixed_low[:, 2].reshape(SEQ_MB, ctx_tok, heads_local, HD)
        gates_own = gate_low.reshape(SEQ_MB, ctx_tok, heads_local)
        logits_own = (
            jnp.einsum(
                "sqhd,skhd->shqk", queries_four, keys_own, preferred_element_type=jnp.float32
            )
            * score_scale
        )
        logits_own = logits_own + jnp.transpose(gates_own, (0, 2, 1))[:, :, None, :].astype(
            jnp.float32
        )
        logits_own = jnp.where(allowed_all[:, None], logits_own, negative_fill)
        probs_own = jnp.exp(logits_own - jnp.transpose(log_every, (0, 2, 1))[..., None])
        d_probs_own = jnp.einsum(
            "sqhd,skhd->shqk", d_att_four, values_own, preferred_element_type=jnp.float32
        )
        d_logits_own = probs_own * (d_probs_own - jnp.transpose(delta_every, (0, 2, 1))[..., None])
        d_keys_own = (
            jnp.einsum(
                "shqk,sqhd->skhd",
                rounded(d_logits_own),
                queries_four,
                preferred_element_type=jnp.float32,
            )
            * score_scale
        )
        d_values_own = jnp.einsum(
            "shqk,sqhd->skhd", rounded(probs_own), d_att_four, preferred_element_type=jnp.float32
        )
        d_kv_mine = jnp.stack([d_keys_own, d_values_own], axis=2).reshape(
            SEQ_MB, ctx_tok, 2 * hidden_local
        )
        d_gate_mine = jnp.transpose(jnp.sum(d_logits_own, axis=2), (0, 2, 1))
        d_kv_low = rounded(d_kv_mine).reshape(tokens, 2, hidden_local)
        gate_grad = (
            lax.optimization_barrier(rounded(d_gate_mine))
            .astype(jnp.float32)
            .reshape(tokens, heads_local)
        )
        d_scoring_low = rounded(gate_grad * jax.nn.sigmoid(-scoring))
        d_queries_low = rounded(d_queries).reshape(tokens, 1, hidden_local)
        d_mixed = jnp.concatenate([d_queries_low, d_kv_low], axis=1).reshape(
            tokens, 3 * hidden_local
        )
        qkv_step = contract(normed_low, d_mixed, 0, 0).reshape(width_full, 3, hidden_local)
        score_step = contract(normed_low, d_scoring_low, 0, 0)
        d_normed_part = contract(d_mixed, qkv_flat, 1, 1) + contract(
            d_scoring_low, score_full, 1, 1
        )
        d_normed = lax.psum(d_normed_part.astype(jnp.bfloat16), "tp").astype(jnp.float32)
        d_inputs = (d_middle + norm_back(d_normed, unit_one, inverse_one, norm1_gain)).reshape(
            SEQ_MB, ctx_tok, width_full
        )
        d_inputs_mine = lax.dynamic_slice_in_dim(d_inputs, own_start, own_tok, 1)
        grad_buffer = lax.dynamic_update_slice_in_dim(
            grad_buffer, rounded(d_inputs_mine), seq_start, 0
        )
        small_step = (
            jnp.sum(d_normed * unit_one, axis=0),
            jnp.sum(d_normed, axis=0),
            jnp.stack(
                [
                    jnp.sum(d_queries_low[:, 0], axis=0, dtype=jnp.float32),
                    jnp.sum(d_kv_low[:, 1], axis=0, dtype=jnp.float32),
                ]
            ),
            jnp.sum(d_middle, axis=0),
            jnp.sum(d_normed_two * unit_two, axis=0),
            jnp.sum(d_normed_two, axis=0),
            jnp.sum(d_before_low, axis=0, dtype=jnp.float32),
            jnp.sum(grad_rows, axis=0),
        )
        big_step = (qkv_step, score_step, out_step, fc1_step, fc2_step)
        big_sums = jax.tree.map(jnp.add, big_sums, big_step)
        small_sums = jax.tree.map(jnp.add, small_sums, small_step)
        return (big_sums, small_sums, out_buffer, grad_buffer)

    big_init = (
        jnp.zeros((width_full, 3, hidden_local), jnp.float32),
        jnp.zeros((width_full, heads_local), jnp.float32),
        jnp.zeros((width_full, hidden_local), jnp.float32),
        jnp.zeros((width_full, units_local), jnp.float32),
        jnp.zeros((width_full, units_local), jnp.float32),
    )
    small_init = (
        jnp.zeros((width_full,), jnp.float32),
        jnp.zeros((width_full,), jnp.float32),
        jnp.zeros((2, hidden_local), jnp.float32),
        jnp.zeros((width_full,), jnp.float32),
        jnp.zeros((width_full,), jnp.float32),
        jnp.zeros((width_full,), jnp.float32),
        jnp.zeros((units_local,), jnp.float32),
        jnp.zeros((width_full,), jnp.float32),
    )
    buffer_init = jnp.zeros(inputs.shape, jnp.bfloat16)
    big_sums, small_sums, out_buffer, grad_buffer = lax.fori_loop(
        0, MICRO, micro_step, (big_init, small_init, buffer_init, buffer_init)
    )
    big_grads = (
        lax.psum_scatter(big_sums[0], ("fsdp", "ctx"), scatter_dimension=0, tiled=True),
        lax.psum_scatter(big_sums[1], ("fsdp", "ctx"), scatter_dimension=0, tiled=True),
        lax.psum_scatter(big_sums[2], ("fsdp", "ctx"), scatter_dimension=0, tiled=True),
        lax.psum_scatter(big_sums[3], ("fsdp", "ctx"), scatter_dimension=0, tiled=True),
        lax.psum_scatter(big_sums[4], ("fsdp", "ctx"), scatter_dimension=0, tiled=True),
    )
    small_grads = lax.psum(
        (
            small_sums[0],
            small_sums[1],
            small_sums[2],
            small_sums[3],
            small_sums[4],
            small_sums[5],
            small_sums[6],
            small_sums[7],
        ),
        ("fsdp", "ctx"),
    )
    return (
        out_buffer,
        grad_buffer,
        small_grads[0],
        small_grads[1],
        big_grads[0],
        small_grads[2],
        big_grads[1],
        big_grads[2],
        small_grads[3],
        small_grads[4],
        small_grads[5],
        big_grads[3],
        small_grads[6],
        big_grads[4],
        small_grads[7],
    )


EPS = 1e-05
MASKED = -1e30
MESH_ID = pl.DeviceIdType.MESH
CH_A, CH_B, CH_1, CH_2 = 0, 1, 2, 3
f32 = jnp.float32
bf16 = jnp.bfloat16


def dot(left, right, left_dim, right_dim):
    return lax.dot_general(
        left, right, (((left_dim,), (right_dim,)), ((), ())), preferred_element_type=f32
    )


def ln_parts(rows):
    centred = rows - jnp.mean(rows, axis=-1, keepdims=True)
    inverse = lax.rsqrt(jnp.mean(centred * centred, axis=-1, keepdims=True) + EPS)
    return centred * inverse, inverse


def ln_back(upstream, unit, inverse, gain):
    scaled = upstream * gain
    return inverse * (
        scaled
        - jnp.mean(scaled, axis=-1, keepdims=True)
        - unit * jnp.mean(scaled * unit, axis=-1, keepdims=True)
    )


def layer_kernel(
    x_hbm, cot_hbm, pa_hbm, pb_hbm, f1_hbm, f2_hbm, sel_hbm, bias_in, vec, pref,
    res_o, ing_o, ga_o, gb_o, g1_o, g2_o, sm_o,
    wa, wb, w1, w2, ga, gb, g1, g2,
    rba, rbb, rb1, rb2, rza, rzb, rz1, rz2, rpa, rpb, rp1, rp2,
    xin, cot, nrm, qb, kb, vb, ksel, vsel, pr, att, mid, n2, act, dbf,
    st, rv, dnr, dml, datt, dkacc, dvacc, scr, stage, selb, biasb, smb, smr,
    ain_s, ain_r, aout_s, aout_r, ag_s, ag_r, rs_s, rs_r, tm_s, tm_r,
    sel_s, sel_r, bias_s, bias_r, sm_s, sm_r, loc,
):
    y = lax.axis_index("fsdp")
    x = lax.axis_index("xo")
    c = lax.axis_index("team")
    z = lax.axis_index("tp")
    zz = z + c * (3 - 2 * z)
    z_up = z + 1 - 2 * c
    z_dn = z - 1 + 2 * c
    source = zz < 2
    own_tok = x_hbm.shape[1]
    width = x_hbm.shape[2]
    tile = 4 * own_tok
    half = 2 * tile
    seq = 2 * half
    my_seq = x * 4 + z
    hbms = (pa_hbm, pb_hbm, f1_hbm, f2_hbm)
    weights = (wa, wb, w1, w2)
    grads = (ga, gb, g1, g2)
    rbs = (rba, rbb, rb1, rb2)
    rzs = (rza, rzb, rz1, rz2)
    rps = (rpa, rpb, rp1, rp2)
    g_outs = (ga_o, gb_o, g1_o, g2_o)
    shard = pa_hbm.shape[0]
    pair = 2 * shard
    up, down = {"tp": z_up}, {"tp": z_dn}
    over_x, over_y, other = {"xo": 1 - x}, {"fsdp": 1 - y}, {"team": 1 - c}

    def block(yy, xx):
        return pl.ds(pl.multiple_of((yy * 4 + xx * 2) * shard, pair), pair)

    mine = block(y, x)

    def own_shard(cc):
        return pl.ds(pl.multiple_of((y * 4 + x * 2 + cc) * shard, shard), shard)

    def rcopy(src, dst, ss, rs, dev):
        return pltpu.make_async_remote_copy(
            src_ref=src, dst_ref=dst, send_sem=ss, recv_sem=rs, device_id=dev, device_id_type=MESH_ID
        )

    bar = pltpu.get_barrier_semaphore()
    peers = []
    for dx in range(2):
        for dz in range(4):
            if dx or dz:
                peers.append({"xo": lax.rem(x + dx, 2), "tp": lax.rem(z + dz, 4)})
    peers += [other, over_y, {"xo": 1 - x, "team": 1 - c}]
    for peer in peers:
        pl.semaphore_signal(bar, 1, device_id=peer, device_id_type=MESH_ID)
    pl.semaphore_wait(bar, len(peers))

    def a2a_in(which, hbm):
        out = []
        for dx in range(2):
            for dz in range(4):
                xx, z2 = lax.rem(x + dx, 2), lax.rem(z + dz, 4)
                if which == 0:
                    at = pl.ds(pl.multiple_of(x * tile + z * own_tok, own_tok), own_tok)
                    dst = xin.at[at]
                else:
                    at = pl.ds(pl.multiple_of(x * half + c * tile + z * own_tok, own_tok), own_tok)
                    dst = cot.at[at]
                idx = dx * 4 + dz
                src = hbm.at[xx * 4 + z2]
                if idx == 0:
                    out.append(pltpu.make_async_copy(src, dst, ain_r.at[which, 0]))
                else:
                    out.append(
                        rcopy(src, dst, ain_s.at[which, idx], ain_r.at[which, idx], {"xo": xx, "tp": z2})
                    )
        return out

    def a2a_in_wait(copies):
        copies[0].wait()
        for cp in copies[1:]:
            cp.wait()

    def p0_local(k):
        return pltpu.make_async_copy(hbms[k], weights[k].at[zz, own_shard(c)], loc.at[k])

    def p0_away(k):
        return rcopy(
            hbms[k], weights[k].at[3 - zz, own_shard(c)], ag_s.at[k, 0], ag_r.at[k, 0], other
        )

    def p0_back(k):
        return rcopy(
            hbms[k], weights[k].at[zz, own_shard(1 - c)], ag_s.at[k, 0], ag_r.at[k, 0], other
        )

    def p0_start(k):
        @pl.when(source)
        def _():
            p0_local(k).start()

        @pl.when(jnp.logical_not(source))
        def _():
            p0_away(k).start()

    def p0_wait(k):
        @pl.when(source)
        def _():
            p0_local(k).wait()
            p0_back(k).wait_recv()

        @pl.when(jnp.logical_not(source))
        def _():
            p0_away(k).wait_send()

    def zcopy(k, which):
        slot, dev, idx = ((0, up, 1), (1, up, 2), (1, down, 3))[which]
        ref = weights[k].at[slot, mine]
        return rcopy(ref, ref, ag_s.at[k, idx], ag_r.at[k, idx], dev)

    UP0, UP1, DN1 = 0, 1, 2

    def z1(k):
        @pl.when(zz == 0)
        def _():
            zcopy(k, UP0).start()

        @pl.when(zz == 1)
        def _():
            zcopy(k, DN1).start()
            zcopy(k, UP1).start()

    def z2(k):
        @pl.when(zz == 1)
        def _():
            zcopy(k, UP0).wait_recv()
            zcopy(k, UP0).start()

        @pl.when(zz == 2)
        def _():
            zcopy(k, UP1).wait_recv()
            zcopy(k, UP1).start()

    def z3(k):
        @pl.when(zz == 2)
        def _():
            zcopy(k, UP0).wait_recv()
            zcopy(k, UP0).start()

    def z_wait(k, slot):
        if slot == 0:
            @pl.when(zz == 3)
            def _():
                zcopy(k, UP0).wait_recv()
        else:
            @pl.when(zz == 0)
            def _():
                zcopy(k, DN1).wait_recv()

            @pl.when(zz == 3)
            def _():
                zcopy(k, UP1).wait_recv()

    def z_drain(k):
        @pl.when(zz < 3)
        def _():
            zcopy(k, UP0).wait_send()

        @pl.when((zz == 1) | (zz == 2))
        def _():
            zcopy(k, UP1).wait_send()

        @pl.when(zz == 1)
        def _():
            zcopy(k, DN1).wait_send()

    def xy(k, which):
        slot, rows, dev = (
            (0, mine, over_x),
            (0, mine, over_y),
            (1, mine, over_y),
            (1, mine, over_x),
            (0, block(y, 1 - x), over_y),
            (1, block(1 - y, x), over_x),
        )[which]
        ref = weights[k].at[slot, rows]
        return rcopy(ref, ref, ag_s.at[k, 4 + which], ag_r.at[k, 4 + which], dev)

    def s1(k):
        z_wait(k, 1)
        xy(k, 2).start()
        z_wait(k, 0)
        xy(k, 0).start()
        xy(k, 3).start()
        xy(k, 1).start()

    def s2(k):
        xy(k, 2).wait_recv()
        xy(k, 5).start()
        xy(k, 0).wait_recv()
        xy(k, 4).start()

    def s3(k):
        for which in (1, 3, 4, 5):
            xy(k, which).wait_recv()

    def ag_drain(k):
        z_drain(k)
        for which in range(6):
            xy(k, which).wait_send()

    def rs_copy(k, which):
        g, rb = grads[k], rbs[k]
        slot, rows, dev = (
            (0, block(1 - y, 1 - x), over_y),
            (0, block(1 - y, x), over_y),
            (0, block(y, 1 - x), over_x),
            (1, block(1 - y, 1 - x), over_x),
            (1, block(y, 1 - x), over_x),
            (1, block(1 - y, x), over_y),
        )[which]
        return rcopy(g.at[slot, rows], rb.at[which], rs_s.at[k, which], rs_r.at[k, which], dev)

    def add_rows(k, slot, rows, bufs):
        g = grads[k]
        total = g[slot, rows, :].astype(f32)
        for buf in bufs:
            total = total + buf[...].astype(f32)
        g[slot, rows, :] = total.astype(bf16)

    def r1(k, slot):
        for which in ((0, 1), (3, 4))[slot]:
            rs_copy(k, which).start()

    def r2(k, slot):
        first, onward, rows = ((0, 2, block(y, 1 - x)), (3, 5, block(1 - y, x)))[slot]
        rs_copy(k, first).wait_recv()
        add_rows(k, slot, rows, [rbs[k].at[first]])
        rs_copy(k, onward).start()

    def r3(k):
        for which in (1, 4, 2, 5):
            rs_copy(k, which).wait_recv()
        add_rows(k, 0, mine, [rbs[k].at[1], rbs[k].at[2]])
        add_rows(k, 1, mine, [rbs[k].at[4], rbs[k].at[5]])

    def rz_copy(k, which):
        slot, dev = ((0, down), (1, down), (1, up))[which]
        return rcopy(
            grads[k].at[slot, mine], rzs[k].at[which], rs_s.at[k, 6 + which], rs_r.at[k, 6 + which], dev
        )

    def rz1_(k):
        @pl.when(zz == 3)
        def _():
            rz_copy(k, 0).start()
            rz_copy(k, 1).start()

        @pl.when(zz == 0)
        def _():
            rz_copy(k, 2).start()

    def rz2_(k):
        @pl.when(zz == 2)
        def _():
            for which in (0, 1):
                rz_copy(k, which).wait_recv()
                add_rows(k, which, mine, [rzs[k].at[which]])
                rz_copy(k, which).start()

    def rz3_(k):
        @pl.when(zz == 1)
        def _():
            rz_copy(k, 0).wait_recv()
            add_rows(k, 0, mine, [rzs[k].at[0]])
            rz_copy(k, 0).start()
            rz_copy(k, 1).wait_recv()
            rz_copy(k, 2).wait_recv()
            add_rows(k, 1, mine, [rzs[k].at[1], rzs[k].at[2]])

    def rz4_(k):
        @pl.when(zz == 0)
        def _():
            rz_copy(k, 0).wait_recv()
            add_rows(k, 0, mine, [rzs[k].at[0]])

    def rp_copy(k):
        return rcopy(
            grads[k].at[zz, own_shard(1 - c)], rps[k], rs_s.at[k, 9], rs_r.at[k, 9], other
        )

    def rp_start(k):
        @pl.when(source)
        def _():
            rp_copy(k).start()
            g_outs[k][...] = grads[k][zz, own_shard(c), :].astype(f32)

    def rp_wait(k):
        @pl.when(jnp.logical_not(source))
        def _():
            rcopy(rps[k], rps[k], rs_s.at[k, 9], rs_r.at[k, 9], other).wait_recv()
            g_outs[k][...] = rps[k][...].astype(f32)

        @pl.when(source)
        def _():
            rp_copy(k).wait_send()

    def rs_drain(k):
        for which in range(6):
            rs_copy(k, which).wait_send()

        @pl.when(zz > 0)
        def _():
            rz_copy(k, 0).wait_send()

        @pl.when(zz > 1)
        def _():
            rz_copy(k, 1).wait_send()

        @pl.when(zz == 0)
        def _():
            rz_copy(k, 2).wait_send()

    def chunk(j, cc):
        return pl.ds(pl.multiple_of(j * half + cc * tile, tile), tile)

    def swap(buf, j, idx):
        return rcopy(buf.at[chunk(j, c)], buf.at[chunk(j, c)], tm_s.at[idx + j], tm_r.at[idx + j], other)

    def swap_wait(buf, j, idx):
        rcopy(buf.at[chunk(j, 1 - c)], buf.at[chunk(j, 1 - c)], tm_s.at[idx + j], tm_r.at[idx + j], other).wait_recv()

    def part(which, j, idx):
        return rcopy(st.at[which, j], rv.at[which, j], tm_s.at[idx + j], tm_r.at[idx + j], other)

    T_NRM, T_COT, T_BR, T_N2, T_MLP, T_DN2, T_DML, T_DNR = range(0, 16, 2)

    lane256 = lax.broadcasted_iota(jnp.int32, (1, 256), 1)
    head_rows = [jnp.where(lane256 // 64 == h, 1.0, 0.0).astype(f32) for h in range(3)]
    q_rows = [
        jnp.where((lane256 // 64 == h) | (lane256 == 192 + h), 1.0, 0.0).astype(f32) for h in range(3)
    ]

    def stack3(rows, masks):
        wide = rows.astype(f32)
        return jnp.concatenate([(wide * m).astype(bf16) for m in masks], axis=0)

    def fold3(stacked):
        n = stacked.shape[0] // 3
        return (
            stacked[:n] * head_rows[0] + stacked[n : 2 * n] * head_rows[1] + stacked[2 * n :] * head_rows[2]
        )

    for k in (CH_A,):
        p0_start(k)
    x_copies = a2a_in(0, x_hbm)
    for cp in x_copies:
        cp.start()
    sel_copies = []
    for dx in range(2):
        for dc in range(2):
            idx = dx * 2 + dc
            xx, cc = lax.rem(x + dx, 2), lax.rem(c + dc, 2)
            src, dst = sel_hbm.at[xx * 4 + z], selb.at[x * 2 + c]
            if idx == 0:
                sel_copies.append(pltpu.make_async_copy(src, dst, sel_r.at[0]))
            else:
                sel_copies.append(
                    rcopy(src, dst, sel_s.at[idx], sel_r.at[idx], {"xo": xx, "team": cc})
                )
    for cp in sel_copies:
        cp.start()

    def bias_copy(dz):
        return rcopy(
            bias_in, biasb.at[zz], bias_s.at[dz], bias_r.at[zz], {"tp": lax.rem(z + dz, 4)}
        )

    @pl.when(source)
    def _():
        for dz in range(1, 4):
            bias_copy(dz).start()
        biasb[zz] = bias_in[...]

    for k in (CH_B, CH_1, CH_2):
        p0_start(k)
    p0_wait(CH_A)
    z1(CH_A)
    zero_k = jnp.zeros((own_tok, 256), bf16)
    for ref in (kb, vb):
        for slot in range(2):
            ref[slot, 0:own_tok, :] = zero_k
            ref[slot, seq + own_tok : seq + 2 * own_tok, :] = zero_k
    smb[...] = jnp.zeros_like(smb)
    z2(CH_A)
    a2a_in_wait(x_copies)

    def natural(i):
        return pl.multiple_of((i // 4) * half + c * tile + (i % 4) * own_tok, own_tok)

    def ln1_body(i, carry):
        rows = xin[pl.ds(pl.multiple_of(i * own_tok, own_tok), own_tok), :].astype(f32)
        unit, _ = ln_parts(rows)
        nrm[pl.ds(natural(i), own_tok), :] = (unit * vec[0:1, :] + vec[1:2, :]).astype(bf16)
        return carry

    lax.fori_loop(0, 8, ln1_body, 0)
    for j in range(2):
        swap(nrm, j, T_NRM).start()
    z3(CH_A)
    p0_wait(CH_B)
    z1(CH_B)
    s1(CH_A)
    z2(CH_B)
    p0_wait(CH_1)
    z1(CH_1)
    s2(CH_A)
    z3(CH_B)
    s1(CH_B)
    c_copies = a2a_in(1, cot_hbm)
    for cp in c_copies:
        cp.start()
    z2(CH_1)
    for cp in sel_copies:
        cp.wait()

    @pl.when(zz != 0)
    def _():
        rcopy(bias_in, biasb.at[0], bias_s.at[0], bias_r.at[0], other).wait_recv()

    @pl.when(zz != 1)
    def _():
        rcopy(bias_in, biasb.at[1], bias_s.at[0], bias_r.at[1], other).wait_recv()

    for j in range(2):
        swap_wait(nrm, j, T_NRM)
    s3(CH_A)

    lane640 = lax.broadcasted_iota(jnp.int32, (1, 640), 1)
    gate_lane = (lane256 >= 192) & (lane256 < 195)

    def qkv_body(i, carry):
        at = pl.ds(pl.multiple_of(i * tile, tile), tile)
        padded = pl.ds(pl.multiple_of(i * tile + own_tok, own_tok), tile)
        rows = nrm[at, :]
        for slot in range(2):
            mixed = dot(rows, wa[slot], 1, 0)
            scr[slot, at, :] = mixed[:, 512:640]
            mixed = mixed + jnp.where(lane640 < 576, biasb[slot, 1:2, 0:640], 0.0)
            q = mixed[:, 0:256].astype(bf16).astype(f32) * 0.125
            q = jnp.where(lane256 < 192, q, jnp.where(gate_lane, 1.0, 0.0))
            qb[slot, at, :] = q.astype(bf16)
            keys = pltpu.roll(mixed[:, 128:384], 192, 1)
            score = mixed[:, 512:640]
            gate = -(jnp.maximum(-score, 0.0) + jnp.log(1.0 + jnp.exp(-jnp.abs(score))))
            gate = jnp.concatenate([gate, gate], axis=1)
            keys = jnp.where(lane256 < 192, keys, jnp.where(gate_lane, gate, 0.0))
            kb[slot, padded, :] = keys.astype(bf16)
            vb[slot, padded, :] = jnp.where(lane256 < 192, mixed[:, 384:640], 0.0).astype(bf16)
        return carry

    lax.fori_loop(0, 2, qkv_body, 0)
    s2(CH_B)
    z3(CH_1)
    lax.fori_loop(2, 4, qkv_body, 0)
    s1(CH_1)
    p0_wait(CH_2)
    z1(CH_2)

    key_iota = lax.broadcasted_iota(jnp.int32, (seq, 256), 0)

    def one_hot(g):
        return jnp.where(key_iota == selb[g, 4:5, :], 1.0, 0.0).astype(bf16)

    def gather_body(g, carry):
        hot = one_hot(g)
        at = pl.ds(pl.multiple_of(g * 256, 256), 256)
        for slot in range(2):
            ksel[slot, at, :] = dot(hot, kb[slot, own_tok : own_tok + seq, :], 0, 0).astype(bf16)
            vsel[slot, at, :] = dot(hot, vb[slot, own_tok : own_tok + seq, :], 0, 0).astype(bf16)
        return carry

    lax.fori_loop(0, 4, gather_body, 0)
    z2(CH_2)
    s2(CH_1)

    prefix_end = pref[0]

    def windows(b, slot):
        near = pl.ds(pl.multiple_of(b * 64, 64), 192)
        at = pl.ds(pl.multiple_of(b * 64, 64), 64)
        keys = jnp.concatenate([kb[slot, near, :], ksel[slot, at, :]], axis=0)
        vals = jnp.concatenate([vb[slot, near, :], vsel[slot, at, :]], axis=0)
        return at, near, keys, vals

    def fwd_body(b, carry):
        picks = selb[b // 4, pl.ds(b % 4, 1), :]
        key_pos = jnp.where(lane256 < 192, (b - 1) * 64 + lane256, picks)
        query_pos = b * 64 + lax.broadcasted_iota(jnp.int32, (64, 256), 0)
        key_pos = jnp.broadcast_to(key_pos, (64, 256))
        inside = (key_pos >= 0) & (key_pos < seq)
        permitted = (key_pos <= query_pos) | ((query_pos < prefix_end) & (key_pos < prefix_end))
        near_by = jnp.abs(query_pos - key_pos) < 64
        is_near = jnp.broadcast_to(lane256 < 192, (64, 256))
        allowed = inside & permitted & (near_by == is_near)
        fill = jnp.where(allowed, 0.0, MASKED)
        for slot in range(2):
            at, near, keys, vals = windows(b, slot)
            stacked = stack3(qb[slot, at, :], q_rows)
            logits = dot(stacked, keys, 1, 1).reshape(3, 64, 256) + fill[None]
            top = jnp.max(logits, axis=-1, keepdims=True)
            p = jnp.exp(logits - top)
            p = p * (1.0 / jnp.sum(p, axis=-1, keepdims=True))
            p = p.reshape(192, 256).astype(bf16)
            pr[b * 2 + slot] = p
            att[slot, at, :] = fold3(dot(p, vals, 1, 0)).astype(bf16)
        return carry

    lax.fori_loop(0, 4, fwd_body, 0)
    z3(CH_2)
    s1(CH_2)
    a2a_in_wait(c_copies)
    for j in range(2):
        swap(cot, j, T_COT).start()
    lax.fori_loop(4, 10, fwd_body, 0)
    s2(CH_2)
    lax.fori_loop(10, 16, fwd_body, 0)

    s3(CH_B)

    def branch_tile(rows):
        return dot(att[0, rows, :], wb[0], 1, 1) + dot(att[1, rows, :], wb[1], 1, 1)

    for j in range(2):
        st[0, j] = branch_tile(chunk(j, 1 - c)).astype(bf16)
        part(0, j, T_BR).start()
    for j in range(2):
        own = branch_tile(chunk(j, c))
        at = slice(j * tile, (j + 1) * tile)
        part(0, j, T_BR).wait_recv()
        mid[at, :] = (
            xin[at, :].astype(f32) + own + rv[0, j].astype(f32) + vec[2:3, :]
        )

        def ln2_body(i, carry, j=j):
            rows = mid[pl.ds(pl.multiple_of(j * tile + i * own_tok, own_tok), own_tok), :]
            unit, _ = ln_parts(rows)
            n2[pl.ds(natural(j * 4 + i), own_tok), :] = (unit * vec[3:4, :] + vec[4:5, :]).astype(bf16)
            return carry

        lax.fori_loop(0, 4, ln2_body, 0)
        swap(n2, j, T_N2).start()

    s3(CH_1)
    s3(CH_2)
    for j in range(2):
        swap_wait(cot, j, T_COT)
        part(0, j, T_BR).wait_send()

    def mlp_tile(rows):
        out, back = None, None
        for slot in range(2):
            before = dot(n2[rows, :], w1[slot], 1, 0) + biasb[slot, 0:1, :]
            d_act = dot(cot[rows, :], w2[slot], 1, 0)
            square = before * before
            t = jnp.tanh(0.7978845608028654 * before * (1.0 + 0.044715 * square))
            gate = 0.5 * (1.0 + t)
            slope = gate + 0.5 * before * (1.0 - t * t) * (
                0.7978845608028654 * (1.0 + 0.134145 * square)
            )
            low = (before * gate).astype(bf16)
            low_back = (d_act * slope).astype(bf16)
            act[slot, rows, :] = low
            dbf[slot, rows, :] = low_back
            smb[pl.ds(8 + slot + c * (3 - 2 * slot), 1), :] += jnp.sum(
                low_back.astype(f32), axis=0, keepdims=True
            )
            o = dot(low, w2[slot], 1, 1)
            d = dot(low_back, w1[slot], 1, 1)
            out = o if out is None else out + o
            back = d if back is None else back + d
        return out, back

    for j in range(2):
        swap_wait(n2, j, T_N2)


    def peer_mlp(j, carry):
        out, back = mlp_tile(chunk(j, 1 - c))
        st[0, j] = out.astype(bf16)
        st[1, j] = back.astype(bf16)
        part(0, j, T_MLP).start()
        part(1, j, T_DN2).start()
        return carry

    lax.fori_loop(0, 2, peer_mlp, 0)

    def a2a_out(which, stage):
        out = []
        for dx in range(2):
            for dz in range(4):
                xx, z2_ = lax.rem(x + dx, 2), lax.rem(z + dz, 4)
                src = stage.at[pl.ds(pl.multiple_of(xx * tile + z2_ * own_tok, own_tok), own_tok)]
                dst = (res_o, ing_o)[which].at[my_seq]
                idx = dx * 4 + dz
                if idx == 0:
                    out.append(pltpu.make_async_copy(src, dst, aout_r.at[which, 0]))
                else:
                    out.append(
                        rcopy(src, dst, aout_s.at[which, idx], aout_r.at[which, idx], {"xo": xx, "tp": z2_})
                    )
        return out

    def own_mlp(j, carry):
        out, back = mlp_tile(chunk(j, c))
        at = pl.ds(pl.multiple_of(j * tile, tile), tile)
        part(0, j, T_MLP).wait_recv()
        part(1, j, T_DN2).wait_recv()
        stage[at, :] = (mid[at, :] + out + rv[0, j].astype(f32) + vec[5:6, :]).astype(bf16)
        dnr[...] = back + rv[1, j].astype(f32)

        def ln2_back(i, carry):
            here = pl.ds(pl.multiple_of(j * tile + i * own_tok, own_tok), own_tok)
            nat = pl.ds(natural(j * 4 + i), own_tok)
            unit, inverse = ln_parts(mid[here, :])
            up_grad = dnr[pl.ds(pl.multiple_of(i * own_tok, own_tok), own_tok), :]
            grad_rows = cot[nat, :].astype(f32)
            d_mid = grad_rows + ln_back(up_grad, unit, inverse, vec[3:4, :])
            mid[here, :] = d_mid
            dml[nat, :] = d_mid.astype(bf16)
            smb[2:3, :] += jnp.sum(d_mid, axis=0, keepdims=True)
            smb[3:4, :] += jnp.sum(up_grad * unit, axis=0, keepdims=True)
            smb[4:5, :] += jnp.sum(up_grad, axis=0, keepdims=True)
            smb[5:6, :] += jnp.sum(grad_rows, axis=0, keepdims=True)
            return carry

        lax.fori_loop(0, 4, ln2_back, 0)
        swap(dml, j, T_DML).start()
        return carry

    lax.fori_loop(0, 2, own_mlp, 0)

    def weight_grad(g, slot, left, right):
        def body(m, carry):
            at = pl.ds(pl.multiple_of(m * 256, 256), 256)
            g[slot, at, :] = dot(left[:, at], right, 0, 0).astype(bf16)
            return carry

        lax.fori_loop(0, 3, body, 0)

    weight_grad(g2, 0, cot, act[0])
    r1(CH_2, 0)
    weight_grad(g2, 1, cot, act[1])
    r1(CH_2, 1)
    weight_grad(g1, 0, n2, dbf[0])
    r1(CH_1, 0)
    r2(CH_2, 0)
    weight_grad(g1, 1, n2, dbf[1])
    r1(CH_1, 1)
    r2(CH_2, 1)
    res_copies = a2a_out(0, stage)
    for cp in res_copies:
        cp.start()
    for j in range(2):
        swap_wait(dml, j, T_DML)

    def datt_body(i, carry):
        at = pl.ds(pl.multiple_of(i * tile, tile), tile)
        for slot in range(2):
            datt[slot, at, :] = dot(dml[at, :], wb[slot], 1, 0).astype(bf16)
        return carry

    lax.fori_loop(0, 4, datt_body, 0)
    for slot in range(2):
        weight_grad(gb, slot, dml, att[slot])
        r1(CH_B, slot)
    for ref in (dkacc, dvacc):
        ref[...] = jnp.zeros_like(ref)

    def bwd_body(b, carry):
        for slot in range(2):
            at, near, keys, vals = windows(b, slot)
            q_stack = stack3(qb[slot, at, :], q_rows)
            d_stack = stack3(datt[slot, at, :], head_rows)
            p_low = pr[b * 2 + slot]
            p = p_low.astype(f32)
            pdp = p * dot(d_stack, vals, 1, 1)
            dl = (pdp - p * jnp.sum(pdp, axis=-1, keepdims=True)).astype(bf16)
            dbf[slot, at, 512:768] = (fold3(dot(dl, keys, 1, 0)) * 0.125).astype(bf16)
            dk = dot(dl, q_stack, 0, 0)
            dv = dot(p_low, d_stack, 0, 0)
            dkacc[slot, near, :] += dk[0:192]
            dvacc[slot, near, :] += dv[0:192]
            dbf[slot, at, 0:256] = dk[192:256].astype(bf16)
            dbf[slot, at, 256:512] = dv[192:256].astype(bf16)
        return carry

    lax.fori_loop(0, 4, bwd_body, 0)
    r2(CH_1, 0)
    r3(CH_2)
    rz1_(CH_2)
    lax.fori_loop(4, 8, bwd_body, 0)
    r2(CH_1, 1)
    rz2_(CH_2)
    lax.fori_loop(8, 12, bwd_body, 0)
    r3(CH_1)
    rz1_(CH_1)
    rz3_(CH_2)
    r2(CH_B, 0)
    r2(CH_B, 1)
    lax.fori_loop(12, 16, bwd_body, 0)
    rz2_(CH_1)
    rz4_(CH_2)
    rp_start(CH_2)

    sel_pos = jnp.concatenate([selb[g, 4:5, :] for g in range(4)], axis=1)

    def mix_body(i, carry):
        at = pl.ds(pl.multiple_of(i * tile, tile), tile)
        padded = pl.ds(pl.multiple_of(i * tile + own_tok, own_tok), tile)
        key_at = i * tile + lax.broadcasted_iota(jnp.int32, (tile, seq), 0)
        hot = jnp.where(key_at == sel_pos, 1.0, 0.0).astype(bf16)
        for slot in range(2):
            far = dot(hot, dbf[slot, :, 0:512], 1, 0)
            dk = (dkacc[slot, padded, :] + far[:, 0:256]).astype(bf16).astype(f32)
            dv = (dvacc[slot, padded, :] + far[:, 256:512]).astype(bf16).astype(f32)
            dq = dbf[slot, at, 512:768].astype(f32)
            turned = pltpu.roll(dk, 64, 1)
            d_score = dk[:, 128:256] / (1.0 + jnp.exp(scr[slot, at, :]))
            lane128 = lane256[:, 0:128]
            v1 = jnp.where(lane128 < 64, dq[:, 128:256], turned[:, 0:128])
            v4 = jnp.where(lane128 < 64, dv[:, 128:256], jnp.where(lane128 < 67, d_score, 0.0))
            mix = jnp.concatenate([dq[:, 0:128], v1, turned[:, 128:256], dv[:, 0:128], v4], axis=1)
            mix = mix.astype(bf16)
            act[slot, at, 0:640] = mix
            smb[pl.ds(12 + slot + c * (3 - 2 * slot), 1), 0:640] += jnp.sum(
                mix.astype(f32), axis=0, keepdims=True
            )
        return carry

    lax.fori_loop(0, 4, mix_body, 0)
    for slot in range(2):
        weight_grad(ga, slot, nrm, act[slot, :, 0:640])
        r1(CH_A, slot)
    for j in range(2):
        part(0, j, T_MLP).wait_send()
        part(1, j, T_DN2).wait_send()
    rz3_(CH_1)
    r3(CH_B)
    rz1_(CH_B)

    def dnorm_tile(rows):
        return dot(act[0, rows, 0:640], wa[0], 1, 1) + dot(act[1, rows, 0:640], wa[1], 1, 1)

    for j in range(2):
        st[0, j] = dnorm_tile(chunk(j, 1 - c)).astype(bf16)
        part(0, j, T_DNR).start()

    res_copies[0].wait()
    for cp in res_copies[1:]:
        cp.wait_send()

    def own_dnorm(j, carry):
        dnr[...] = dnorm_tile(chunk(j, c))
        part(0, j, T_DNR).wait_recv()

        def ln1_back(i, carry):
            here = pl.ds(pl.multiple_of(j * tile + i * own_tok, own_tok), own_tok)
            local = pl.ds(pl.multiple_of(i * own_tok, own_tok), own_tok)
            unit, inverse = ln_parts(xin[here, :].astype(f32))
            up_grad = dnr[local, :] + rv[0, j, local, :].astype(f32)
            grad = mid[here, :] + ln_back(up_grad, unit, inverse, vec[0:1, :])
            stage[here, :] = grad.astype(bf16)
            smb[0:1, :] += jnp.sum(up_grad * unit, axis=0, keepdims=True)
            smb[1:2, :] += jnp.sum(up_grad, axis=0, keepdims=True)
            return carry

        lax.fori_loop(0, 4, ln1_back, 0)
        return carry

    lax.fori_loop(0, 2, own_dnorm, 0)
    ing_copies = a2a_out(1, stage)
    for cp in ing_copies:
        cp.start()
    for slot in range(2):
        r2(CH_A, slot)
    rz4_(CH_1)
    rp_start(CH_1)
    rz2_(CH_B)
    rz3_(CH_B)
    r3(CH_A)
    rz1_(CH_A)

    hops = [other, over_x, over_y, {"tp": z + 1 - 2 * lax.rem(z, 2)}, {"tp": lax.rem(z + 2, 4)}]

    def hop(i):
        cp = rcopy(smb, smr.at[i], sm_s.at[i], sm_r.at[i], hops[i])
        cp.start()
        cp.wait()
        smb[...] += smr[i]

    hop(0)
    hop(1)
    rz4_(CH_B)
    rp_start(CH_B)
    rz2_(CH_A)
    hop(2)
    hop(3)
    rz3_(CH_A)
    hop(4)
    sm_o[...] = smb[...]
    rz4_(CH_A)
    rp_start(CH_A)

    for k in range(4):
        rp_wait(k)
        ag_drain(k)
        rs_drain(k)
    for j in range(2):
        for buf, idx in ((nrm, T_NRM), (cot, T_COT), (n2, T_N2), (dml, T_DML)):
            swap(buf, j, idx).wait_send()
        part(0, j, T_DNR).wait_send()

    @pl.when(source)
    def _():
        for dz in range(1, 4):
            bias_copy(dz).wait_send()

    for cp in res_copies[1:]:
        cp.wait_recv()
    for cp in ing_copies:
        cp.wait()


def fast_layer(
    inputs, norm1_gain, norm1_bias, qkv_weight, qv_bias, score_weight, out_weight, out_bias,
    norm2_gain, norm2_bias, fc1_weight, fc1_bias, fc2_weight, fc2_bias, prefix, selected, cotangent,
):
    shard, _, cols = qkv_weight.shape
    heads = score_weight.shape[1]
    width = inputs.shape[2]
    own_tok = inputs.shape[1]
    seqs = inputs.shape[0]
    pack_a = jnp.concatenate(
        [qkv_weight.reshape(shard, 3 * cols), score_weight, jnp.zeros((shard, 64 - heads), bf16)], axis=1
    )
    pack_b = jnp.pad(out_weight, ((0, 0), (0, 256 - cols)))
    gap = jnp.zeros((cols,), f32)
    bias_in = jnp.stack(
        [fc1_bias, jnp.concatenate([qv_bias[0], gap, qv_bias[1], gap])] + [jnp.zeros((width,), f32)] * 6
    )
    nothing = jnp.zeros((width,), f32)
    vec = jnp.stack(
        [norm1_gain, norm1_bias, out_bias, norm2_gain, norm2_bias, fc2_bias, nothing, nothing]
    )
    keys = (selected[..., None] * KB + jnp.arange(KB, dtype=jnp.int32)).reshape(seqs, 4, 64)
    sel_rows = jnp.concatenate(
        [
            jnp.pad(keys, ((0, 0), (0, 0), (192, 0))),
            keys.reshape(seqs, 1, 256),
            jnp.zeros((seqs, 3, 256), jnp.int32),
        ],
        axis=1,
    )
    my_prefix = lax.dynamic_slice_in_dim(prefix, lax.axis_index("xo") * 4 + lax.axis_index("tp"), 1, 0)
    seq = 16 * own_tok
    vm = pltpu.VMEM
    ncols = (640, 256, 768, 768)
    hbm = pl.BlockSpec(memory_space=pl.ANY)
    vmem = pl.BlockSpec(memory_space=pltpu.VMEM)
    dma = pltpu.SemaphoreType.DMA
    outs = pl.pallas_call(
        layer_kernel,
        out_shape=[
            jax.ShapeDtypeStruct(inputs.shape, bf16),
            jax.ShapeDtypeStruct(inputs.shape, bf16),
        ]
        + [jax.ShapeDtypeStruct((shard, n), f32) for n in ncols]
        + [jax.ShapeDtypeStruct((16, width), f32)],
        in_specs=[hbm] * 7 + [vmem, vmem, pl.BlockSpec(memory_space=pltpu.SMEM)],
        out_specs=[hbm, hbm] + [vmem] * 5,
        scratch_shapes=[vm((2, 768, n), bf16) for n in ncols]
        + [vm((2, 768, n), bf16) for n in ncols]
        + [vm((6, 2 * shard, n), bf16) for n in ncols]
        + [vm((3, 2 * shard, n), bf16) for n in ncols]
        + [vm((shard, n), bf16) for n in ncols]
        + [
            vm((seq // 2, width), bf16),
            vm((seq, width), bf16),
            vm((seq, width), bf16),
            vm((2, seq, 256), bf16),
            vm((2, seq + 2 * own_tok, 256), bf16),
            vm((2, seq + 2 * own_tok, 256), bf16),
            vm((2, seq, 256), bf16),
            vm((2, seq, 256), bf16),
            vm((32, 192, 256), bf16),
            vm((2, seq, 256), bf16),
            vm((seq // 2, width), f32),
            vm((seq, width), bf16),
            vm((2, seq, 768), bf16),
            vm((2, seq, 768), bf16),
            vm((2, 2, seq // 4, width), bf16),
            vm((2, 2, seq // 4, width), bf16),
            vm((seq // 4, width), f32),
            vm((seq, width), bf16),
            vm((2, seq, 256), bf16),
            vm((2, seq + 2 * own_tok, 256), f32),
            vm((2, seq + 2 * own_tok, 256), f32),
            vm((2, seq, 128), f32),
            vm((seq // 2, width), bf16),
            vm((4, 8, 256), jnp.int32),
            vm((2, 8, 768), f32),
            vm((16, 768), f32),
            vm((5, 16, 768), f32),
            dma((2, 8)), dma((2, 8)), dma((2, 8)), dma((2, 8)),
            dma((4, 10)), dma((4, 10)), dma((4, 10)), dma((4, 10)),
            dma((16,)), dma((16,)), dma((4,)), dma((4,)), dma((4,)), dma((2,)),
            dma((5,)), dma((5,)), dma((4,)),
        ],
        compiler_params=pltpu.CompilerParams(
            collective_id=0, has_side_effects=True, vmem_limit_bytes=67043328
        ),
    )(
        inputs, cotangent, pack_a, pack_b, fc1_weight, fc2_weight, sel_rows, bias_in, vec, my_prefix
    )
    result, input_grad, d_a, d_b, d_1, d_2, small = outs
    tp = lax.axis_index("tp")
    fc1_bias_grad = lax.dynamic_slice_in_dim(small, 8 + tp, 1, 0)[0]
    mixed_sums = lax.dynamic_slice_in_dim(small, 12 + tp, 1, 0)[0]
    return (
        result,
        input_grad,
        small[0],
        small[1],
        d_a[:, : 3 * cols].reshape(shard, 3, cols),
        jnp.stack([mixed_sums[:cols], mixed_sums[2 * cols : 3 * cols]]),
        d_a[:, 3 * cols : 3 * cols + heads],
        d_b[:, :cols],
        small[2],
        small[3],
        small[4],
        d_1,
        fc1_bias_grad,
        d_2,
        small[5],
    )


def general(mesh):
    placed = (
        P("fsdp", ("ctx", "tp"), None),
        P(),
        P(),
        P(("fsdp", "ctx"), None, "tp"),
        P(None, "tp"),
        P(("fsdp", "ctx"), "tp"),
        P(("fsdp", "ctx"), "tp"),
        P(),
        P(),
        P(),
        P(("fsdp", "ctx"), "tp"),
        P("tp"),
        P(("fsdp", "ctx"), "tp"),
        P(),
        P("fsdp"),
        P("fsdp", "ctx", None),
        P("fsdp", ("ctx", "tp"), None),
    )
    return jax.shard_map(
        shards,
        mesh=mesh,
        in_specs=placed,
        out_specs=(
            P("fsdp", ("ctx", "tp"), None),
            P("fsdp", ("ctx", "tp"), None),
            P(),
            P(),
            P(("fsdp", "ctx"), None, "tp"),
            P(None, "tp"),
            P(("fsdp", "ctx"), "tp"),
            P(("fsdp", "ctx"), "tp"),
            P(),
            P(),
            P(),
            P(("fsdp", "ctx"), "tp"),
            P("tp"),
            P(("fsdp", "ctx"), "tp"),
            P(),
        ),
        check_vma=False,
    )


def solution(mesh):
    shape = dict(mesh.shape)
    if shape != {"fsdp": 2, "ctx": 4, "tp": 4}:
        return general(mesh)
    split = Mesh(mesh.devices.reshape(2, 2, 2, 4), ("fsdp", "xo", "team", "tp"))
    ctx = ("xo", "team")
    rows = ("fsdp", "xo", "team")
    tokens = P("fsdp", ("xo", "team", "tp"), None)
    placed = (
        tokens, P(), P(), P(rows, None, "tp"), P(None, "tp"), P(rows, "tp"), P(rows, "tp"), P(), P(), P(),
        P(rows, "tp"), P("tp"), P(rows, "tp"), P(), P("fsdp"), P("fsdp", ctx, None), tokens,
    )
    given = (
        tokens, tokens, P(), P(), P(rows, None, "tp"), P(None, "tp"), P(rows, "tp"), P(rows, "tp"),
        P(), P(), P(), P(rows, "tp"), P("tp"), P(rows, "tp"), P(),
    )
    return jax.shard_map(fast_layer, mesh=split, in_specs=placed, out_specs=given, check_vma=False)
```

```python
from functools import partial

import jax
import jax.numpy as jnp
from jax import lax
from jax.experimental import pallas as pl
from jax.experimental.pallas import tpu as pltpu
from jax.sharding import Mesh
from jax.sharding import PartitionSpec as P

HD = 64
QB = 64
KB = 16
SEL = 4
WIN = 64
SEQ_MB = 4
MICRO = 2


epsilon = 1e-05
negative_fill = -1e30


def contract(left, right, left_dim, right_dim):
    return lax.dot_general(
        left, right, (((left_dim,), (right_dim,)), ((), ())), preferred_element_type=jnp.float32
    )


def rounded(values):
    return values.astype(jnp.bfloat16)


def norm_rows(values, gain, shift):
    centred = values - jnp.mean(values, axis=-1, keepdims=True)
    inverse = lax.rsqrt(jnp.mean(centred * centred, axis=-1, keepdims=True) + epsilon)
    unit_rows = centred * inverse
    return (unit_rows * gain + shift, unit_rows, inverse)


def norm_back(upstream, unit_rows, inverse, gain):
    scaled = upstream * gain
    centred = scaled - jnp.mean(scaled, axis=-1, keepdims=True)
    return inverse * (centred - unit_rows * jnp.mean(scaled * unit_rows, axis=-1, keepdims=True))


def pick_rows(source, key_picks):
    return jax.vmap(lambda table_in, places: table_in[places])(source, key_picks)


def shards(
    inputs,
    norm1_gain,
    norm1_bias,
    qkv_weight,
    qv_bias,
    score_weight,
    out_weight,
    out_bias,
    norm2_gain,
    norm2_bias,
    fc1_weight,
    fc1_bias,
    fc2_weight,
    fc2_bias,
    prefix,
    selected,
    cotangent,
):
    all_seqs, own_tok, width_full = inputs.shape
    ctx_tok = own_tok * lax.axis_size("tp")
    heads_local = score_weight.shape[1]
    hidden_local = out_weight.shape[1]
    units_local = fc1_bias.shape[0]
    seq_full = ctx_tok * lax.axis_size("ctx")
    blocks_local = ctx_tok // QB
    near_span = QB + 2 * WIN
    chosen_span = SEL * KB
    key_count = chosen_span + near_span
    tokens = SEQ_MB * ctx_tok
    score_scale = HD ** (-0.5)
    own_start = lax.axis_index("tp") * own_tok
    block_ids = lax.axis_index("ctx") * blocks_local + jnp.arange(blocks_local, dtype=jnp.int32)
    query_pos = block_ids[:, None] * QB + jnp.arange(QB, dtype=jnp.int32)[None, :]
    near_picks = block_ids[:, None] * QB + jnp.arange(near_span, dtype=jnp.int32)[None, :]
    is_chosen = jnp.arange(key_count) < chosen_span
    qkv_offsets = jnp.stack([qv_bias[0], jnp.zeros_like(qv_bias[0]), qv_bias[1]])
    key_own = lax.axis_index("ctx") * ctx_tok + jnp.arange(ctx_tok, dtype=jnp.int32)
    every_query = jnp.arange(seq_full, dtype=jnp.int32)
    chosen_every = lax.all_gather(selected, "ctx", axis=1, tiled=True)

    def scores_of(queries, keys_near, gates_near, allowed):
        raw_scores = (
            jnp.einsum("sbqhd,sbkhd->sbhqk", queries, keys_near, preferred_element_type=jnp.float32)
            * score_scale
        )
        logits = raw_scores + jnp.transpose(gates_near, (0, 1, 3, 2))[:, :, :, None, :].astype(
            jnp.float32
        )
        return jnp.where(allowed[:, :, None], logits, negative_fill)

    def micro_step(micro_index, carried):
        big_sums, small_sums, out_buffer, grad_buffer = carried
        qkv_full, score_full, out_full, fc1_full, fc2_full = (
            lax.all_gather(qkv_weight, ("fsdp", "ctx"), axis=0, tiled=True),
            lax.all_gather(score_weight, ("fsdp", "ctx"), axis=0, tiled=True),
            lax.all_gather(out_weight, ("fsdp", "ctx"), axis=0, tiled=True),
            lax.all_gather(fc1_weight, ("fsdp", "ctx"), axis=0, tiled=True),
            lax.all_gather(fc2_weight, ("fsdp", "ctx"), axis=0, tiled=True),
        )
        seq_start = micro_index * SEQ_MB
        local_rows = lax.dynamic_slice_in_dim(inputs, seq_start, SEQ_MB, 0)
        full_rows = (
            lax.all_gather(local_rows, "tp", axis=1, tiled=True)
            .astype(jnp.float32)
            .reshape(tokens, width_full)
        )
        normed, unit_one, inverse_one = norm_rows(full_rows, norm1_gain, norm1_bias)
        normed_low = rounded(normed)
        qkv_flat = qkv_full.reshape(width_full, 3 * hidden_local)
        mixed_rows = contract(normed_low, qkv_flat, 1, 0).reshape(tokens, 3, hidden_local)
        mixed_low = rounded(mixed_rows + qkv_offsets)
        scoring = contract(normed_low, score_full, 1, 0)
        gate_low = rounded(jax.nn.log_sigmoid(scoring))
        kv_local = mixed_low[:, 1:].reshape(SEQ_MB, ctx_tok, 2 * hidden_local)
        kv_all, gate_all = (
            lax.all_gather(kv_local, "ctx", axis=1, tiled=True),
            lax.all_gather(
                gate_low.reshape(SEQ_MB, ctx_tok, heads_local), "ctx", axis=1, tiled=True
            ),
        )
        kv_padded = jnp.pad(kv_all, ((0, 0), (WIN, WIN), (0, 0)))
        gate_padded = jnp.pad(gate_all, ((0, 0), (WIN, WIN), (0, 0)))
        chosen = lax.dynamic_slice_in_dim(selected, seq_start, SEQ_MB, 0)
        chosen_picks = (chosen[..., None] * KB + jnp.arange(KB, dtype=jnp.int32) + WIN).reshape(
            SEQ_MB, blocks_local, chosen_span
        )
        key_picks = jnp.concatenate(
            [chosen_picks, jnp.broadcast_to(near_picks, (SEQ_MB, blocks_local, near_span))], axis=-1
        )
        key_pos = (key_picks - WIN)[:, :, None, :]
        query_at = query_pos[None, :, :, None]
        prefix_now = lax.dynamic_slice_in_dim(prefix, seq_start, SEQ_MB, 0)
        prefix_end = prefix_now[:, None, None, None]
        permitted = (key_pos <= query_at) | (query_at < prefix_end) & (key_pos < prefix_end)
        inside = (key_pos >= 0) & (key_pos < seq_full)
        near_by = jnp.abs(query_at - key_pos) < WIN
        allowed = inside & permitted & jnp.where(is_chosen, jnp.logical_not(near_by), near_by)
        kv_near = pick_rows(kv_padded, key_picks).reshape(
            SEQ_MB, blocks_local, key_count, 2, heads_local, HD
        )
        keys_near = kv_near[:, :, :, 0]
        values_near = kv_near[:, :, :, 1]
        gates_near = pick_rows(gate_padded, key_picks)
        queries = mixed_low[:, 0].reshape(SEQ_MB, blocks_local, QB, heads_local, HD)
        logits = scores_of(queries, keys_near, gates_near, allowed)
        row_max = jnp.max(logits, axis=-1, keepdims=True)
        log_total = row_max + jnp.log(jnp.sum(jnp.exp(logits - row_max), axis=-1, keepdims=True))
        probs_low = rounded(jnp.exp(logits - log_total))
        attended = jnp.einsum(
            "sbhqk,sbkhd->sbqhd", probs_low, values_near, preferred_element_type=jnp.float32
        )
        attended_low = rounded(attended).reshape(tokens, hidden_local)
        branch = contract(attended_low, out_full, 1, 1).reshape(SEQ_MB, ctx_tok, width_full)
        middle = (
            local_rows.astype(jnp.float32)
            + lax.psum_scatter(branch, "tp", scatter_dimension=1, tiled=True)
            + out_bias
        )
        middle_full = lax.all_gather(middle, "tp", axis=1, tiled=True).reshape(tokens, width_full)
        normed_two, unit_two, inverse_two = norm_rows(middle_full, norm2_gain, norm2_bias)
        normed_two_low = rounded(normed_two)
        before = contract(normed_two_low, fc1_full, 1, 0) + fc1_bias
        activated, gelu_back = jax.vjp(partial(jax.nn.gelu, approximate=True), before)
        activated_low = rounded(activated)
        mlp_terms = contract(activated_low, fc2_full, 1, 1).reshape(SEQ_MB, ctx_tok, width_full)
        outcome = (
            middle
            + lax.psum_scatter(
                mlp_terms.astype(jnp.bfloat16), "tp", scatter_dimension=1, tiled=True
            ).astype(jnp.float32)
            + fc2_bias
        )
        out_buffer = lax.dynamic_update_slice_in_dim(out_buffer, rounded(outcome), seq_start, 0)
        grad_local = lax.dynamic_slice_in_dim(cotangent, seq_start, SEQ_MB, 0)
        grad_low = lax.all_gather(grad_local, "tp", axis=1, tiled=True).reshape(tokens, width_full)
        grad_rows = grad_low.astype(jnp.float32)
        d_activated = contract(grad_low, fc2_full, 1, 0)
        d_before_low = rounded(gelu_back(d_activated)[0])
        fc2_step = contract(grad_low, activated_low, 0, 0)
        fc1_step = contract(normed_two_low, d_before_low, 0, 0)
        d_normed_two = lax.psum(contract(d_before_low, fc1_full, 1, 1), "tp")
        d_middle = grad_rows + norm_back(d_normed_two, unit_two, inverse_two, norm2_gain)
        d_middle_low = rounded(d_middle)
        out_step = contract(d_middle_low, attended_low, 0, 0)
        d_attended = rounded(contract(d_middle_low, out_full, 1, 0)).reshape(
            SEQ_MB, blocks_local, QB, heads_local, HD
        )
        probs_again = jnp.exp(scores_of(queries, keys_near, gates_near, allowed) - log_total)
        d_probs = jnp.einsum(
            "sbqhd,sbkhd->sbhqk", d_attended, values_near, preferred_element_type=jnp.float32
        )
        row_delta = jnp.sum(probs_again * d_probs, axis=-1, keepdims=True)
        d_logits = probs_again * (d_probs - row_delta)
        d_logits_low = rounded(d_logits)
        d_queries = (
            jnp.einsum(
                "sbhqk,sbkhd->sbqhd", d_logits_low, keys_near, preferred_element_type=jnp.float32
            )
            * score_scale
        )
        stats_local = (
            jnp.transpose(log_total, (0, 1, 3, 2, 4)).reshape(SEQ_MB, ctx_tok, heads_local),
            jnp.transpose(row_delta, (0, 1, 3, 2, 4)).reshape(SEQ_MB, ctx_tok, heads_local),
        )
        queries_flat = mixed_low[:, 0].reshape(SEQ_MB, ctx_tok, hidden_local)
        d_att_flat = d_attended.reshape(SEQ_MB, ctx_tok, hidden_local)
        queries_every, d_att_every = (
            lax.all_gather(queries_flat, "ctx", axis=1, tiled=True),
            lax.all_gather(d_att_flat, "ctx", axis=1, tiled=True),
        )
        log_every, delta_every = (
            lax.all_gather(stats_local[0], "ctx", axis=1, tiled=True),
            lax.all_gather(stats_local[1], "ctx", axis=1, tiled=True),
        )
        chosen_now = lax.dynamic_slice_in_dim(chosen_every, seq_start, SEQ_MB, 0)
        query_all = every_query[None, :, None]
        key_all = key_own[None, None, :]
        end_all = prefix_now[:, None, None]
        permitted_all = (key_all <= query_all) | (query_all < end_all) & (key_all < end_all)
        near_all = jnp.abs(query_all - key_all) < WIN
        block_hits = jnp.any(
            chosen_now[:, :, :, None] == (key_own // KB)[None, None, None, :], axis=2
        )
        member = jnp.repeat(block_hits, QB, axis=1)
        allowed_all = permitted_all & (near_all | member)
        queries_four = queries_every.reshape(SEQ_MB, seq_full, heads_local, HD)
        d_att_four = d_att_every.reshape(SEQ_MB, seq_full, heads_local, HD)
        keys_own = mixed_low[:, 1].reshape(SEQ_MB, ctx_tok, heads_local, HD)
        values_own = mixed_low[:, 2].reshape(SEQ_MB, ctx_tok, heads_local, HD)
        gates_own = gate_low.reshape(SEQ_MB, ctx_tok, heads_local)
        logits_own = (
            jnp.einsum(
                "sqhd,skhd->shqk", queries_four, keys_own, preferred_element_type=jnp.float32
            )
            * score_scale
        )
        logits_own = logits_own + jnp.transpose(gates_own, (0, 2, 1))[:, :, None, :].astype(
            jnp.float32
        )
        logits_own = jnp.where(allowed_all[:, None], logits_own, negative_fill)
        probs_own = jnp.exp(logits_own - jnp.transpose(log_every, (0, 2, 1))[..., None])
        d_probs_own = jnp.einsum(
            "sqhd,skhd->shqk", d_att_four, values_own, preferred_element_type=jnp.float32
        )
        d_logits_own = probs_own * (d_probs_own - jnp.transpose(delta_every, (0, 2, 1))[..., None])
        d_keys_own = (
            jnp.einsum(
                "shqk,sqhd->skhd",
                rounded(d_logits_own),
                queries_four,
                preferred_element_type=jnp.float32,
            )
            * score_scale
        )
        d_values_own = jnp.einsum(
            "shqk,sqhd->skhd", rounded(probs_own), d_att_four, preferred_element_type=jnp.float32
        )
        d_kv_mine = jnp.stack([d_keys_own, d_values_own], axis=2).reshape(
            SEQ_MB, ctx_tok, 2 * hidden_local
        )
        d_gate_mine = jnp.transpose(jnp.sum(d_logits_own, axis=2), (0, 2, 1))
        d_kv_low = rounded(d_kv_mine).reshape(tokens, 2, hidden_local)
        gate_grad = (
            lax.optimization_barrier(rounded(d_gate_mine))
            .astype(jnp.float32)
            .reshape(tokens, heads_local)
        )
        d_scoring_low = rounded(gate_grad * jax.nn.sigmoid(-scoring))
        d_queries_low = rounded(d_queries).reshape(tokens, 1, hidden_local)
        d_mixed = jnp.concatenate([d_queries_low, d_kv_low], axis=1).reshape(
            tokens, 3 * hidden_local
        )
        qkv_step = contract(normed_low, d_mixed, 0, 0).reshape(width_full, 3, hidden_local)
        score_step = contract(normed_low, d_scoring_low, 0, 0)
        d_normed_part = contract(d_mixed, qkv_flat, 1, 1) + contract(
            d_scoring_low, score_full, 1, 1
        )
        d_normed = lax.psum(d_normed_part.astype(jnp.bfloat16), "tp").astype(jnp.float32)
        d_inputs = (d_middle + norm_back(d_normed, unit_one, inverse_one, norm1_gain)).reshape(
            SEQ_MB, ctx_tok, width_full
        )
        d_inputs_mine = lax.dynamic_slice_in_dim(d_inputs, own_start, own_tok, 1)
        grad_buffer = lax.dynamic_update_slice_in_dim(
            grad_buffer, rounded(d_inputs_mine), seq_start, 0
        )
        small_step = (
            jnp.sum(d_normed * unit_one, axis=0),
            jnp.sum(d_normed, axis=0),
            jnp.stack(
                [
                    jnp.sum(d_queries_low[:, 0], axis=0, dtype=jnp.float32),
                    jnp.sum(d_kv_low[:, 1], axis=0, dtype=jnp.float32),
                ]
            ),
            jnp.sum(d_middle, axis=0),
            jnp.sum(d_normed_two * unit_two, axis=0),
            jnp.sum(d_normed_two, axis=0),
            jnp.sum(d_before_low, axis=0, dtype=jnp.float32),
            jnp.sum(grad_rows, axis=0),
        )
        big_step = (qkv_step, score_step, out_step, fc1_step, fc2_step)
        big_sums = jax.tree.map(jnp.add, big_sums, big_step)
        small_sums = jax.tree.map(jnp.add, small_sums, small_step)
        return (big_sums, small_sums, out_buffer, grad_buffer)

    big_init = (
        jnp.zeros((width_full, 3, hidden_local), jnp.float32),
        jnp.zeros((width_full, heads_local), jnp.float32),
        jnp.zeros((width_full, hidden_local), jnp.float32),
        jnp.zeros((width_full, units_local), jnp.float32),
        jnp.zeros((width_full, units_local), jnp.float32),
    )
    small_init = (
        jnp.zeros((width_full,), jnp.float32),
        jnp.zeros((width_full,), jnp.float32),
        jnp.zeros((2, hidden_local), jnp.float32),
        jnp.zeros((width_full,), jnp.float32),
        jnp.zeros((width_full,), jnp.float32),
        jnp.zeros((width_full,), jnp.float32),
        jnp.zeros((units_local,), jnp.float32),
        jnp.zeros((width_full,), jnp.float32),
    )
    buffer_init = jnp.zeros(inputs.shape, jnp.bfloat16)
    big_sums, small_sums, out_buffer, grad_buffer = lax.fori_loop(
        0, MICRO, micro_step, (big_init, small_init, buffer_init, buffer_init)
    )
    big_grads = (
        lax.psum_scatter(big_sums[0], ("fsdp", "ctx"), scatter_dimension=0, tiled=True),
        lax.psum_scatter(big_sums[1], ("fsdp", "ctx"), scatter_dimension=0, tiled=True),
        lax.psum_scatter(big_sums[2], ("fsdp", "ctx"), scatter_dimension=0, tiled=True),
        lax.psum_scatter(big_sums[3], ("fsdp", "ctx"), scatter_dimension=0, tiled=True),
        lax.psum_scatter(big_sums[4], ("fsdp", "ctx"), scatter_dimension=0, tiled=True),
    )
    small_grads = lax.psum(
        (
            small_sums[0],
            small_sums[1],
            small_sums[2],
            small_sums[3],
            small_sums[4],
            small_sums[5],
            small_sums[6],
            small_sums[7],
        ),
        ("fsdp", "ctx"),
    )
    return (
        out_buffer,
        grad_buffer,
        small_grads[0],
        small_grads[1],
        big_grads[0],
        small_grads[2],
        big_grads[1],
        big_grads[2],
        small_grads[3],
        small_grads[4],
        small_grads[5],
        big_grads[3],
        small_grads[6],
        big_grads[4],
        small_grads[7],
    )


EPS = 1e-05
MASKED = -1e30
MESH_ID = pl.DeviceIdType.MESH
CH_A, CH_B, CH_1, CH_2 = 0, 1, 2, 3
f32 = jnp.float32
bf16 = jnp.bfloat16


def dot(left, right, left_dim, right_dim):
    return lax.dot_general(
        left, right, (((left_dim,), (right_dim,)), ((), ())), preferred_element_type=f32
    )


def ln_parts(rows):
    centred = rows - jnp.mean(rows, axis=-1, keepdims=True)
    inverse = lax.rsqrt(jnp.mean(centred * centred, axis=-1, keepdims=True) + EPS)
    return centred * inverse, inverse


def ln_back(upstream, unit, inverse, gain):
    scaled = upstream * gain
    return inverse * (
        scaled
        - jnp.mean(scaled, axis=-1, keepdims=True)
        - unit * jnp.mean(scaled * unit, axis=-1, keepdims=True)
    )


PLAN = {
    "front": (("p0w", 0), ("za", 0, 0), ("za", 0, 1), ("a2a", "x"), ("s1", 0, 0), ("p0w", 2),),
    "x_wait": (("s1", 0, 1), ("p0w", 1), ("za", 1, 0), ("s2", 0, 1), ("s2", 0, 0), ("za", 2, 0), ("p0w", 3),),
    "ln1": (("za", 3, 1), ("s1", 2, 0), ("za", 3, 0),),
    "nrm_wait": (("s1", 1, 0), ("za", 1, 1),),
    "qkv2": (("a2a", "cot"),),
    "gat0": (("s2", 2, 0),),
    "gat1": (("s1", 1, 1),),
    "gat3": (("s1", 3, 0),),
    "fwd5": (("s2", 1, 1),),
    "fwd6": (("s2", 1, 0),),
    "fwd8": (("s2", 3, 0),),
    "fwd14": (("cotw",),),
    "brs": (("s1", 3, 1),),
    "br0": (("za", 2, 1),),
    "mlpa0": (("s1", 2, 1),),
    "mlpa3": (("s2", 3, 1), ("s2", 2, 1),),
    "om1": (("r2", 2, 0), ("r2", 3, 0),),
    "datt": (("r3", 2, 0),),
    "bwd5": (("r3b", 2, 0), ("r3", 3, 0),),
    "bwd7": (("a2a", "res"),),
    "bwd12": (("r2", 3, 1),),
    "bwd15": (("r2", 1, 0), ("r2", 2, 1),),
    "ga0": (("r3", 2, 1),),
    "dn0": (("r3", 3, 1),),
    "od0": (("r3b", 3, 0), ("r2", 1, 1),),
    "e0": (("hs", 0),),
    "e2": (("r2", 0, 0),),
    "e3": (("r3b", 3, 1),),
    "e4": (("r3", 1, 0), ("r3", 0, 0),),
    "e5": (("hw", 0), ("hs", 1), ("r2", 0, 1), ("r3b", 2, 1), ("hw", 1),),
    "e6": (("r3", 1, 1), ("r4", 2),),
    "e10": (("hs", 2),),
    "e11": (("hw", 2), ("r3b", 1, 0),),
    "e12": (("r3b", 0, 0), ("hs", 3),),
    "e13": (("r3b", 1, 1),),
    "e15": (("r4", 1),),
    "e16": (("r4", 3),),
    "e19": (("r3", 0, 1), ("hw", 3),),
    "e20": (("hs", 4), ("r3b", 0, 1), ("r4", 0),),
    "e21": (("hw", 4),),
}
AG_DIRECT, RS_DIRECT = (), ()
AG_XLIGHT = {(2, 0), (3, 1), (0, 0), (1, 0), (1, 1)}
RS_XLIGHT = {(2, 0), (3, 1), (0, 0), (0, 1), (1, 0), (1, 1)}


def layer_kernel(
    x_hbm, cot_hbm, wq_hbm, ws_hbm, wo_hbm, f1_hbm, f2_hbm, sel_hbm, n1g, n1b, ob, n2g, n2b, f2b, f1b, qvb, pref,
    res_o, ing_o, ga_o, gb_o, g1_o, g2_o, sm_o,
    wa, wb, w1, w2, ga,
    rba, rbb, rb1, rb2, rza, rzb, rz1, rz2, rpa, rpb, rp1, rp2,
    xin, cot, nrm, qb, kb, vb, ksel, vsel, pr, att, mid, n2, act, dbf,
    st, rv, dnr, dml, datt, acc, scr, stage, selraw, selb, wq, ws, wo, pa, pb, v0, v1, v2, v3, v4, v5, fb0, fb1, qvbb, smb, smr,
    ain_s, ain_r, aout_s, aout_r, ag_s, ag_r, rs_s, rs_r, tm_s, tm_r,
    sel_s, sel_r, bias_s, bias_r, sm_s, sm_r, loc, gout,
):
    y = lax.axis_index("fsdp")
    x = lax.axis_index("xo")
    c = lax.axis_index("team")
    z = lax.axis_index("tp")
    zz = z + c * (3 - 2 * z)
    source = zz < 2
    own_tok = x_hbm.shape[1]
    width = x_hbm.shape[2]
    tile = 4 * own_tok
    half = 2 * tile
    seq = 2 * half
    my_seq = x * 4 + z
    hbms = (pa, pb, f1_hbm, f2_hbm)
    weights = (wa, wb, w1, w2)
    grads = (ga, wb, w1, w2)
    rbs = (rba, rbb, rb1, rb2)
    rzs = (rza, rzb, rz1, rz2)
    rps = (rpa, rpb, rp1, rp2)
    g_outs = (ga_o, gb_o, g1_o, g2_o)
    shard = f1_hbm.shape[0]
    pair = 2 * shard
    over_x, over_y, other = {"xo": 1 - x}, {"fsdp": 1 - y}, {"team": 1 - c}

    def block(yy, xx):
        return pl.ds(pl.multiple_of((yy * 4 + xx * 2) * shard, pair), pair)

    mine = block(y, x)
    vecs, fbs = (v0, v1, v2, v3, v4, v5), (fb0, fb1)

    def vec(i):
        return vecs[i][...].reshape(1, width)

    far_x, far_y = block(y, 1 - x), block(1 - y, x)
    far_xy = block(1 - y, 1 - x)

    def at_zz(q):
        return {"tp": q + c * (3 - 2 * q)}

    def own_shard(cc):
        return pl.ds(pl.multiple_of((y * 4 + x * 2 + cc) * shard, shard), shard)

    def rcopy(src, dst, ss, rs, dev):
        return pltpu.make_async_remote_copy(
            src_ref=src, dst_ref=dst, send_sem=ss, recv_sem=rs, device_id=dev, device_id_type=MESH_ID
        )

    bar = pltpu.get_barrier_semaphore()
    peers = []
    for dx in range(2):
        for dz in range(4):
            if dx or dz:
                peers.append({"xo": lax.rem(x + dx, 2), "tp": lax.rem(z + dz, 4)})
    peers += [other, over_y, {"xo": 1 - x, "team": 1 - c}]
    for peer in peers:
        pl.semaphore_signal(bar, 1, device_id=peer, device_id_type=MESH_ID)
    pl.semaphore_wait(bar, len(peers))

    def a2a_in(which, hbm):
        out = []
        for dx in range(2):
            for dz in range(4):
                xx, z2 = lax.rem(x + dx, 2), lax.rem(z + dz, 4)
                if which == 0:
                    at = pl.ds(pl.multiple_of(x * tile + z * own_tok, own_tok), own_tok)
                    dst = xin.at[at]
                else:
                    at = pl.ds(pl.multiple_of(x * half + c * tile + z * own_tok, own_tok), own_tok)
                    dst = cot.at[at]
                idx = dx * 4 + dz
                src = hbm.at[xx * 4 + z2]
                if idx == 0:
                    out.append(pltpu.make_async_copy(src, dst, ain_r.at[which, 0]))
                else:
                    out.append(
                        rcopy(src, dst, ain_s.at[which, idx], ain_r.at[which, idx], {"xo": xx, "tp": z2})
                    )
        return out

    def a2a_in_wait(copies):
        copies[0].wait()
        for cp in copies[1:]:
            cp.wait()

    def p0_local(k):
        return pltpu.make_async_copy(hbms[k], weights[k].at[zz, own_shard(c)], loc.at[k])

    def p0_away(k):
        return rcopy(
            hbms[k], weights[k].at[3 - zz, own_shard(c)], ag_s.at[k, 5], ag_r.at[k, 2], other
        )

    def p0_back(k):
        return rcopy(
            hbms[k], weights[k].at[zz, own_shard(1 - c)], ag_s.at[k, 5], ag_r.at[k, 2], other
        )

    def p0_start(k):
        @pl.when(source)
        def _():
            p0_local(k).start()

        @pl.when(jnp.logical_not(source))
        def _():
            p0_away(k).start()

    def p0_wait(k):
        @pl.when(source)
        def _():
            p0_local(k).wait()
            p0_back(k).wait_recv()

        @pl.when(jnp.logical_not(source))
        def _():
            p0_away(k).wait_send()

    def z_copy(k, s, q, idx):
        ref = weights[k].at[s, mine]
        return rcopy(ref, ref, ag_s.at[k, idx], ag_r.at[k, s], at_zz(q))

    def z_sends(k, s):
        out = [z_copy(k, s, 2, 0), z_copy(k, s, 1 - s, 1)]
        if k in AG_DIRECT:
            out.append(z_copy(k, s, 3, 2))
        return out

    def z_start(k, s):
        @pl.when(zz == s)
        def _():
            for cp in z_sends(k, s):
                cp.start()

    def xy(k, s, which):
        light = (k, s) in AG_XLIGHT
        rows, dev = (
            (mine, over_x),
            (mine, over_y),
            (far_x, over_y) if light else (far_y, over_x),
        )[which]
        ref = weights[k].at[s, rows]
        return rcopy(ref, ref, ag_s.at[k, 6 + 3 * s + which], ag_r.at[k, 3 + 3 * s + which], dev)

    def s1(k, s):
        @pl.when(zz != s)
        def _():
            z_copy(k, s, 2, 0).wait_recv()

        if k not in AG_DIRECT:
            @pl.when(zz == 2)
            def _():
                z_copy(k, s, 3, 3 + s).start()

        for which in (0, 1) if (k, s) in AG_XLIGHT else (1, 0):
            xy(k, s, which).start()

    def s2(k, s):
        xy(k, s, 0 if (k, s) in AG_XLIGHT else 1).wait_recv()
        xy(k, s, 2).start()

    def s3(k, s):
        for which in (1 if (k, s) in AG_XLIGHT else 0, 2):
            xy(k, s, which).wait_recv()

    def ag_drain(k, s):
        @pl.when(zz == s)
        def _():
            for cp in z_sends(k, s):
                cp.wait_send()

        if k not in AG_DIRECT:
            @pl.when(zz == 2)
            def _():
                z_copy(k, s, 3, 3 + s).wait_send()

        for which in range(3):
            xy(k, s, which).wait_send()

    def rs_copy(k, s, which):
        light = (k, s) in RS_XLIGHT
        rows, dev = (
            (far_xy, over_y if light else over_x),
            (far_y, over_y) if light else (far_x, over_x),
            (far_x, over_x) if light else (far_y, over_y),
        )[which]
        i = 3 * s + which
        return rcopy(grads[k].at[s, rows], rbs[k].at[i], rs_s.at[k, i], rs_r.at[k, i], dev)

    def add_rows(k, slot, rows, bufs):
        g = grads[k]
        total = g[slot, rows, :].astype(f32)
        for buf in bufs:
            total = total + buf[...].astype(f32)
        g[slot, rows, :] = total.astype(bf16)

    def r1(k, s):
        for which in range(2):
            rs_copy(k, s, which).start()

    def r2(k, s):
        rs_copy(k, s, 0).wait_recv()
        add_rows(k, s, far_x if (k, s) in RS_XLIGHT else far_y, [rbs[k].at[3 * s]])
        rs_copy(k, s, 2).start()

    def rz_copy(k, s, q, idx):
        return rcopy(
            grads[k].at[s, mine], rzs[k].at[idx], rs_s.at[k, 6 + s], rs_r.at[k, 6 + idx], at_zz(q)
        )

    def rz_last(k, s):
        return rz_copy(k, s, s, 2) if k in RS_DIRECT else rz_copy(k, s, 2, s)

    def r3(k, s):
        for which in range(1, 3):
            rs_copy(k, s, which).wait_recv()
        add_rows(k, s, mine, [rbs[k].at[3 * s + 1], rbs[k].at[3 * s + 2]])

        @pl.when(zz == 3)
        def _():
            rz_last(k, s).start()

        @pl.when(zz == 1 - s)
        def _():
            rz_copy(k, s, s, 0).start()

    def r3b(k, s):
        @pl.when(zz == 2)
        def _():
            if k not in RS_DIRECT:
                rz_copy(k, s, 2, s).wait_recv()
                add_rows(k, s, mine, [rzs[k].at[s]])
            rz_copy(k, s, s, 1).start()

    def rp_copy(k):
        return rcopy(
            grads[k].at[zz, own_shard(1 - c)], rps[k], rs_s.at[k, 8], rs_r.at[k, 9], other
        )

    def keep_own(k):
        return pltpu.make_async_copy(grads[k].at[zz, own_shard(c)], g_outs[k], gout.at[k])

    def keep_got(k):
        return pltpu.make_async_copy(rps[k], g_outs[k], gout.at[k])

    def r4(k):
        came = range(3) if k in RS_DIRECT else range(2)
        for s in range(2):
            @pl.when(zz == s)
            def _(s=s):
                for idx in came:
                    rz_copy(k, s, s, idx).wait_recv()
                add_rows(k, s, mine, [rzs[k].at[idx] for idx in came])

        @pl.when(source)
        def _():
            rp_copy(k).start()
            keep_own(k).start()

    def rp_wait(k):
        @pl.when(jnp.logical_not(source))
        def _():
            rcopy(rps[k], rps[k], rs_s.at[k, 8], rs_r.at[k, 9], other).wait_recv()
            keep_got(k).start()

        @pl.when(source)
        def _():
            rp_copy(k).wait_send()

    def rs_drain(k):
        keep_got(k).wait()
        for s in range(2):
            for which in range(3):
                rs_copy(k, s, which).wait_send()

            @pl.when((zz >= 2) | (zz == 1 - s))
            def _(s=s):
                rz_copy(k, s, s, 0).wait_send()

    def chunk(j, cc):
        return pl.ds(pl.multiple_of(j * half + cc * tile, tile), tile)

    def swap(buf, j, idx):
        return rcopy(buf.at[chunk(j, c)], buf.at[chunk(j, c)], tm_s.at[idx + j], tm_r.at[idx + j], other)

    def swap_wait(buf, j, idx):
        rcopy(buf.at[chunk(j, 1 - c)], buf.at[chunk(j, 1 - c)], tm_s.at[idx + j], tm_r.at[idx + j], other).wait_recv()

    def part(which, j, idx):
        return rcopy(st.at[which, j], rv.at[which, j], tm_s.at[idx + j], tm_r.at[idx + j], other)

    T_NRM, T_COT, T_BR, T_N2, T_MLP, T_DN2, T_DML, T_DNR = range(0, 16, 2)

    lane256 = lax.broadcasted_iota(jnp.int32, (1, 256), 1)
    head_rows = [jnp.where(lane256 // 64 == h, 1.0, 0.0).astype(f32) for h in range(3)]
    q_rows = [
        jnp.where((lane256 // 64 == h) | (lane256 == 192 + h), 1.0, 0.0).astype(f32) for h in range(3)
    ]

    def stack3(rows, masks):
        wide = rows.astype(f32)
        return jnp.concatenate([(wide * m).astype(bf16) for m in masks], axis=0)

    def fold3(stacked):
        n = stacked.shape[0] // 3
        return (
            stacked[:n] * head_rows[0] + stacked[n : 2 * n] * head_rows[1] + stacked[2 * n :] * head_rows[2]
        )

    sends = {"x": lambda: a2a_in(0, x_hbm), "cot": lambda: a2a_in(1, cot_hbm), "res": lambda: a2a_out(0, stage)}
    hops = [other, over_x, over_y, {"tp": z + 1 - 2 * lax.rem(z, 2)}, {"tp": lax.rem(z + 2, 4)}]

    def hop(i):
        return rcopy(smb, smr.at[i], sm_s.at[i], sm_r.at[i], hops[i])

    def hop_wait(i):
        hop(i).wait()
        smb[...] += smr[i]

    def a2a_start(name):
        for cp in sends[name]():
            cp.start()

    def cot_here():
        a2a_in_wait(a2a_in(1, cot_hbm))
        for j in range(2):
            swap(cot, j, T_COT).start()

    steps = {
        "p0w": p0_wait, "za": z_start, "s1": s1, "s2": s2, "r2": r2, "r3": r3, "r3b": r3b, "r4": r4,
        "a2a": a2a_start, "cotw": cot_here, "hs": lambda i: hop(i).start(), "hw": hop_wait,
    }

    def point(name):
        for step in PLAN.get(name, ()):
            steps[step[0]](*step[1:])

    def points(name, i, count):
        for n in range(count):
            if name + str(n) in PLAN:
                @pl.when(i == n)
                def _(n=n):
                    point(name + str(n))

    def a2a_out(which, stage):
        out = []
        for dx in range(2):
            for dz in range(4):
                xx, z2_ = lax.rem(x + dx, 2), lax.rem(z + dz, 4)
                src = stage.at[pl.ds(pl.multiple_of(xx * tile + z2_ * own_tok, own_tok), own_tok)]
                dst = (res_o, ing_o)[which].at[my_seq]
                idx = dx * 4 + dz
                if idx == 0:
                    out.append(pltpu.make_async_copy(src, dst, aout_r.at[which, 0]))
                else:
                    out.append(
                        rcopy(src, dst, aout_s.at[which, idx], aout_r.at[which, idx], {"xo": xx, "tp": z2_})
                    )
        return out

    def weights_in():
        return [
            pltpu.make_async_copy(src, dst, loc.at[4 + i])
            for i, (src, dst) in enumerate(((wq_hbm, wq), (ws_hbm, ws), (wo_hbm, wo)))
        ]

    def vectors_in():
        return [
            pltpu.make_async_copy(src, dst, loc.at[7 + i])
            for i, (src, dst) in enumerate(zip((n1g, n1b, ob, n2g, n2b, f2b), vecs))
        ]

    def bias_copies(s, dz):
        dev = {"tp": lax.rem(z + dz, 4)}
        return [
            rcopy(src, buf, bias_s.at[i, dz], bias_r.at[i, s], dev)
            for i, (src, buf) in enumerate(((f1b, fbs[s]), (qvb, qvbb.at[s])))
        ]

    def bias_own(s):
        return [
            pltpu.make_async_copy(src, buf, bias_s.at[i, 0])
            for i, (src, buf) in enumerate(((f1b, fbs[s]), (qvb, qvbb.at[s])))
        ]

    for cp in weights_in():
        cp.start()
    for cp in vectors_in():
        cp.start()
    for k in (CH_1, CH_2):
        p0_start(k)

    def place(rows, cols, first):
        i = lax.broadcasted_iota(jnp.int32, (rows, cols), 0)
        j = lax.broadcasted_iota(jnp.int32, (rows, cols), 1)
        return jnp.where(j == i + first, 1.0, 0.0).astype(bf16)

    for cp in weights_in():
        cp.wait()
    head_cols = wq.shape[2]
    packed = dot(ws[...], place(ws.shape[0], 640, 3 * head_cols), 0, 0)
    for i in range(3):
        packed = packed + dot(wq[i], place(head_cols, 640, i * head_cols), 1, 0)
    pa[...] = packed.astype(bf16)
    pb[...] = dot(wo[...], place(head_cols, 256, 0), 1, 0).astype(bf16)
    for k in (CH_A, CH_B):
        p0_start(k)
    point("front")
    sel_copies = []
    for dx in range(2):
        for dc in range(2):
            idx = dx * 2 + dc
            xx, cc = lax.rem(x + dx, 2), lax.rem(c + dc, 2)
            src, dst = sel_hbm, selraw.at[x * 2 + c]
            if idx == 0:
                sel_copies.append(pltpu.make_async_copy(src, dst, sel_r.at[0]))
            else:
                sel_copies.append(
                    rcopy(src, dst, sel_s.at[idx], sel_r.at[idx], {"xo": xx, "team": cc})
                )
    for cp in sel_copies:
        cp.start()

    for s in range(2):
        @pl.when(zz == s)
        def _(s=s):
            for dz in range(1, 4):
                for cp in bias_copies(s, dz):
                    cp.start()
            for cp in bias_own(s):
                cp.start()

    zero_k = jnp.zeros((own_tok, 256), bf16)
    for ref in (kb, vb):
        for slot in range(2):
            ref[slot, 0:own_tok, :] = zero_k
            ref[slot, seq + own_tok : seq + 2 * own_tok, :] = zero_k
    smb[...] = jnp.zeros_like(smb)
    for cp in vectors_in():
        cp.wait()
    point("x_wait")
    a2a_in_wait(a2a_in(0, x_hbm))

    def natural(i):
        return pl.multiple_of((i // 4) * half + c * tile + (i % 4) * own_tok, own_tok)

    def ln1_body(i, carry):
        rows = xin[pl.ds(pl.multiple_of(i * own_tok, own_tok), own_tok), :].astype(f32)
        unit, _ = ln_parts(rows)
        nrm[pl.ds(natural(i), own_tok), :] = (unit * vec(0) + vec(1)).astype(bf16)
        return carry

    point("ln1")
    lax.fori_loop(0, 8, ln1_body, 0)
    for j in range(2):
        swap(nrm, j, T_NRM).start()

    for cp in sel_copies:
        cp.wait()
    lane_seq = lax.broadcasted_iota(jnp.int32, selraw.shape[1:], 2)
    sub = lax.broadcasted_iota(jnp.int32, (SEL, 256), 0)
    lane = lax.broadcasted_iota(jnp.int32, (SEL, 256), 1)
    inner = (lane % KB).astype(f32)
    for g in range(4):
        chosen = jnp.sum(jnp.where(lane_seq == my_seq, selraw[g].astype(f32), 0.0), axis=2, keepdims=True)
        every = jnp.zeros((1, 256), f32)
        for b in range(4):
            keys = jnp.broadcast_to(chosen[b], (SEL, 256)) * KB + inner
            here = jnp.sum(jnp.where(lane // KB == sub + 192 // KB, keys, 0.0), axis=0, keepdims=True)
            selb[g, b : b + 1, :] = here.astype(jnp.int32)
            every = every + jnp.sum(
                jnp.where(lane // KB == sub + b * SEL, keys, 0.0), axis=0, keepdims=True
            )
        selb[g, 4:5, :] = every.astype(jnp.int32)

    for s in range(2):
        @pl.when(zz != s)
        def _(s=s):
            for cp in bias_copies(s, 1):
                cp.wait_recv()

        @pl.when(zz == s)
        def _(s=s):
            for cp in bias_own(s):
                cp.wait()

    point("nrm_wait")
    for j in range(2):
        swap_wait(nrm, j, T_NRM)
    for s in range(2):
        s3(CH_A, s)

    gate_lane = (lane256 >= 192) & (lane256 < 195)

    gap = jnp.zeros((1, 640 - 3 * head_cols), f32)
    none = jnp.zeros((1, head_cols), f32)
    mix_bias = [
        jnp.concatenate([qvbb[slot, 0:1, :], none, qvbb[slot, 1:2, :], gap], axis=1) for slot in range(2)
    ]

    def qkv_body(i, carry):
        points("qkv", i, 4)
        at = pl.ds(pl.multiple_of(i * tile, tile), tile)
        padded = pl.ds(pl.multiple_of(i * tile + own_tok, own_tok), tile)
        rows = nrm[at, :]
        for slot in range(2):
            mixed = dot(rows, wa[slot], 1, 0)
            scr[slot, at, :] = mixed[:, 512:640]
            mixed = mixed + mix_bias[slot]
            q = mixed[:, 0:256].astype(bf16).astype(f32) * 0.125
            q = jnp.where(lane256 < 192, q, jnp.where(gate_lane, 1.0, 0.0))
            qb[slot, at, :] = q.astype(bf16)
            keys = pltpu.roll(mixed[:, 128:384], 192, 1)
            score = mixed[:, 512:640]
            gate = -(jnp.maximum(-score, 0.0) + jnp.log(1.0 + jnp.exp(-jnp.abs(score))))
            gate = jnp.concatenate([gate, gate], axis=1)
            keys = jnp.where(lane256 < 192, keys, jnp.where(gate_lane, gate, 0.0))
            kb[slot, padded, :] = keys.astype(bf16)
            vb[slot, padded, :] = jnp.where(lane256 < 192, mixed[:, 384:640], 0.0).astype(bf16)
        return carry

    lax.fori_loop(0, 4, qkv_body, 0)

    key_iota = lax.broadcasted_iota(jnp.int32, (seq, 256), 0)

    def one_hot(g):
        return jnp.where(key_iota == selb[g, 4:5, :], 1.0, 0.0).astype(bf16)

    def gather_body(g, carry):
        points("gat", g, 4)
        hot = one_hot(g)
        at = pl.ds(pl.multiple_of(g * 256, 256), 256)
        for slot in range(2):
            ksel[slot, at, :] = dot(hot, kb[slot, own_tok : own_tok + seq, :], 0, 0).astype(bf16)
            vsel[slot, at, :] = dot(hot, vb[slot, own_tok : own_tok + seq, :], 0, 0).astype(bf16)
        return carry

    lax.fori_loop(0, 4, gather_body, 0)

    prefix_end = pref[my_seq]

    def windows(b, slot):
        near = pl.ds(pl.multiple_of(b * 64, 64), 192)
        at = pl.ds(pl.multiple_of(b * 64, 64), 64)
        keys = jnp.concatenate([kb[slot, near, :], ksel[slot, at, :]], axis=0)
        vals = jnp.concatenate([vb[slot, near, :], vsel[slot, at, :]], axis=0)
        return at, near, keys, vals

    def fwd_body(b, carry):
        points("fwd", b, 16)
        picks = selb[b // 4, pl.ds(b % 4, 1), :]
        key_pos = jnp.where(lane256 < 192, (b - 1) * 64 + lane256, picks)
        query_pos = b * 64 + lax.broadcasted_iota(jnp.int32, (64, 256), 0)
        key_pos = jnp.broadcast_to(key_pos, (64, 256))
        inside = (key_pos >= 0) & (key_pos < seq)
        permitted = (key_pos <= query_pos) | ((query_pos < prefix_end) & (key_pos < prefix_end))
        near_by = jnp.abs(query_pos - key_pos) < 64
        is_near = jnp.broadcast_to(lane256 < 192, (64, 256))
        allowed = inside & permitted & (near_by == is_near)
        fill = jnp.where(allowed, 0.0, MASKED)
        for slot in range(2):
            at, near, keys, vals = windows(b, slot)
            stacked = stack3(qb[slot, at, :], q_rows)
            logits = dot(stacked, keys, 1, 1).reshape(3, 64, 256) + fill[None]
            top = jnp.max(logits, axis=-1, keepdims=True)
            p = jnp.exp(logits - top)
            p = p * (1.0 / jnp.sum(p, axis=-1, keepdims=True))
            p = p.reshape(192, 256).astype(bf16)
            pr[b * 2 + slot] = p
            att[slot, at, :] = fold3(dot(p, vals, 1, 0)).astype(bf16)
        return carry

    lax.fori_loop(0, 16, fwd_body, 0)

    point("brs")
    for s in range(2):
        s3(CH_B, s)

    def branch_tile(rows):
        return dot(att[0, rows, :], wb[0], 1, 1) + dot(att[1, rows, :], wb[1], 1, 1)

    for j in range(2):
        st[0, j] = branch_tile(chunk(j, 1 - c)).astype(bf16)
        part(0, j, T_BR).start()
    for j in range(2):
        point("br" + str(j))
        own = branch_tile(chunk(j, c))
        at = slice(j * tile, (j + 1) * tile)
        part(0, j, T_BR).wait_recv()
        mid[at, :] = (
            xin[at, :].astype(f32) + own + rv[0, j].astype(f32) + vec(2)
        )

        def ln2_body(i, carry, j=j):
            rows = mid[pl.ds(pl.multiple_of(j * tile + i * own_tok, own_tok), own_tok), :]
            unit, _ = ln_parts(rows)
            n2[pl.ds(natural(j * 4 + i), own_tok), :] = (unit * vec(3) + vec(4)).astype(bf16)
            return carry

        lax.fori_loop(0, 4, ln2_body, 0)
        swap(n2, j, T_N2).start()

    point("mlpa0")
    for k in (CH_1, CH_2):
        s3(k, 0)
    for j in range(2):
        swap_wait(cot, j, T_COT)
        part(0, j, T_BR).wait_send()
        swap_wait(n2, j, T_N2)

    def mlp_tile(rows, slot):
        before = dot(n2[rows, :], w1[slot], 1, 0) + fbs[slot][...].reshape(1, width)
        d_act = dot(cot[rows, :], w2[slot], 1, 0)
        square = before * before
        t = jnp.tanh(0.7978845608028654 * before * (1.0 + 0.044715 * square))
        gate = 0.5 * (1.0 + t)
        slope = gate + 0.5 * before * (1.0 - t * t) * (
            0.7978845608028654 * (1.0 + 0.134145 * square)
        )
        low = (before * gate).astype(bf16)
        low_back = (d_act * slope).astype(bf16)
        act[slot, rows, :] = low
        dbf[slot, rows, :] = low_back
        smb[pl.ds(8 + slot + c * (3 - 2 * slot), 1), :] += jnp.sum(
            low_back.astype(f32), axis=0, keepdims=True
        )
        return dot(low, w2[slot], 1, 1), dot(low_back, w1[slot], 1, 1)

    def first_mlp(i, carry):
        @pl.when(i > 0)
        def _():
            points("mlpa", i, 4)

        at = pl.ds(pl.multiple_of(i * tile, tile), tile)
        out, back = mlp_tile(at, 0)
        acc[0, at, :] = out
        acc[1, at, :] = back
        return carry

    lax.fori_loop(0, 4, first_mlp, 0)

    def weight_grad(g, slot, left, right):
        def body(m, carry):
            at = pl.ds(pl.multiple_of(m * 256, 256), 256)
            g[slot, at, :] = dot(left[:, at], right, 0, 0).astype(bf16)
            return carry

        lax.fori_loop(0, 3, body, 0)

    def ff_grads(slot):
        for k, name, left, right in ((CH_2, "g2", cot, act), (CH_1, "g1", n2, dbf)):
            point(name + str(slot))
            ag_drain(k, slot)
            weight_grad(grads[k], slot, left, right[slot])
            r1(k, slot)

    ff_grads(0)
    point("pm0")
    for k in (CH_1, CH_2):
        s3(k, 1)

    def peer_mlp(j, carry):
        @pl.when(j == 1)
        def _():
            point("pm1")

        rows = chunk(j, 1 - c)
        out, back = mlp_tile(rows, 1)
        st[0, j] = (acc[0, rows, :] + out).astype(bf16)
        st[1, j] = (acc[1, rows, :] + back).astype(bf16)
        part(0, j, T_MLP).start()
        part(1, j, T_DN2).start()
        return carry

    lax.fori_loop(0, 2, peer_mlp, 0)

    def own_mlp(j, carry):
        points("om", j, 2)
        rows = chunk(j, c)
        out, back = mlp_tile(rows, 1)
        out = acc[0, rows, :] + out
        back = acc[1, rows, :] + back
        at = pl.ds(pl.multiple_of(j * tile, tile), tile)
        part(0, j, T_MLP).wait_recv()
        part(1, j, T_DN2).wait_recv()
        stage[at, :] = (mid[at, :] + out + rv[0, j].astype(f32) + vec(5)).astype(bf16)
        dnr[...] = back + rv[1, j].astype(f32)

        def ln2_back(i, carry):
            here = pl.ds(pl.multiple_of(j * tile + i * own_tok, own_tok), own_tok)
            nat = pl.ds(natural(j * 4 + i), own_tok)
            unit, inverse = ln_parts(mid[here, :])
            up_grad = dnr[pl.ds(pl.multiple_of(i * own_tok, own_tok), own_tok), :]
            grad_rows = cot[nat, :].astype(f32)
            d_mid = grad_rows + ln_back(up_grad, unit, inverse, vec(3))
            mid[here, :] = d_mid
            dml[nat, :] = d_mid.astype(bf16)
            smb[2:3, :] += jnp.sum(d_mid, axis=0, keepdims=True)
            smb[3:4, :] += jnp.sum(up_grad * unit, axis=0, keepdims=True)
            smb[4:5, :] += jnp.sum(up_grad, axis=0, keepdims=True)
            smb[5:6, :] += jnp.sum(grad_rows, axis=0, keepdims=True)
            return carry

        lax.fori_loop(0, 4, ln2_back, 0)
        swap(dml, j, T_DML).start()
        return carry

    lax.fori_loop(0, 2, own_mlp, 0)

    ff_grads(1)
    point("datt")
    for j in range(2):
        swap_wait(dml, j, T_DML)

    def datt_body(i, carry):
        at = pl.ds(pl.multiple_of(i * tile, tile), tile)
        for slot in range(2):
            datt[slot, at, :] = dot(dml[at, :], wb[slot], 1, 0).astype(bf16)
        return carry

    lax.fori_loop(0, 4, datt_body, 0)
    for slot in range(2):
        point("gb" + str(slot))
        ag_drain(CH_B, slot)
        weight_grad(wb, slot, dml, att[slot])
        r1(CH_B, slot)
    acc[:, :, 0:512] = jnp.zeros((2, seq + 2 * own_tok, 512), f32)

    def bwd_body(b, carry):
        points("bwd", b, 16)
        for slot in range(2):
            at, near, keys, vals = windows(b, slot)
            q_stack = stack3(qb[slot, at, :], q_rows)
            d_stack = stack3(datt[slot, at, :], head_rows)
            p_low = pr[b * 2 + slot]
            p = p_low.astype(f32)
            pdp = p * dot(d_stack, vals, 1, 1)
            dl = (pdp - p * jnp.sum(pdp, axis=-1, keepdims=True)).astype(bf16)
            dbf[slot, at, 512:768] = (fold3(dot(dl, keys, 1, 0)) * 0.125).astype(bf16)
            dk = dot(dl, q_stack, 0, 0)
            dv = dot(p_low, d_stack, 0, 0)
            side = slice(slot * 256, slot * 256 + 256)
            acc[0, near, side] += dk[0:192]
            acc[1, near, side] += dv[0:192]
            dbf[slot, at, 0:256] = dk[192:256].astype(bf16)
            dbf[slot, at, 256:512] = dv[192:256].astype(bf16)
        return carry

    lax.fori_loop(0, 16, bwd_body, 0)
    point("mix")

    sel_pos = jnp.concatenate([selb[g, 4:5, :] for g in range(4)], axis=1)

    def mix_body(i, carry):
        at = pl.ds(pl.multiple_of(i * tile, tile), tile)
        padded = pl.ds(pl.multiple_of(i * tile + own_tok, own_tok), tile)
        key_at = i * tile + lax.broadcasted_iota(jnp.int32, (tile, seq), 0)
        hot = jnp.where(key_at == sel_pos, 1.0, 0.0).astype(bf16)
        for slot in range(2):
            far = dot(hot, dbf[slot, :, 0:512], 1, 0)
            dk = (acc[0, padded, slot * 256 : slot * 256 + 256] + far[:, 0:256]).astype(bf16).astype(f32)
            dv = (acc[1, padded, slot * 256 : slot * 256 + 256] + far[:, 256:512]).astype(bf16).astype(f32)
            dq = dbf[slot, at, 512:768].astype(f32)
            turned = pltpu.roll(dk, 64, 1)
            d_score = dk[:, 128:256] / (1.0 + jnp.exp(scr[slot, at, :]))
            lane128 = lane256[:, 0:128]
            v1 = jnp.where(lane128 < 64, dq[:, 128:256], turned[:, 0:128])
            v4 = jnp.where(lane128 < 64, dv[:, 128:256], jnp.where(lane128 < 67, d_score, 0.0))
            mix = jnp.concatenate([dq[:, 0:128], v1, turned[:, 128:256], dv[:, 0:128], v4], axis=1)
            mix = mix.astype(bf16)
            act[slot, at, 0:640] = mix
            smb[pl.ds(12 + slot + c * (3 - 2 * slot), 1), 0:640] += jnp.sum(
                mix.astype(f32), axis=0, keepdims=True
            )
        return carry

    lax.fori_loop(0, 4, mix_body, 0)
    for slot in range(2):
        point("ga" + str(slot))
        weight_grad(ga, slot, nrm, act[slot, :, 0:640])
        r1(CH_A, slot)
    point("dn0")
    for j in range(2):
        part(0, j, T_MLP).wait_send()
        part(1, j, T_DN2).wait_send()

    def dnorm_tile(rows):
        return dot(act[0, rows, 0:640], wa[0], 1, 1) + dot(act[1, rows, 0:640], wa[1], 1, 1)

    for j in range(2):
        st[0, j] = dnorm_tile(chunk(j, 1 - c)).astype(bf16)
        part(0, j, T_DNR).start()

    res_copies = a2a_out(0, stage)
    res_copies[0].wait()
    for cp in res_copies[1:]:
        cp.wait_send()

    def own_dnorm(j, carry):
        points("od", j, 2)
        dnr[...] = dnorm_tile(chunk(j, c))
        part(0, j, T_DNR).wait_recv()

        def ln1_back(i, carry):
            here = pl.ds(pl.multiple_of(j * tile + i * own_tok, own_tok), own_tok)
            local = pl.ds(pl.multiple_of(i * own_tok, own_tok), own_tok)
            unit, inverse = ln_parts(xin[here, :].astype(f32))
            up_grad = dnr[local, :] + rv[0, j, local, :].astype(f32)
            grad = mid[here, :] + ln_back(up_grad, unit, inverse, vec(0))
            stage[here, :] = grad.astype(bf16)
            smb[0:1, :] += jnp.sum(up_grad * unit, axis=0, keepdims=True)
            smb[1:2, :] += jnp.sum(up_grad, axis=0, keepdims=True)
            return carry

        lax.fori_loop(0, 4, ln1_back, 0)
        return carry

    lax.fori_loop(0, 2, own_dnorm, 0)
    ing_copies = a2a_out(1, stage)
    for cp in ing_copies:
        cp.start()
    for i in range(24):
        point("e" + str(i))

    small = pltpu.make_async_copy(smb, sm_o, gout.at[4])
    small.start()
    for k in (CH_2, CH_1, CH_B, CH_A):
        rp_wait(k)
    for s in range(2):
        ag_drain(CH_A, s)
    for k in range(4):
        rs_drain(k)
    small.wait()
    for j in range(2):
        for buf, idx in ((nrm, T_NRM), (cot, T_COT), (n2, T_N2), (dml, T_DML)):
            swap(buf, j, idx).wait_send()
        part(0, j, T_DNR).wait_send()

    for s in range(2):
        @pl.when(zz == s)
        def _(s=s):
            for dz in range(1, 4):
                for cp in bias_copies(s, dz):
                    cp.wait_send()

    for cp in res_copies[1:]:
        cp.wait_recv()
    for cp in ing_copies:
        cp.wait()


def finish_kernel(
    res_i, ing_i, ga_i, gb_i, g1_i, g2_i, sm_i,
    res_o, ing_o, n1g, n1b, wq_o, qvb, ws_o, wo_o, ob, n2g, n2b, g1_o, f1b, g2_o, f2b,
    res, ing, sem,
):
    moves = [(res_i, res, res_o), (ing_i, ing, ing_o)]
    for i, (src, buf, _) in enumerate(moves):
        pltpu.make_async_copy(src, buf, sem.at[0, i]).start()
    z = lax.axis_index("tp")
    for row, ref in enumerate((n1g, n1b, ob, n2g, n2b, f2b)):
        ref[...] = sm_i[row, :]
    f1b[...] = sm_i[pl.ds(8 + z, 1), :][0]
    cols = wo_o.shape[1]
    mixed = sm_i[pl.ds(12 + z, 1), :]
    qvb[0:1, :] = mixed[:, 0:cols]
    qvb[1:2, :] = mixed[:, 2 * cols : 3 * cols]
    g1_o[...] = g1_i[...].astype(f32)
    g2_o[...] = g2_i[...].astype(f32)
    wo_o[...] = gb_i[:, 0:cols].astype(f32)
    i = lax.broadcasted_iota(jnp.int32, (640, cols), 0)
    j = lax.broadcasted_iota(jnp.int32, (640, cols), 1)
    for part in range(3):
        wq_o[part] = dot(ga_i[...], jnp.where(i == j + part * cols, 1.0, 0.0).astype(bf16), 1, 0)
    heads = ws_o.shape[0]
    i = lax.broadcasted_iota(jnp.int32, (heads, 640), 0)
    j = lax.broadcasted_iota(jnp.int32, (heads, 640), 1)
    ws_o[...] = dot(jnp.where(j == i + 3 * cols, 1.0, 0.0).astype(bf16), ga_i[...], 1, 1)
    for i, (src, buf, dst) in enumerate(moves):
        pltpu.make_async_copy(src, buf, sem.at[0, i]).wait()
        pltpu.make_async_copy(buf, dst, sem.at[1, i]).start()
    for i, (src, buf, dst) in enumerate(moves):
        pltpu.make_async_copy(buf, dst, sem.at[1, i]).wait()


def fast_layer(
    inputs, norm1_gain, norm1_bias, qkv_weight, qv_bias, score_weight, out_weight, out_bias,
    norm2_gain, norm2_bias, fc1_weight, fc1_bias, fc2_weight, fc2_bias, prefix, selected, cotangent,
):
    shard, _, cols = qkv_weight.shape
    heads = score_weight.shape[1]
    width = inputs.shape[2]
    own_tok = inputs.shape[1]
    seqs = inputs.shape[0]
    seq = 16 * own_tok
    vm = pltpu.VMEM
    ncols = (640, 256, 768, 768)
    hbm = pl.BlockSpec(memory_space=pl.ANY)
    vmem = pl.BlockSpec(memory_space=pltpu.VMEM)
    dma = pltpu.SemaphoreType.DMA
    outs = pl.pallas_call(
        layer_kernel,
        out_shape=[
            jax.ShapeDtypeStruct(inputs.shape, bf16),
            jax.ShapeDtypeStruct(inputs.shape, bf16),
        ]
        + [jax.ShapeDtypeStruct((shard, n), bf16) for n in ncols]
        + [jax.ShapeDtypeStruct((16, width), f32)],
        in_specs=[hbm] * 16 + [pl.BlockSpec(memory_space=pltpu.SMEM)],
        out_specs=[hbm] * 7,
        scratch_shapes=[vm((2, 768, n), bf16) for n in ncols]
        + [vm((2, 768, 640), bf16)]
        + [vm((6, 2 * shard, n), bf16) for n in ncols]
        + [vm((3 if k in RS_DIRECT else 2, 2 * shard, n), bf16) for k, n in enumerate(ncols)]
        + [vm((shard, n), bf16) for n in ncols]
        + [
            vm((seq // 2, width), bf16),
            vm((seq, width), bf16),
            vm((seq, width), bf16),
            vm((2, seq, 256), bf16),
            vm((2, seq + 2 * own_tok, 256), bf16),
            vm((2, seq + 2 * own_tok, 256), bf16),
            vm((2, seq, 256), bf16),
            vm((2, seq, 256), bf16),
            vm((32, 192, 256), bf16),
            vm((2, seq, 256), bf16),
            vm((seq // 2, width), f32),
            vm((seq, width), bf16),
            vm((2, seq, 768), bf16),
            vm((2, seq, 768), bf16),
            vm((2, 2, seq // 4, width), bf16),
            vm((2, 2, seq // 4, width), bf16),
            vm((seq // 4, width), f32),
            vm((seq, width), bf16),
            vm((2, seq, 256), bf16),
            vm((2, seq + 2 * own_tok, 768), f32),
            vm((2, seq, 128), f32),
            vm((seq // 2, width), bf16),
            vm((4, 4, 4, seqs), jnp.int32),
            vm((4, 8, 256), jnp.int32),
            vm((3, shard, cols), bf16),
            vm((heads, shard), bf16),
            vm((shard, cols), bf16),
            vm((shard, 640), bf16),
            vm((shard, 256), bf16),
        ]
        + [vm((width,), f32)] * 8
        + [
            vm((2, 2, cols), f32),
            vm((16, 768), f32),
            vm((5, 16, 768), f32),
            dma((2, 8)), dma((2, 8)), dma((2, 8)), dma((2, 8)),
            dma((4, 12)), dma((4, 9)), dma((4, 9)), dma((4, 10)),
            dma((16,)), dma((16,)), dma((4,)), dma((4,)), dma((2, 4)), dma((2, 2)),
            dma((5,)), dma((5,)), dma((13,)), dma((5,)),
        ],
        compiler_params=pltpu.CompilerParams(
            collective_id=0, has_side_effects=True, vmem_limit_bytes=67043328
        ),
    )(
        inputs, cotangent, jnp.transpose(qkv_weight, (1, 0, 2)), jnp.transpose(score_weight), out_weight,
        fc1_weight, fc2_weight, jnp.transpose(selected, (1, 2, 0)), norm1_gain, norm1_bias,
        out_bias, norm2_gain, norm2_bias, fc2_bias, fc1_bias, qv_bias, prefix,
    )
    line = jax.ShapeDtypeStruct((width,), f32)
    square = jax.ShapeDtypeStruct((shard, 768), f32)
    done = pl.pallas_call(
        finish_kernel,
        out_shape=[
            jax.ShapeDtypeStruct(inputs.shape, bf16), jax.ShapeDtypeStruct(inputs.shape, bf16), line, line,
            jax.ShapeDtypeStruct((3, shard, cols), f32), jax.ShapeDtypeStruct((2, cols), f32),
            jax.ShapeDtypeStruct((heads, shard), f32), jax.ShapeDtypeStruct((shard, cols), f32),
            line, line, line, square, line, square, line,
        ],
        in_specs=[hbm, hbm] + [vmem] * 5,
        out_specs=[hbm, hbm] + [vmem] * 13,
        scratch_shapes=[vm(inputs.shape, bf16), vm(inputs.shape, bf16), dma((2, 2))],
    )(*outs)
    done = list(done)
    done[4] = jnp.transpose(done[4], (1, 0, 2))
    done[6] = jnp.transpose(done[6])
    return tuple(done)


def general(mesh):
    placed = (
        P("fsdp", ("ctx", "tp"), None),
        P(),
        P(),
        P(("fsdp", "ctx"), None, "tp"),
        P(None, "tp"),
        P(("fsdp", "ctx"), "tp"),
        P(("fsdp", "ctx"), "tp"),
        P(),
        P(),
        P(),
        P(("fsdp", "ctx"), "tp"),
        P("tp"),
        P(("fsdp", "ctx"), "tp"),
        P(),
        P("fsdp"),
        P("fsdp", "ctx", None),
        P("fsdp", ("ctx", "tp"), None),
    )
    return jax.shard_map(
        shards,
        mesh=mesh,
        in_specs=placed,
        out_specs=(
            P("fsdp", ("ctx", "tp"), None),
            P("fsdp", ("ctx", "tp"), None),
            P(),
            P(),
            P(("fsdp", "ctx"), None, "tp"),
            P(None, "tp"),
            P(("fsdp", "ctx"), "tp"),
            P(("fsdp", "ctx"), "tp"),
            P(),
            P(),
            P(),
            P(("fsdp", "ctx"), "tp"),
            P("tp"),
            P(("fsdp", "ctx"), "tp"),
            P(),
        ),
        check_vma=False,
    )


def solution(mesh):
    shape = dict(mesh.shape)
    if shape != {"fsdp": 2, "ctx": 4, "tp": 4}:
        return general(mesh)
    split = Mesh(mesh.devices.reshape(2, 2, 2, 4), ("fsdp", "xo", "team", "tp"))
    ctx = ("xo", "team")
    rows = ("fsdp", "xo", "team")
    tokens = P("fsdp", ("xo", "team", "tp"), None)
    placed = (
        tokens, P(), P(), P(rows, None, "tp"), P(None, "tp"), P(rows, "tp"), P(rows, "tp"), P(), P(), P(),
        P(rows, "tp"), P("tp"), P(rows, "tp"), P(), P("fsdp"), P("fsdp", ctx, None), tokens,
    )
    given = (
        tokens, tokens, P(), P(), P(rows, None, "tp"), P(None, "tp"), P(rows, "tp"), P(rows, "tp"),
        P(), P(), P(), P(rows, "tp"), P("tp"), P(rows, "tp"), P(),
    )
    return jax.shard_map(fast_layer, mesh=split, in_specs=placed, out_specs=given, check_vma=False)
```

```python
from functools import partial

import jax
import jax.numpy as jnp
from jax import lax
from jax.experimental import pallas as pl
from jax.experimental.pallas import tpu as pltpu
from jax.sharding import Mesh
from jax.sharding import PartitionSpec as P

HD = 64
QB = 64
KB = 16
SEL = 4
WIN = 64
SEQ_MB = 4
MICRO = 2


epsilon = 1e-05
negative_fill = -1e30


def contract(left, right, left_dim, right_dim):
    return lax.dot_general(
        left, right, (((left_dim,), (right_dim,)), ((), ())), preferred_element_type=jnp.float32
    )


def rounded(values):
    return values.astype(jnp.bfloat16)


def norm_rows(values, gain, shift):
    centred = values - jnp.mean(values, axis=-1, keepdims=True)
    inverse = lax.rsqrt(jnp.mean(centred * centred, axis=-1, keepdims=True) + epsilon)
    unit_rows = centred * inverse
    return (unit_rows * gain + shift, unit_rows, inverse)


def norm_back(upstream, unit_rows, inverse, gain):
    scaled = upstream * gain
    centred = scaled - jnp.mean(scaled, axis=-1, keepdims=True)
    return inverse * (centred - unit_rows * jnp.mean(scaled * unit_rows, axis=-1, keepdims=True))


def pick_rows(source, key_picks):
    return jax.vmap(lambda table_in, places: table_in[places])(source, key_picks)


def shards(
    inputs,
    norm1_gain,
    norm1_bias,
    qkv_weight,
    qv_bias,
    score_weight,
    out_weight,
    out_bias,
    norm2_gain,
    norm2_bias,
    fc1_weight,
    fc1_bias,
    fc2_weight,
    fc2_bias,
    prefix,
    selected,
    cotangent,
):
    all_seqs, own_tok, width_full = inputs.shape
    ctx_tok = own_tok * lax.axis_size("tp")
    heads_local = score_weight.shape[1]
    hidden_local = out_weight.shape[1]
    units_local = fc1_bias.shape[0]
    seq_full = ctx_tok * lax.axis_size("ctx")
    blocks_local = ctx_tok // QB
    near_span = QB + 2 * WIN
    chosen_span = SEL * KB
    key_count = chosen_span + near_span
    tokens = SEQ_MB * ctx_tok
    score_scale = HD ** (-0.5)
    own_start = lax.axis_index("tp") * own_tok
    block_ids = lax.axis_index("ctx") * blocks_local + jnp.arange(blocks_local, dtype=jnp.int32)
    query_pos = block_ids[:, None] * QB + jnp.arange(QB, dtype=jnp.int32)[None, :]
    near_picks = block_ids[:, None] * QB + jnp.arange(near_span, dtype=jnp.int32)[None, :]
    is_chosen = jnp.arange(key_count) < chosen_span
    qkv_offsets = jnp.stack([qv_bias[0], jnp.zeros_like(qv_bias[0]), qv_bias[1]])
    key_own = lax.axis_index("ctx") * ctx_tok + jnp.arange(ctx_tok, dtype=jnp.int32)
    every_query = jnp.arange(seq_full, dtype=jnp.int32)
    chosen_every = lax.all_gather(selected, "ctx", axis=1, tiled=True)

    def scores_of(queries, keys_near, gates_near, allowed):
        raw_scores = (
            jnp.einsum("sbqhd,sbkhd->sbhqk", queries, keys_near, preferred_element_type=jnp.float32)
            * score_scale
        )
        logits = raw_scores + jnp.transpose(gates_near, (0, 1, 3, 2))[:, :, :, None, :].astype(
            jnp.float32
        )
        return jnp.where(allowed[:, :, None], logits, negative_fill)

    def micro_step(micro_index, carried):
        big_sums, small_sums, out_buffer, grad_buffer = carried
        qkv_full, score_full, out_full, fc1_full, fc2_full = (
            lax.all_gather(qkv_weight, ("fsdp", "ctx"), axis=0, tiled=True),
            lax.all_gather(score_weight, ("fsdp", "ctx"), axis=0, tiled=True),
            lax.all_gather(out_weight, ("fsdp", "ctx"), axis=0, tiled=True),
            lax.all_gather(fc1_weight, ("fsdp", "ctx"), axis=0, tiled=True),
            lax.all_gather(fc2_weight, ("fsdp", "ctx"), axis=0, tiled=True),
        )
        seq_start = micro_index * SEQ_MB
        local_rows = lax.dynamic_slice_in_dim(inputs, seq_start, SEQ_MB, 0)
        full_rows = (
            lax.all_gather(local_rows, "tp", axis=1, tiled=True)
            .astype(jnp.float32)
            .reshape(tokens, width_full)
        )
        normed, unit_one, inverse_one = norm_rows(full_rows, norm1_gain, norm1_bias)
        normed_low = rounded(normed)
        qkv_flat = qkv_full.reshape(width_full, 3 * hidden_local)
        mixed_rows = contract(normed_low, qkv_flat, 1, 0).reshape(tokens, 3, hidden_local)
        mixed_low = rounded(mixed_rows + qkv_offsets)
        scoring = contract(normed_low, score_full, 1, 0)
        gate_low = rounded(jax.nn.log_sigmoid(scoring))
        kv_local = mixed_low[:, 1:].reshape(SEQ_MB, ctx_tok, 2 * hidden_local)
        kv_all, gate_all = (
            lax.all_gather(kv_local, "ctx", axis=1, tiled=True),
            lax.all_gather(
                gate_low.reshape(SEQ_MB, ctx_tok, heads_local), "ctx", axis=1, tiled=True
            ),
        )
        kv_padded = jnp.pad(kv_all, ((0, 0), (WIN, WIN), (0, 0)))
        gate_padded = jnp.pad(gate_all, ((0, 0), (WIN, WIN), (0, 0)))
        chosen = lax.dynamic_slice_in_dim(selected, seq_start, SEQ_MB, 0)
        chosen_picks = (chosen[..., None] * KB + jnp.arange(KB, dtype=jnp.int32) + WIN).reshape(
            SEQ_MB, blocks_local, chosen_span
        )
        key_picks = jnp.concatenate(
            [chosen_picks, jnp.broadcast_to(near_picks, (SEQ_MB, blocks_local, near_span))], axis=-1
        )
        key_pos = (key_picks - WIN)[:, :, None, :]
        query_at = query_pos[None, :, :, None]
        prefix_now = lax.dynamic_slice_in_dim(prefix, seq_start, SEQ_MB, 0)
        prefix_end = prefix_now[:, None, None, None]
        permitted = (key_pos <= query_at) | (query_at < prefix_end) & (key_pos < prefix_end)
        inside = (key_pos >= 0) & (key_pos < seq_full)
        near_by = jnp.abs(query_at - key_pos) < WIN
        allowed = inside & permitted & jnp.where(is_chosen, jnp.logical_not(near_by), near_by)
        kv_near = pick_rows(kv_padded, key_picks).reshape(
            SEQ_MB, blocks_local, key_count, 2, heads_local, HD
        )
        keys_near = kv_near[:, :, :, 0]
        values_near = kv_near[:, :, :, 1]
        gates_near = pick_rows(gate_padded, key_picks)
        queries = mixed_low[:, 0].reshape(SEQ_MB, blocks_local, QB, heads_local, HD)
        logits = scores_of(queries, keys_near, gates_near, allowed)
        row_max = jnp.max(logits, axis=-1, keepdims=True)
        log_total = row_max + jnp.log(jnp.sum(jnp.exp(logits - row_max), axis=-1, keepdims=True))
        probs_low = rounded(jnp.exp(logits - log_total))
        attended = jnp.einsum(
            "sbhqk,sbkhd->sbqhd", probs_low, values_near, preferred_element_type=jnp.float32
        )
        attended_low = rounded(attended).reshape(tokens, hidden_local)
        branch = contract(attended_low, out_full, 1, 1).reshape(SEQ_MB, ctx_tok, width_full)
        middle = (
            local_rows.astype(jnp.float32)
            + lax.psum_scatter(branch, "tp", scatter_dimension=1, tiled=True)
            + out_bias
        )
        middle_full = lax.all_gather(middle, "tp", axis=1, tiled=True).reshape(tokens, width_full)
        normed_two, unit_two, inverse_two = norm_rows(middle_full, norm2_gain, norm2_bias)
        normed_two_low = rounded(normed_two)
        before = contract(normed_two_low, fc1_full, 1, 0) + fc1_bias
        activated, gelu_back = jax.vjp(partial(jax.nn.gelu, approximate=True), before)
        activated_low = rounded(activated)
        mlp_terms = contract(activated_low, fc2_full, 1, 1).reshape(SEQ_MB, ctx_tok, width_full)
        outcome = (
            middle
            + lax.psum_scatter(
                mlp_terms.astype(jnp.bfloat16), "tp", scatter_dimension=1, tiled=True
            ).astype(jnp.float32)
            + fc2_bias
        )
        out_buffer = lax.dynamic_update_slice_in_dim(out_buffer, rounded(outcome), seq_start, 0)
        grad_local = lax.dynamic_slice_in_dim(cotangent, seq_start, SEQ_MB, 0)
        grad_low = lax.all_gather(grad_local, "tp", axis=1, tiled=True).reshape(tokens, width_full)
        grad_rows = grad_low.astype(jnp.float32)
        d_activated = contract(grad_low, fc2_full, 1, 0)
        d_before_low = rounded(gelu_back(d_activated)[0])
        fc2_step = contract(grad_low, activated_low, 0, 0)
        fc1_step = contract(normed_two_low, d_before_low, 0, 0)
        d_normed_two = lax.psum(contract(d_before_low, fc1_full, 1, 1), "tp")
        d_middle = grad_rows + norm_back(d_normed_two, unit_two, inverse_two, norm2_gain)
        d_middle_low = rounded(d_middle)
        out_step = contract(d_middle_low, attended_low, 0, 0)
        d_attended = rounded(contract(d_middle_low, out_full, 1, 0)).reshape(
            SEQ_MB, blocks_local, QB, heads_local, HD
        )
        probs_again = jnp.exp(scores_of(queries, keys_near, gates_near, allowed) - log_total)
        d_probs = jnp.einsum(
            "sbqhd,sbkhd->sbhqk", d_attended, values_near, preferred_element_type=jnp.float32
        )
        row_delta = jnp.sum(probs_again * d_probs, axis=-1, keepdims=True)
        d_logits = probs_again * (d_probs - row_delta)
        d_logits_low = rounded(d_logits)
        d_queries = (
            jnp.einsum(
                "sbhqk,sbkhd->sbqhd", d_logits_low, keys_near, preferred_element_type=jnp.float32
            )
            * score_scale
        )
        stats_local = (
            jnp.transpose(log_total, (0, 1, 3, 2, 4)).reshape(SEQ_MB, ctx_tok, heads_local),
            jnp.transpose(row_delta, (0, 1, 3, 2, 4)).reshape(SEQ_MB, ctx_tok, heads_local),
        )
        queries_flat = mixed_low[:, 0].reshape(SEQ_MB, ctx_tok, hidden_local)
        d_att_flat = d_attended.reshape(SEQ_MB, ctx_tok, hidden_local)
        queries_every, d_att_every = (
            lax.all_gather(queries_flat, "ctx", axis=1, tiled=True),
            lax.all_gather(d_att_flat, "ctx", axis=1, tiled=True),
        )
        log_every, delta_every = (
            lax.all_gather(stats_local[0], "ctx", axis=1, tiled=True),
            lax.all_gather(stats_local[1], "ctx", axis=1, tiled=True),
        )
        chosen_now = lax.dynamic_slice_in_dim(chosen_every, seq_start, SEQ_MB, 0)
        query_all = every_query[None, :, None]
        key_all = key_own[None, None, :]
        end_all = prefix_now[:, None, None]
        permitted_all = (key_all <= query_all) | (query_all < end_all) & (key_all < end_all)
        near_all = jnp.abs(query_all - key_all) < WIN
        block_hits = jnp.any(
            chosen_now[:, :, :, None] == (key_own // KB)[None, None, None, :], axis=2
        )
        member = jnp.repeat(block_hits, QB, axis=1)
        allowed_all = permitted_all & (near_all | member)
        queries_four = queries_every.reshape(SEQ_MB, seq_full, heads_local, HD)
        d_att_four = d_att_every.reshape(SEQ_MB, seq_full, heads_local, HD)
        keys_own = mixed_low[:, 1].reshape(SEQ_MB, ctx_tok, heads_local, HD)
        values_own = mixed_low[:, 2].reshape(SEQ_MB, ctx_tok, heads_local, HD)
        gates_own = gate_low.reshape(SEQ_MB, ctx_tok, heads_local)
        logits_own = (
            jnp.einsum(
                "sqhd,skhd->shqk", queries_four, keys_own, preferred_element_type=jnp.float32
            )
            * score_scale
        )
        logits_own = logits_own + jnp.transpose(gates_own, (0, 2, 1))[:, :, None, :].astype(
            jnp.float32
        )
        logits_own = jnp.where(allowed_all[:, None], logits_own, negative_fill)
        probs_own = jnp.exp(logits_own - jnp.transpose(log_every, (0, 2, 1))[..., None])
        d_probs_own = jnp.einsum(
            "sqhd,skhd->shqk", d_att_four, values_own, preferred_element_type=jnp.float32
        )
        d_logits_own = probs_own * (d_probs_own - jnp.transpose(delta_every, (0, 2, 1))[..., None])
        d_keys_own = (
            jnp.einsum(
                "shqk,sqhd->skhd",
                rounded(d_logits_own),
                queries_four,
                preferred_element_type=jnp.float32,
            )
            * score_scale
        )
        d_values_own = jnp.einsum(
            "shqk,sqhd->skhd", rounded(probs_own), d_att_four, preferred_element_type=jnp.float32
        )
        d_kv_mine = jnp.stack([d_keys_own, d_values_own], axis=2).reshape(
            SEQ_MB, ctx_tok, 2 * hidden_local
        )
        d_gate_mine = jnp.transpose(jnp.sum(d_logits_own, axis=2), (0, 2, 1))
        d_kv_low = rounded(d_kv_mine).reshape(tokens, 2, hidden_local)
        gate_grad = (
            lax.optimization_barrier(rounded(d_gate_mine))
            .astype(jnp.float32)
            .reshape(tokens, heads_local)
        )
        d_scoring_low = rounded(gate_grad * jax.nn.sigmoid(-scoring))
        d_queries_low = rounded(d_queries).reshape(tokens, 1, hidden_local)
        d_mixed = jnp.concatenate([d_queries_low, d_kv_low], axis=1).reshape(
            tokens, 3 * hidden_local
        )
        qkv_step = contract(normed_low, d_mixed, 0, 0).reshape(width_full, 3, hidden_local)
        score_step = contract(normed_low, d_scoring_low, 0, 0)
        d_normed_part = contract(d_mixed, qkv_flat, 1, 1) + contract(
            d_scoring_low, score_full, 1, 1
        )
        d_normed = lax.psum(d_normed_part.astype(jnp.bfloat16), "tp").astype(jnp.float32)
        d_inputs = (d_middle + norm_back(d_normed, unit_one, inverse_one, norm1_gain)).reshape(
            SEQ_MB, ctx_tok, width_full
        )
        d_inputs_mine = lax.dynamic_slice_in_dim(d_inputs, own_start, own_tok, 1)
        grad_buffer = lax.dynamic_update_slice_in_dim(
            grad_buffer, rounded(d_inputs_mine), seq_start, 0
        )
        small_step = (
            jnp.sum(d_normed * unit_one, axis=0),
            jnp.sum(d_normed, axis=0),
            jnp.stack(
                [
                    jnp.sum(d_queries_low[:, 0], axis=0, dtype=jnp.float32),
                    jnp.sum(d_kv_low[:, 1], axis=0, dtype=jnp.float32),
                ]
            ),
            jnp.sum(d_middle, axis=0),
            jnp.sum(d_normed_two * unit_two, axis=0),
            jnp.sum(d_normed_two, axis=0),
            jnp.sum(d_before_low, axis=0, dtype=jnp.float32),
            jnp.sum(grad_rows, axis=0),
        )
        big_step = (qkv_step, score_step, out_step, fc1_step, fc2_step)
        big_sums = jax.tree.map(jnp.add, big_sums, big_step)
        small_sums = jax.tree.map(jnp.add, small_sums, small_step)
        return (big_sums, small_sums, out_buffer, grad_buffer)

    big_init = (
        jnp.zeros((width_full, 3, hidden_local), jnp.float32),
        jnp.zeros((width_full, heads_local), jnp.float32),
        jnp.zeros((width_full, hidden_local), jnp.float32),
        jnp.zeros((width_full, units_local), jnp.float32),
        jnp.zeros((width_full, units_local), jnp.float32),
    )
    small_init = (
        jnp.zeros((width_full,), jnp.float32),
        jnp.zeros((width_full,), jnp.float32),
        jnp.zeros((2, hidden_local), jnp.float32),
        jnp.zeros((width_full,), jnp.float32),
        jnp.zeros((width_full,), jnp.float32),
        jnp.zeros((width_full,), jnp.float32),
        jnp.zeros((units_local,), jnp.float32),
        jnp.zeros((width_full,), jnp.float32),
    )
    buffer_init = jnp.zeros(inputs.shape, jnp.bfloat16)
    big_sums, small_sums, out_buffer, grad_buffer = lax.fori_loop(
        0, MICRO, micro_step, (big_init, small_init, buffer_init, buffer_init)
    )
    big_grads = (
        lax.psum_scatter(big_sums[0], ("fsdp", "ctx"), scatter_dimension=0, tiled=True),
        lax.psum_scatter(big_sums[1], ("fsdp", "ctx"), scatter_dimension=0, tiled=True),
        lax.psum_scatter(big_sums[2], ("fsdp", "ctx"), scatter_dimension=0, tiled=True),
        lax.psum_scatter(big_sums[3], ("fsdp", "ctx"), scatter_dimension=0, tiled=True),
        lax.psum_scatter(big_sums[4], ("fsdp", "ctx"), scatter_dimension=0, tiled=True),
    )
    small_grads = lax.psum(
        (
            small_sums[0],
            small_sums[1],
            small_sums[2],
            small_sums[3],
            small_sums[4],
            small_sums[5],
            small_sums[6],
            small_sums[7],
        ),
        ("fsdp", "ctx"),
    )
    return (
        out_buffer,
        grad_buffer,
        small_grads[0],
        small_grads[1],
        big_grads[0],
        small_grads[2],
        big_grads[1],
        big_grads[2],
        small_grads[3],
        small_grads[4],
        small_grads[5],
        big_grads[3],
        small_grads[6],
        big_grads[4],
        small_grads[7],
    )


EPS = 1e-05
MASKED = -1e30
MESH_ID = pl.DeviceIdType.MESH
CH_A, CH_B, CH_1, CH_2 = 0, 1, 2, 3
f32 = jnp.float32
bf16 = jnp.bfloat16


def dot(left, right, left_dim, right_dim):
    return lax.dot_general(
        left, right, (((left_dim,), (right_dim,)), ((), ())), preferred_element_type=f32
    )


def ln_parts(rows):
    centred = rows - jnp.mean(rows, axis=-1, keepdims=True)
    inverse = lax.rsqrt(jnp.mean(centred * centred, axis=-1, keepdims=True) + EPS)
    return centred * inverse, inverse


def ln_back(upstream, unit, inverse, gain):
    scaled = upstream * gain
    return inverse * (
        scaled
        - jnp.mean(scaled, axis=-1, keepdims=True)
        - unit * jnp.mean(scaled * unit, axis=-1, keepdims=True)
    )


PLAN = {
    "front": (("p0w", 0), ("p0w", 1), ("za", 0, 0), ("za", 0, 1), ("p0w", 2), ("a2a", "x"), ("za", 2, 0), ("s1", 0, 1), ("p0w", 3), ("za", 1, 1),),
    "x_wait": (("s1", 0, 0), ("s2", 0, 1),),
    "ln1": (("za", 1, 0),),
    "nrm_wait": (("s2", 0, 0), ("za", 3, 1), ("s1", 1, 1),),
    "qkv2": (("s1", 1, 0),),
    "qkv3": (("s1", 2, 0),),
    "gat2": (("za", 3, 0),),
    "fwd0": (("a2a", "cot"), ("s2", 1, 0),),
    "fwd5": (("s2", 2, 0), ("s1", 3, 0),),
    "fwd9": (("s2", 1, 1),),
    "fwd11": (("za", 2, 1),),
    "fwd13": (("s2", 3, 0), ("s1", 3, 1),),
    "fwd14": (("cotw",),),
    "br0": (("s1", 2, 1),),
    "mlpa1": (("s2", 3, 1), ("s2", 2, 1),),
    "g21": (("r2", 2, 0), ("r2", 3, 0),),
    "bwd2": (("a2a", "res"),),
    "bwd4": (("r2", 1, 1),),
    "bwd5": (("r3", 2, 0),),
    "bwd6": (("r2", 3, 1),),
    "bwd11": (("r3", 3, 0),),
    "mix": (("r2", 2, 1),),
    "dn0": (("r3", 3, 1),),
    "od0": (("r3b", 3, 0),),
    "od1": (("r3", 2, 1), ("r3b", 2, 0),),
    "e0": (("hs", 0),),
    "e1": (("hw", 0), ("r3", 1, 1),),
    "e2": (("r3b", 3, 1), ("r2", 1, 0),),
    "e3": (("hs", 1), ("r3", 1, 0),),
    "e4": (("r2", 0, 0),),
    "e5": (("hw", 1), ("r3b", 2, 1),),
    "e6": (("r3", 0, 0), ("r2", 0, 1),),
    "e7": (("r3b", 1, 1), ("hs", 2),),
    "e8": (("r3", 0, 1), ("hw", 2),),
    "e9": (("r3b", 1, 0),),
    "e10": (("r4", 2), ("r4", 3),),
    "e12": (("r3b", 0, 0),),
    "e13": (("r3b", 0, 1), ("hs", 3),),
    "e14": (("hw", 3),),
    "e16": (("hs", 4),),
    "e19": (("r4", 1),),
    "e20": (("r4", 0),),
    "e22": (("hw", 4),),
}
PEER_FIRST, FF_GRADS_LATER, QKV_GRADS_LAST = False, False, True
AG_DIRECT, RS_DIRECT = (), ()
AG_XLIGHT = {(2, 0), (2, 1), (3, 0), (0, 0), (1, 0)}
RS_XLIGHT = {(2, 0), (2, 1), (3, 1), (0, 0), (0, 1), (1, 0)}


def layer_kernel(
    x_hbm, cot_hbm, wq_hbm, ws_hbm, wo_hbm, f1_hbm, f2_hbm, sel_hbm, n1g, n1b, ob, n2g, n2b, f2b, f1b, qvb, pref,
    res_o, ing_o, ga_o, gb_o, g1_o, g2_o, sm_o,
    wa, wb, w1, w2, ga,
    rba, rbb, rb1, rb2, rza, rzb, rz1, rz2, rpa, rpb, rp1, rp2,
    xin, cot, nrm, qb, kb, vb, ksel, vsel, pr, att, mid, n2, act, dbf,
    st, rv, dnr, dml, datt, acc, scr, stage, selraw, selb, wq, ws, wo, pa, pb, v0, v1, v2, v3, v4, v5, fb0, fb1, qvbb, smb, smr,
    ain_s, ain_r, aout_s, aout_r, ag_s, ag_r, rs_s, rs_r, tm_s, tm_r,
    sel_s, sel_r, bias_s, bias_r, sm_s, sm_r, loc, gout,
):
    y = lax.axis_index("fsdp")
    x = lax.axis_index("xo")
    c = lax.axis_index("team")
    z = lax.axis_index("tp")
    zz = z + c * (3 - 2 * z)
    source = zz < 2
    own_tok = x_hbm.shape[1]
    width = x_hbm.shape[2]
    tile = 4 * own_tok
    half = 2 * tile
    seq = 2 * half
    my_seq = x * 4 + z
    hbms = (pa, pb, f1_hbm, f2_hbm)
    weights = (wa, wb, w1, w2)
    grads = (ga, wb, w1, w2)
    rbs = (rba, rbb, rb1, rb2)
    rzs = (rza, rzb, rz1, rz2)
    rps = (rpa, rpb, rp1, rp2)
    g_outs = (ga_o, gb_o, g1_o, g2_o)
    shard = f1_hbm.shape[0]
    pair = 2 * shard
    over_x, over_y, other = {"xo": 1 - x}, {"fsdp": 1 - y}, {"team": 1 - c}

    def block(yy, xx):
        return pl.ds(pl.multiple_of((yy * 4 + xx * 2) * shard, pair), pair)

    mine = block(y, x)
    vecs, fbs = (v0, v1, v2, v3, v4, v5), (fb0, fb1)

    def vec(i):
        return vecs[i][...].reshape(1, width)

    far_x, far_y = block(y, 1 - x), block(1 - y, x)
    far_xy = block(1 - y, 1 - x)

    def at_zz(q):
        return {"tp": q + c * (3 - 2 * q)}

    def own_shard(cc):
        return pl.ds(pl.multiple_of((y * 4 + x * 2 + cc) * shard, shard), shard)

    def rcopy(src, dst, ss, rs, dev):
        return pltpu.make_async_remote_copy(
            src_ref=src, dst_ref=dst, send_sem=ss, recv_sem=rs, device_id=dev, device_id_type=MESH_ID
        )

    bar = pltpu.get_barrier_semaphore()
    peers = []
    for dx in range(2):
        for dz in range(4):
            if dx or dz:
                peers.append({"xo": lax.rem(x + dx, 2), "tp": lax.rem(z + dz, 4)})
    peers += [other, over_y, {"xo": 1 - x, "team": 1 - c}]
    for peer in peers:
        pl.semaphore_signal(bar, 1, device_id=peer, device_id_type=MESH_ID)
    pl.semaphore_wait(bar, len(peers))

    def a2a_in(which, hbm):
        out = []
        for dx in range(2):
            for dz in range(4):
                xx, z2 = lax.rem(x + dx, 2), lax.rem(z + dz, 4)
                if which == 0:
                    at = pl.ds(pl.multiple_of(x * tile + z * own_tok, own_tok), own_tok)
                    dst = xin.at[at]
                else:
                    at = pl.ds(pl.multiple_of(x * half + c * tile + z * own_tok, own_tok), own_tok)
                    dst = cot.at[at]
                idx = dx * 4 + dz
                src = hbm.at[xx * 4 + z2]
                if idx == 0:
                    out.append(pltpu.make_async_copy(src, dst, ain_r.at[which, 0]))
                else:
                    out.append(
                        rcopy(src, dst, ain_s.at[which, idx], ain_r.at[which, idx], {"xo": xx, "tp": z2})
                    )
        return out

    def a2a_in_wait(copies):
        copies[0].wait()
        for cp in copies[1:]:
            cp.wait()

    def p0_local(k):
        return pltpu.make_async_copy(hbms[k], weights[k].at[zz, own_shard(c)], loc.at[k])

    def p0_away(k):
        return rcopy(
            hbms[k], weights[k].at[3 - zz, own_shard(c)], ag_s.at[k, 5], ag_r.at[k, 2], other
        )

    def p0_back(k):
        return rcopy(
            hbms[k], weights[k].at[zz, own_shard(1 - c)], ag_s.at[k, 5], ag_r.at[k, 2], other
        )

    def p0_start(k):
        @pl.when(source)
        def _():
            p0_local(k).start()

        @pl.when(jnp.logical_not(source))
        def _():
            p0_away(k).start()

    def p0_wait(k):
        @pl.when(source)
        def _():
            p0_local(k).wait()
            p0_back(k).wait_recv()

        @pl.when(jnp.logical_not(source))
        def _():
            p0_away(k).wait_send()

    def z_copy(k, s, q, idx):
        ref = weights[k].at[s, mine]
        return rcopy(ref, ref, ag_s.at[k, idx], ag_r.at[k, s], at_zz(q))

    def z_sends(k, s):
        out = [z_copy(k, s, 2, 0), z_copy(k, s, 1 - s, 1)]
        if k in AG_DIRECT:
            out.append(z_copy(k, s, 3, 2))
        return out

    def z_start(k, s):
        @pl.when(zz == s)
        def _():
            for cp in z_sends(k, s):
                cp.start()

    def xy(k, s, which):
        light = (k, s) in AG_XLIGHT
        rows, dev = (
            (mine, over_x),
            (mine, over_y),
            (far_x, over_y) if light else (far_y, over_x),
        )[which]
        ref = weights[k].at[s, rows]
        return rcopy(ref, ref, ag_s.at[k, 6 + 3 * s + which], ag_r.at[k, 3 + 3 * s + which], dev)

    def s1(k, s):
        @pl.when(zz != s)
        def _():
            z_copy(k, s, 2, 0).wait_recv()

        if k not in AG_DIRECT:
            @pl.when(zz == 2)
            def _():
                z_copy(k, s, 3, 3 + s).start()

        for which in (0, 1) if (k, s) in AG_XLIGHT else (1, 0):
            xy(k, s, which).start()

    def s2(k, s):
        xy(k, s, 0 if (k, s) in AG_XLIGHT else 1).wait_recv()
        xy(k, s, 2).start()

    def s3(k, s):
        for which in (1 if (k, s) in AG_XLIGHT else 0, 2):
            xy(k, s, which).wait_recv()

    def ag_drain(k, s):
        @pl.when(zz == s)
        def _():
            for cp in z_sends(k, s):
                cp.wait_send()

        if k not in AG_DIRECT:
            @pl.when(zz == 2)
            def _():
                z_copy(k, s, 3, 3 + s).wait_send()

        for which in range(3):
            xy(k, s, which).wait_send()

    def rs_copy(k, s, which):
        light = (k, s) in RS_XLIGHT
        rows, dev = (
            (far_xy, over_y if light else over_x),
            (far_y, over_y) if light else (far_x, over_x),
            (far_x, over_x) if light else (far_y, over_y),
        )[which]
        i = 3 * s + which
        return rcopy(grads[k].at[s, rows], rbs[k].at[i], rs_s.at[k, i], rs_r.at[k, i], dev)

    def add_rows(k, slot, rows, bufs):
        g = grads[k]
        total = g[slot, rows, :].astype(f32)
        for buf in bufs:
            total = total + buf[...].astype(f32)
        g[slot, rows, :] = total.astype(bf16)

    def r1(k, s):
        for which in range(2):
            rs_copy(k, s, which).start()

    def r2(k, s):
        rs_copy(k, s, 0).wait_recv()
        add_rows(k, s, far_x if (k, s) in RS_XLIGHT else far_y, [rbs[k].at[3 * s]])
        rs_copy(k, s, 2).start()

    def rz_copy(k, s, q, idx):
        return rcopy(
            grads[k].at[s, mine], rzs[k].at[idx], rs_s.at[k, 6 + s], rs_r.at[k, 6 + idx], at_zz(q)
        )

    def rz_last(k, s):
        return rz_copy(k, s, s, 2) if k in RS_DIRECT else rz_copy(k, s, 2, s)

    def r3(k, s):
        for which in range(1, 3):
            rs_copy(k, s, which).wait_recv()
        add_rows(k, s, mine, [rbs[k].at[3 * s + 1], rbs[k].at[3 * s + 2]])

        @pl.when(zz == 3)
        def _():
            rz_last(k, s).start()

        @pl.when(zz == 1 - s)
        def _():
            rz_copy(k, s, s, 0).start()

    def r3b(k, s):
        @pl.when(zz == 2)
        def _():
            if k not in RS_DIRECT:
                rz_copy(k, s, 2, s).wait_recv()
                add_rows(k, s, mine, [rzs[k].at[s]])
            rz_copy(k, s, s, 1).start()

    def rp_copy(k):
        return rcopy(
            grads[k].at[zz, own_shard(1 - c)], rps[k], rs_s.at[k, 8], rs_r.at[k, 9], other
        )

    def keep_own(k):
        return pltpu.make_async_copy(grads[k].at[zz, own_shard(c)], g_outs[k], gout.at[k])

    def keep_got(k):
        return pltpu.make_async_copy(rps[k], g_outs[k], gout.at[k])

    def r4(k):
        came = range(3) if k in RS_DIRECT else range(2)
        for s in range(2):
            @pl.when(zz == s)
            def _(s=s):
                for idx in came:
                    rz_copy(k, s, s, idx).wait_recv()
                add_rows(k, s, mine, [rzs[k].at[idx] for idx in came])

        @pl.when(source)
        def _():
            rp_copy(k).start()
            keep_own(k).start()

    def rp_wait(k):
        @pl.when(jnp.logical_not(source))
        def _():
            rcopy(rps[k], rps[k], rs_s.at[k, 8], rs_r.at[k, 9], other).wait_recv()
            keep_got(k).start()

        @pl.when(source)
        def _():
            rp_copy(k).wait_send()

    def rs_drain(k):
        keep_got(k).wait()
        for s in range(2):
            for which in range(3):
                rs_copy(k, s, which).wait_send()

            @pl.when((zz >= 2) | (zz == 1 - s))
            def _(s=s):
                rz_copy(k, s, s, 0).wait_send()

    def chunk(j, cc):
        return pl.ds(pl.multiple_of(j * half + cc * tile, tile), tile)

    def swap(buf, j, idx):
        return rcopy(buf.at[chunk(j, c)], buf.at[chunk(j, c)], tm_s.at[idx + j], tm_r.at[idx + j], other)

    def swap_wait(buf, j, idx):
        rcopy(buf.at[chunk(j, 1 - c)], buf.at[chunk(j, 1 - c)], tm_s.at[idx + j], tm_r.at[idx + j], other).wait_recv()

    def part(which, j, idx):
        return rcopy(st.at[which, j], rv.at[which, j], tm_s.at[idx + j], tm_r.at[idx + j], other)

    T_NRM, T_COT, T_BR, T_N2, T_MLP, T_DN2, T_DML, T_DNR = range(0, 16, 2)

    lane256 = lax.broadcasted_iota(jnp.int32, (1, 256), 1)
    head_rows = [jnp.where(lane256 // 64 == h, 1.0, 0.0).astype(f32) for h in range(3)]
    q_rows = [
        jnp.where((lane256 // 64 == h) | (lane256 == 192 + h), 1.0, 0.0).astype(f32) for h in range(3)
    ]

    def stack3(rows, masks):
        wide = rows.astype(f32)
        return jnp.concatenate([(wide * m).astype(bf16) for m in masks], axis=0)

    def fold3(stacked):
        n = stacked.shape[0] // 3
        return (
            stacked[:n] * head_rows[0] + stacked[n : 2 * n] * head_rows[1] + stacked[2 * n :] * head_rows[2]
        )

    sends = {"x": lambda: a2a_in(0, x_hbm), "cot": lambda: a2a_in(1, cot_hbm), "res": lambda: a2a_out(0, stage)}
    hops = [other, over_x, over_y, {"tp": z + 1 - 2 * lax.rem(z, 2)}, {"tp": lax.rem(z + 2, 4)}]

    def hop(i):
        return rcopy(smb, smr.at[i], sm_s.at[i], sm_r.at[i], hops[i])

    def hop_wait(i):
        hop(i).wait()
        smb[...] += smr[i]

    def a2a_start(name):
        for cp in sends[name]():
            cp.start()

    def cot_here():
        a2a_in_wait(a2a_in(1, cot_hbm))
        for j in range(2):
            swap(cot, j, T_COT).start()

    steps = {
        "p0w": p0_wait, "za": z_start, "s1": s1, "s2": s2, "r2": r2, "r3": r3, "r3b": r3b, "r4": r4,
        "a2a": a2a_start, "cotw": cot_here, "hs": lambda i: hop(i).start(), "hw": hop_wait,
    }

    def point(name):
        for step in PLAN.get(name, ()):
            steps[step[0]](*step[1:])

    def points(name, i, count):
        for n in range(count):
            if name + str(n) in PLAN:
                @pl.when(i == n)
                def _(n=n):
                    point(name + str(n))

    def a2a_out(which, stage):
        out = []
        for dx in range(2):
            for dz in range(4):
                xx, z2_ = lax.rem(x + dx, 2), lax.rem(z + dz, 4)
                src = stage.at[pl.ds(pl.multiple_of(xx * tile + z2_ * own_tok, own_tok), own_tok)]
                dst = (res_o, ing_o)[which].at[my_seq]
                idx = dx * 4 + dz
                if idx == 0:
                    out.append(pltpu.make_async_copy(src, dst, aout_r.at[which, 0]))
                else:
                    out.append(
                        rcopy(src, dst, aout_s.at[which, idx], aout_r.at[which, idx], {"xo": xx, "tp": z2_})
                    )
        return out

    def weights_in():
        return [
            pltpu.make_async_copy(src, dst, loc.at[4 + i])
            for i, (src, dst) in enumerate(((wq_hbm, wq), (ws_hbm, ws), (wo_hbm, wo)))
        ]

    def vectors_in():
        return [
            pltpu.make_async_copy(src, dst, loc.at[7 + i])
            for i, (src, dst) in enumerate(zip((n1g, n1b, ob, n2g, n2b, f2b), vecs))
        ]

    def bias_copies(s, dz):
        dev = {"tp": lax.rem(z + dz, 4)}
        return [
            rcopy(src, buf, bias_s.at[i, dz], bias_r.at[i, s], dev)
            for i, (src, buf) in enumerate(((f1b, fbs[s]), (qvb, qvbb.at[s])))
        ]

    def bias_own(s):
        return [
            pltpu.make_async_copy(src, buf, bias_s.at[i, 0])
            for i, (src, buf) in enumerate(((f1b, fbs[s]), (qvb, qvbb.at[s])))
        ]

    for cp in weights_in():
        cp.start()
    for cp in vectors_in():
        cp.start()
    for k in (CH_1, CH_2):
        p0_start(k)

    def place(rows, cols, first):
        i = lax.broadcasted_iota(jnp.int32, (rows, cols), 0)
        j = lax.broadcasted_iota(jnp.int32, (rows, cols), 1)
        return jnp.where(j == i + first, 1.0, 0.0).astype(bf16)

    for cp in weights_in():
        cp.wait()
    head_cols = wq.shape[2]
    packed = dot(ws[...], place(ws.shape[0], 640, 3 * head_cols), 0, 0)
    for i in range(3):
        packed = packed + dot(wq[i], place(head_cols, 640, i * head_cols), 1, 0)
    pa[...] = packed.astype(bf16)
    pb[...] = dot(wo[...], place(head_cols, 256, 0), 1, 0).astype(bf16)
    for k in (CH_A, CH_B):
        p0_start(k)
    point("front")
    sel_copies = []
    for dx in range(2):
        for dc in range(2):
            idx = dx * 2 + dc
            xx, cc = lax.rem(x + dx, 2), lax.rem(c + dc, 2)
            src, dst = sel_hbm, selraw.at[x * 2 + c]
            if idx == 0:
                sel_copies.append(pltpu.make_async_copy(src, dst, sel_r.at[0]))
            else:
                sel_copies.append(
                    rcopy(src, dst, sel_s.at[idx], sel_r.at[idx], {"xo": xx, "team": cc})
                )
    for cp in sel_copies:
        cp.start()

    for s in range(2):
        @pl.when(zz == s)
        def _(s=s):
            for dz in range(1, 4):
                for cp in bias_copies(s, dz):
                    cp.start()
            for cp in bias_own(s):
                cp.start()

    zero_k = jnp.zeros((own_tok, 256), bf16)
    for ref in (kb, vb):
        for slot in range(2):
            ref[slot, 0:own_tok, :] = zero_k
            ref[slot, seq + own_tok : seq + 2 * own_tok, :] = zero_k
    smb[...] = jnp.zeros_like(smb)
    for cp in vectors_in():
        cp.wait()
    point("x_wait")
    a2a_in_wait(a2a_in(0, x_hbm))

    def natural(i):
        return pl.multiple_of((i // 4) * half + c * tile + (i % 4) * own_tok, own_tok)

    def ln1_body(i, carry):
        rows = xin[pl.ds(pl.multiple_of(i * own_tok, own_tok), own_tok), :].astype(f32)
        unit, _ = ln_parts(rows)
        nrm[pl.ds(natural(i), own_tok), :] = (unit * vec(0) + vec(1)).astype(bf16)
        return carry

    point("ln1")
    lax.fori_loop(0, 8, ln1_body, 0)
    for j in range(2):
        swap(nrm, j, T_NRM).start()

    for cp in sel_copies:
        cp.wait()
    lane_seq = lax.broadcasted_iota(jnp.int32, selraw.shape[1:], 2)
    sub = lax.broadcasted_iota(jnp.int32, (SEL, 256), 0)
    lane = lax.broadcasted_iota(jnp.int32, (SEL, 256), 1)
    inner = (lane % KB).astype(f32)
    for g in range(4):
        chosen = jnp.sum(jnp.where(lane_seq == my_seq, selraw[g].astype(f32), 0.0), axis=2, keepdims=True)
        every = jnp.zeros((1, 256), f32)
        for b in range(4):
            keys = jnp.broadcast_to(chosen[b], (SEL, 256)) * KB + inner
            here = jnp.sum(jnp.where(lane // KB == sub + 192 // KB, keys, 0.0), axis=0, keepdims=True)
            selb[g, b : b + 1, :] = here.astype(jnp.int32)
            every = every + jnp.sum(
                jnp.where(lane // KB == sub + b * SEL, keys, 0.0), axis=0, keepdims=True
            )
        selb[g, 4:5, :] = every.astype(jnp.int32)

    for s in range(2):
        @pl.when(zz != s)
        def _(s=s):
            for cp in bias_copies(s, 1):
                cp.wait_recv()

        @pl.when(zz == s)
        def _(s=s):
            for cp in bias_own(s):
                cp.wait()

    point("nrm_wait")
    for j in range(2):
        swap_wait(nrm, j, T_NRM)
    for s in range(2):
        s3(CH_A, s)

    gate_lane = (lane256 >= 192) & (lane256 < 195)

    gap = jnp.zeros((1, 640 - 3 * head_cols), f32)
    none = jnp.zeros((1, head_cols), f32)
    mix_bias = [
        jnp.concatenate([qvbb[slot, 0:1, :], none, qvbb[slot, 1:2, :], gap], axis=1) for slot in range(2)
    ]

    def qkv_body(i, carry):
        points("qkv", i, 4)
        at = pl.ds(pl.multiple_of(i * tile, tile), tile)
        padded = pl.ds(pl.multiple_of(i * tile + own_tok, own_tok), tile)
        rows = nrm[at, :]
        for slot in range(2):
            mixed = dot(rows, wa[slot], 1, 0)
            scr[slot, at, :] = mixed[:, 512:640]
            mixed = mixed + mix_bias[slot]
            q = mixed[:, 0:256].astype(bf16).astype(f32) * 0.125
            q = jnp.where(lane256 < 192, q, jnp.where(gate_lane, 1.0, 0.0))
            qb[slot, at, :] = q.astype(bf16)
            keys = pltpu.roll(mixed[:, 128:384], 192, 1)
            score = mixed[:, 512:640]
            gate = -(jnp.maximum(-score, 0.0) + jnp.log(1.0 + jnp.exp(-jnp.abs(score))))
            gate = jnp.concatenate([gate, gate], axis=1)
            keys = jnp.where(lane256 < 192, keys, jnp.where(gate_lane, gate, 0.0))
            kb[slot, padded, :] = keys.astype(bf16)
            vb[slot, padded, :] = jnp.where(lane256 < 192, mixed[:, 384:640], 0.0).astype(bf16)
        return carry

    lax.fori_loop(0, 4, qkv_body, 0)

    key_iota = lax.broadcasted_iota(jnp.int32, (seq, 256), 0)

    def one_hot(g):
        return jnp.where(key_iota == selb[g, 4:5, :], 1.0, 0.0).astype(bf16)

    def gather_body(g, carry):
        points("gat", g, 4)
        hot = one_hot(g)
        at = pl.ds(pl.multiple_of(g * 256, 256), 256)
        for slot in range(2):
            ksel[slot, at, :] = dot(hot, kb[slot, own_tok : own_tok + seq, :], 0, 0).astype(bf16)
            vsel[slot, at, :] = dot(hot, vb[slot, own_tok : own_tok + seq, :], 0, 0).astype(bf16)
        return carry

    lax.fori_loop(0, 4, gather_body, 0)

    prefix_end = pref[my_seq]

    def windows(b, slot):
        near = pl.ds(pl.multiple_of(b * 64, 64), 192)
        at = pl.ds(pl.multiple_of(b * 64, 64), 64)
        keys = jnp.concatenate([kb[slot, near, :], ksel[slot, at, :]], axis=0)
        vals = jnp.concatenate([vb[slot, near, :], vsel[slot, at, :]], axis=0)
        return at, near, keys, vals

    def fwd_body(b, carry):
        points("fwd", b, 16)
        picks = selb[b // 4, pl.ds(b % 4, 1), :]
        key_pos = jnp.where(lane256 < 192, (b - 1) * 64 + lane256, picks)
        query_pos = b * 64 + lax.broadcasted_iota(jnp.int32, (64, 256), 0)
        key_pos = jnp.broadcast_to(key_pos, (64, 256))
        inside = (key_pos >= 0) & (key_pos < seq)
        permitted = (key_pos <= query_pos) | ((query_pos < prefix_end) & (key_pos < prefix_end))
        near_by = jnp.abs(query_pos - key_pos) < 64
        is_near = jnp.broadcast_to(lane256 < 192, (64, 256))
        allowed = inside & permitted & (near_by == is_near)
        fill = jnp.where(allowed, 0.0, MASKED)
        for slot in range(2):
            at, near, keys, vals = windows(b, slot)
            stacked = stack3(qb[slot, at, :], q_rows)
            logits = dot(stacked, keys, 1, 1).reshape(3, 64, 256) + fill[None]
            top = jnp.max(logits, axis=-1, keepdims=True)
            p = jnp.exp(logits - top)
            p = p * (1.0 / jnp.sum(p, axis=-1, keepdims=True))
            p = p.reshape(192, 256).astype(bf16)
            pr[b * 2 + slot] = p
            att[slot, at, :] = fold3(dot(p, vals, 1, 0)).astype(bf16)
        return carry

    lax.fori_loop(0, 16, fwd_body, 0)

    point("brs")
    for s in range(2):
        s3(CH_B, s)

    def branch_tile(rows):
        return dot(att[0, rows, :], wb[0], 1, 1) + dot(att[1, rows, :], wb[1], 1, 1)

    for j in range(2):
        st[0, j] = branch_tile(chunk(j, 1 - c)).astype(bf16)
        part(0, j, T_BR).start()
    for j in range(2):
        point("br" + str(j))
        own = branch_tile(chunk(j, c))
        at = slice(j * tile, (j + 1) * tile)
        part(0, j, T_BR).wait_recv()
        mid[at, :] = (
            xin[at, :].astype(f32) + own + rv[0, j].astype(f32) + vec(2)
        )

        def ln2_body(i, carry, j=j):
            rows = mid[pl.ds(pl.multiple_of(j * tile + i * own_tok, own_tok), own_tok), :]
            unit, _ = ln_parts(rows)
            n2[pl.ds(natural(j * 4 + i), own_tok), :] = (unit * vec(3) + vec(4)).astype(bf16)
            return carry

        lax.fori_loop(0, 4, ln2_body, 0)
        swap(n2, j, T_N2).start()

    point("mlpa0")
    for k in (CH_1, CH_2):
        s3(k, 0)
    for j in range(2):
        swap_wait(cot, j, T_COT)
        part(0, j, T_BR).wait_send()
        swap_wait(n2, j, T_N2)

    def mlp_tile(rows, slot):
        before = dot(n2[rows, :], w1[slot], 1, 0) + fbs[slot][...].reshape(1, width)
        d_act = dot(cot[rows, :], w2[slot], 1, 0)
        square = before * before
        t = jnp.tanh(0.7978845608028654 * before * (1.0 + 0.044715 * square))
        gate = 0.5 * (1.0 + t)
        slope = gate + 0.5 * before * (1.0 - t * t) * (
            0.7978845608028654 * (1.0 + 0.134145 * square)
        )
        low = (before * gate).astype(bf16)
        low_back = (d_act * slope).astype(bf16)
        act[slot, rows, :] = low
        dbf[slot, rows, :] = low_back
        smb[pl.ds(8 + slot + c * (3 - 2 * slot), 1), :] += jnp.sum(
            low_back.astype(f32), axis=0, keepdims=True
        )
        return dot(low, w2[slot], 1, 1), dot(low_back, w1[slot], 1, 1)

    def first_mlp(i, carry):
        @pl.when(i > 0)
        def _():
            points("mlpa", i, 4)

        at = pl.ds(pl.multiple_of(i * tile, tile), tile)
        out, back = mlp_tile(at, 0)
        acc[0, at, :] = out
        acc[1, at, :] = back
        return carry

    lax.fori_loop(0, 4, first_mlp, 0)

    def weight_grad(g, slot, left, right):
        def body(m, carry):
            at = pl.ds(pl.multiple_of(m * 256, 256), 256)
            g[slot, at, :] = dot(left[:, at], right, 0, 0).astype(bf16)
            return carry

        lax.fori_loop(0, 3, body, 0)

    def ff_grads(slot):
        for k, name, left, right in ((CH_2, "g2", cot, act), (CH_1, "g1", n2, dbf)):
            point(name + str(slot))
            ag_drain(k, slot)
            weight_grad(grads[k], slot, left, right[slot])
            r1(k, slot)

    def peer_mlp(j, carry):
        @pl.when(j == 1)
        def _():
            point("pm1")

        rows = chunk(j, 1 - c)
        out, back = mlp_tile(rows, 1)
        st[0, j] = (acc[0, rows, :] + out).astype(bf16)
        st[1, j] = (acc[1, rows, :] + back).astype(bf16)
        part(0, j, T_MLP).start()
        part(1, j, T_DN2).start()
        return carry

    if not PEER_FIRST:
        ff_grads(0)
    point("pm0")
    for k in (CH_1, CH_2):
        s3(k, 1)
    lax.fori_loop(0, 2, peer_mlp, 0)
    if PEER_FIRST:
        ff_grads(0)

    def own_mlp(j, carry):
        points("om", j, 2)
        rows = chunk(j, c)
        out, back = mlp_tile(rows, 1)
        out = acc[0, rows, :] + out
        back = acc[1, rows, :] + back
        at = pl.ds(pl.multiple_of(j * tile, tile), tile)
        part(0, j, T_MLP).wait_recv()
        part(1, j, T_DN2).wait_recv()
        stage[at, :] = (mid[at, :] + out + rv[0, j].astype(f32) + vec(5)).astype(bf16)
        dnr[...] = back + rv[1, j].astype(f32)

        def ln2_back(i, carry):
            here = pl.ds(pl.multiple_of(j * tile + i * own_tok, own_tok), own_tok)
            nat = pl.ds(natural(j * 4 + i), own_tok)
            unit, inverse = ln_parts(mid[here, :])
            up_grad = dnr[pl.ds(pl.multiple_of(i * own_tok, own_tok), own_tok), :]
            grad_rows = cot[nat, :].astype(f32)
            d_mid = grad_rows + ln_back(up_grad, unit, inverse, vec(3))
            mid[here, :] = d_mid
            dml[nat, :] = d_mid.astype(bf16)
            smb[2:3, :] += jnp.sum(d_mid, axis=0, keepdims=True)
            smb[3:4, :] += jnp.sum(up_grad * unit, axis=0, keepdims=True)
            smb[4:5, :] += jnp.sum(up_grad, axis=0, keepdims=True)
            smb[5:6, :] += jnp.sum(grad_rows, axis=0, keepdims=True)
            return carry

        lax.fori_loop(0, 4, ln2_back, 0)
        swap(dml, j, T_DML).start()
        return carry

    lax.fori_loop(0, 2, own_mlp, 0)

    if not FF_GRADS_LATER:
        ff_grads(1)
    point("datt")
    for j in range(2):
        swap_wait(dml, j, T_DML)

    def datt_body(i, carry):
        at = pl.ds(pl.multiple_of(i * tile, tile), tile)
        for slot in range(2):
            datt[slot, at, :] = dot(dml[at, :], wb[slot], 1, 0).astype(bf16)
        return carry

    lax.fori_loop(0, 4, datt_body, 0)
    for slot in range(2):
        point("gb" + str(slot))
        ag_drain(CH_B, slot)
        weight_grad(wb, slot, dml, att[slot])
        r1(CH_B, slot)
    if FF_GRADS_LATER:
        ff_grads(1)
    acc[:, :, 0:512] = jnp.zeros((2, seq + 2 * own_tok, 512), f32)

    def bwd_body(b, carry):
        points("bwd", b, 16)
        for slot in range(2):
            at, near, keys, vals = windows(b, slot)
            q_stack = stack3(qb[slot, at, :], q_rows)
            d_stack = stack3(datt[slot, at, :], head_rows)
            p_low = pr[b * 2 + slot]
            p = p_low.astype(f32)
            pdp = p * dot(d_stack, vals, 1, 1)
            dl = (pdp - p * jnp.sum(pdp, axis=-1, keepdims=True)).astype(bf16)
            dbf[slot, at, 512:768] = (fold3(dot(dl, keys, 1, 0)) * 0.125).astype(bf16)
            dk = dot(dl, q_stack, 0, 0)
            dv = dot(p_low, d_stack, 0, 0)
            side = slice(slot * 256, slot * 256 + 256)
            acc[0, near, side] += dk[0:192]
            acc[1, near, side] += dv[0:192]
            dbf[slot, at, 0:256] = dk[192:256].astype(bf16)
            dbf[slot, at, 256:512] = dv[192:256].astype(bf16)
        return carry

    lax.fori_loop(0, 16, bwd_body, 0)
    point("mix")

    sel_pos = jnp.concatenate([selb[g, 4:5, :] for g in range(4)], axis=1)

    def mix_body(i, carry):
        at = pl.ds(pl.multiple_of(i * tile, tile), tile)
        padded = pl.ds(pl.multiple_of(i * tile + own_tok, own_tok), tile)
        key_at = i * tile + lax.broadcasted_iota(jnp.int32, (tile, seq), 0)
        hot = jnp.where(key_at == sel_pos, 1.0, 0.0).astype(bf16)
        for slot in range(2):
            far = dot(hot, dbf[slot, :, 0:512], 1, 0)
            dk = (acc[0, padded, slot * 256 : slot * 256 + 256] + far[:, 0:256]).astype(bf16).astype(f32)
            dv = (acc[1, padded, slot * 256 : slot * 256 + 256] + far[:, 256:512]).astype(bf16).astype(f32)
            dq = dbf[slot, at, 512:768].astype(f32)
            turned = pltpu.roll(dk, 64, 1)
            d_score = dk[:, 128:256] / (1.0 + jnp.exp(scr[slot, at, :]))
            lane128 = lane256[:, 0:128]
            v1 = jnp.where(lane128 < 64, dq[:, 128:256], turned[:, 0:128])
            v4 = jnp.where(lane128 < 64, dv[:, 128:256], jnp.where(lane128 < 67, d_score, 0.0))
            mix = jnp.concatenate([dq[:, 0:128], v1, turned[:, 128:256], dv[:, 0:128], v4], axis=1)
            mix = mix.astype(bf16)
            act[slot, at, 0:640] = mix
            smb[pl.ds(12 + slot + c * (3 - 2 * slot), 1), 0:640] += jnp.sum(
                mix.astype(f32), axis=0, keepdims=True
            )
        return carry

    lax.fori_loop(0, 4, mix_body, 0)
    def qkv_grads():
        for slot in range(2):
            point("ga" + str(slot))
            weight_grad(ga, slot, nrm, act[slot, :, 0:640])
            r1(CH_A, slot)

    if not QKV_GRADS_LAST:
        qkv_grads()
    point("dn0")
    for j in range(2):
        part(0, j, T_MLP).wait_send()
        part(1, j, T_DN2).wait_send()

    def dnorm_tile(rows):
        return dot(act[0, rows, 0:640], wa[0], 1, 1) + dot(act[1, rows, 0:640], wa[1], 1, 1)

    for j in range(2):
        st[0, j] = dnorm_tile(chunk(j, 1 - c)).astype(bf16)
        part(0, j, T_DNR).start()

    res_copies = a2a_out(0, stage)
    res_copies[0].wait()
    for cp in res_copies[1:]:
        cp.wait_send()

    def own_dnorm(j, carry):
        points("od", j, 2)
        dnr[...] = dnorm_tile(chunk(j, c))
        part(0, j, T_DNR).wait_recv()

        def ln1_back(i, carry):
            here = pl.ds(pl.multiple_of(j * tile + i * own_tok, own_tok), own_tok)
            local = pl.ds(pl.multiple_of(i * own_tok, own_tok), own_tok)
            unit, inverse = ln_parts(xin[here, :].astype(f32))
            up_grad = dnr[local, :] + rv[0, j, local, :].astype(f32)
            grad = mid[here, :] + ln_back(up_grad, unit, inverse, vec(0))
            stage[here, :] = grad.astype(bf16)
            smb[0:1, :] += jnp.sum(up_grad * unit, axis=0, keepdims=True)
            smb[1:2, :] += jnp.sum(up_grad, axis=0, keepdims=True)
            return carry

        lax.fori_loop(0, 4, ln1_back, 0)
        return carry

    lax.fori_loop(0, 2, own_dnorm, 0)
    ing_copies = a2a_out(1, stage)
    for cp in ing_copies:
        cp.start()
    if QKV_GRADS_LAST:
        qkv_grads()
    for i in range(24):
        point("e" + str(i))

    small = pltpu.make_async_copy(smb, sm_o, gout.at[4])
    small.start()
    for k in (CH_2, CH_1, CH_B, CH_A):
        rp_wait(k)
    for s in range(2):
        ag_drain(CH_A, s)
    for k in range(4):
        rs_drain(k)
    small.wait()
    for j in range(2):
        for buf, idx in ((nrm, T_NRM), (cot, T_COT), (n2, T_N2), (dml, T_DML)):
            swap(buf, j, idx).wait_send()
        part(0, j, T_DNR).wait_send()

    for s in range(2):
        @pl.when(zz == s)
        def _(s=s):
            for dz in range(1, 4):
                for cp in bias_copies(s, dz):
                    cp.wait_send()

    for cp in res_copies[1:]:
        cp.wait_recv()
    for cp in ing_copies:
        cp.wait()


def finish_kernel(
    res_i, ing_i, ga_i, gb_i, g1_i, g2_i, sm_i,
    res_o, ing_o, n1g, n1b, wq_o, qvb, ws_o, wo_o, ob, n2g, n2b, g1_o, f1b, g2_o, f2b,
    res, ing, sem,
):
    moves = [(res_i, res, res_o), (ing_i, ing, ing_o)]
    for i, (src, buf, _) in enumerate(moves):
        pltpu.make_async_copy(src, buf, sem.at[0, i]).start()
    z = lax.axis_index("tp")
    for row, ref in enumerate((n1g, n1b, ob, n2g, n2b, f2b)):
        ref[...] = sm_i[row, :]
    f1b[...] = sm_i[pl.ds(8 + z, 1), :][0]
    cols = wo_o.shape[1]
    mixed = sm_i[pl.ds(12 + z, 1), :]
    qvb[0:1, :] = mixed[:, 0:cols]
    qvb[1:2, :] = mixed[:, 2 * cols : 3 * cols]
    g1_o[...] = g1_i[...].astype(f32)
    g2_o[...] = g2_i[...].astype(f32)
    wo_o[...] = gb_i[:, 0:cols].astype(f32)
    i = lax.broadcasted_iota(jnp.int32, (640, cols), 0)
    j = lax.broadcasted_iota(jnp.int32, (640, cols), 1)
    for part in range(3):
        wq_o[part] = dot(ga_i[...], jnp.where(i == j + part * cols, 1.0, 0.0).astype(bf16), 1, 0)
    heads = ws_o.shape[0]
    i = lax.broadcasted_iota(jnp.int32, (heads, 640), 0)
    j = lax.broadcasted_iota(jnp.int32, (heads, 640), 1)
    ws_o[...] = dot(jnp.where(j == i + 3 * cols, 1.0, 0.0).astype(bf16), ga_i[...], 1, 1)
    for i, (src, buf, dst) in enumerate(moves):
        pltpu.make_async_copy(src, buf, sem.at[0, i]).wait()
        pltpu.make_async_copy(buf, dst, sem.at[1, i]).start()
    for i, (src, buf, dst) in enumerate(moves):
        pltpu.make_async_copy(buf, dst, sem.at[1, i]).wait()


def fast_layer(
    inputs, norm1_gain, norm1_bias, qkv_weight, qv_bias, score_weight, out_weight, out_bias,
    norm2_gain, norm2_bias, fc1_weight, fc1_bias, fc2_weight, fc2_bias, prefix, selected, cotangent,
):
    shard, _, cols = qkv_weight.shape
    heads = score_weight.shape[1]
    width = inputs.shape[2]
    own_tok = inputs.shape[1]
    seqs = inputs.shape[0]
    seq = 16 * own_tok
    vm = pltpu.VMEM
    ncols = (640, 256, 768, 768)
    hbm = pl.BlockSpec(memory_space=pl.ANY)
    vmem = pl.BlockSpec(memory_space=pltpu.VMEM)
    dma = pltpu.SemaphoreType.DMA
    outs = pl.pallas_call(
        layer_kernel,
        out_shape=[
            jax.ShapeDtypeStruct(inputs.shape, bf16),
            jax.ShapeDtypeStruct(inputs.shape, bf16),
        ]
        + [jax.ShapeDtypeStruct((shard, n), bf16) for n in ncols]
        + [jax.ShapeDtypeStruct((16, width), f32)],
        in_specs=[hbm] * 16 + [pl.BlockSpec(memory_space=pltpu.SMEM)],
        out_specs=[hbm] * 7,
        scratch_shapes=[vm((2, 768, n), bf16) for n in ncols]
        + [vm((2, 768, 640), bf16)]
        + [vm((6, 2 * shard, n), bf16) for n in ncols]
        + [vm((3 if k in RS_DIRECT else 2, 2 * shard, n), bf16) for k, n in enumerate(ncols)]
        + [vm((shard, n), bf16) for n in ncols]
        + [
            vm((seq // 2, width), bf16),
            vm((seq, width), bf16),
            vm((seq, width), bf16),
            vm((2, seq, 256), bf16),
            vm((2, seq + 2 * own_tok, 256), bf16),
            vm((2, seq + 2 * own_tok, 256), bf16),
            vm((2, seq, 256), bf16),
            vm((2, seq, 256), bf16),
            vm((32, 192, 256), bf16),
            vm((2, seq, 256), bf16),
            vm((seq // 2, width), f32),
            vm((seq, width), bf16),
            vm((2, seq, 768), bf16),
            vm((2, seq, 768), bf16),
            vm((2, 2, seq // 4, width), bf16),
            vm((2, 2, seq // 4, width), bf16),
            vm((seq // 4, width), f32),
            vm((seq, width), bf16),
            vm((2, seq, 256), bf16),
            vm((2, seq + 2 * own_tok, 768), f32),
            vm((2, seq, 128), f32),
            vm((seq // 2, width), bf16),
            vm((4, 4, 4, seqs), jnp.int32),
            vm((4, 8, 256), jnp.int32),
            vm((3, shard, cols), bf16),
            vm((heads, shard), bf16),
            vm((shard, cols), bf16),
            vm((shard, 640), bf16),
            vm((shard, 256), bf16),
        ]
        + [vm((width,), f32)] * 8
        + [
            vm((2, 2, cols), f32),
            vm((16, 768), f32),
            vm((5, 16, 768), f32),
            dma((2, 8)), dma((2, 8)), dma((2, 8)), dma((2, 8)),
            dma((4, 12)), dma((4, 9)), dma((4, 9)), dma((4, 10)),
            dma((16,)), dma((16,)), dma((4,)), dma((4,)), dma((2, 4)), dma((2, 2)),
            dma((5,)), dma((5,)), dma((13,)), dma((5,)),
        ],
        compiler_params=pltpu.CompilerParams(
            collective_id=0, has_side_effects=True, vmem_limit_bytes=67043328
        ),
    )(
        inputs, cotangent, jnp.transpose(qkv_weight, (1, 0, 2)), jnp.transpose(score_weight), out_weight,
        fc1_weight, fc2_weight, jnp.transpose(selected, (1, 2, 0)), norm1_gain, norm1_bias,
        out_bias, norm2_gain, norm2_bias, fc2_bias, fc1_bias, qv_bias, prefix,
    )
    line = jax.ShapeDtypeStruct((width,), f32)
    square = jax.ShapeDtypeStruct((shard, 768), f32)
    done = pl.pallas_call(
        finish_kernel,
        out_shape=[
            jax.ShapeDtypeStruct(inputs.shape, bf16), jax.ShapeDtypeStruct(inputs.shape, bf16), line, line,
            jax.ShapeDtypeStruct((3, shard, cols), f32), jax.ShapeDtypeStruct((2, cols), f32),
            jax.ShapeDtypeStruct((heads, shard), f32), jax.ShapeDtypeStruct((shard, cols), f32),
            line, line, line, square, line, square, line,
        ],
        in_specs=[hbm, hbm] + [vmem] * 5,
        out_specs=[hbm, hbm] + [vmem] * 13,
        scratch_shapes=[vm(inputs.shape, bf16), vm(inputs.shape, bf16), dma((2, 2))],
    )(*outs)
    done = list(done)
    done[4] = jnp.transpose(done[4], (1, 0, 2))
    done[6] = jnp.transpose(done[6])
    return tuple(done)


def general(mesh):
    placed = (
        P("fsdp", ("ctx", "tp"), None),
        P(),
        P(),
        P(("fsdp", "ctx"), None, "tp"),
        P(None, "tp"),
        P(("fsdp", "ctx"), "tp"),
        P(("fsdp", "ctx"), "tp"),
        P(),
        P(),
        P(),
        P(("fsdp", "ctx"), "tp"),
        P("tp"),
        P(("fsdp", "ctx"), "tp"),
        P(),
        P("fsdp"),
        P("fsdp", "ctx", None),
        P("fsdp", ("ctx", "tp"), None),
    )
    return jax.shard_map(
        shards,
        mesh=mesh,
        in_specs=placed,
        out_specs=(
            P("fsdp", ("ctx", "tp"), None),
            P("fsdp", ("ctx", "tp"), None),
            P(),
            P(),
            P(("fsdp", "ctx"), None, "tp"),
            P(None, "tp"),
            P(("fsdp", "ctx"), "tp"),
            P(("fsdp", "ctx"), "tp"),
            P(),
            P(),
            P(),
            P(("fsdp", "ctx"), "tp"),
            P("tp"),
            P(("fsdp", "ctx"), "tp"),
            P(),
        ),
        check_vma=False,
    )


def solution(mesh):
    shape = dict(mesh.shape)
    if shape != {"fsdp": 2, "ctx": 4, "tp": 4}:
        return general(mesh)
    split = Mesh(mesh.devices.reshape(2, 2, 2, 4), ("fsdp", "xo", "team", "tp"))
    ctx = ("xo", "team")
    rows = ("fsdp", "xo", "team")
    tokens = P("fsdp", ("xo", "team", "tp"), None)
    placed = (
        tokens, P(), P(), P(rows, None, "tp"), P(None, "tp"), P(rows, "tp"), P(rows, "tp"), P(), P(), P(),
        P(rows, "tp"), P("tp"), P(rows, "tp"), P(), P("fsdp"), P("fsdp", ctx, None), tokens,
    )
    given = (
        tokens, tokens, P(), P(), P(rows, None, "tp"), P(None, "tp"), P(rows, "tp"), P(rows, "tp"),
        P(), P(), P(), P(rows, "tp"), P("tp"), P(rows, "tp"), P(),
    )
    return jax.shard_map(fast_layer, mesh=split, in_specs=placed, out_specs=given, check_vma=False)
```

```python
from functools import partial

import jax
import jax.numpy as jnp
from jax import lax
from jax.experimental import pallas as pl
from jax.experimental.pallas import tpu as pltpu
from jax.sharding import Mesh
from jax.sharding import PartitionSpec as P

HD = 64
QB = 64
KB = 16
SEL = 4
WIN = 64
SEQ_MB = 4
MICRO = 2


epsilon = 1e-05
negative_fill = -1e30


def contract(left, right, left_dim, right_dim):
    return lax.dot_general(
        left, right, (((left_dim,), (right_dim,)), ((), ())), preferred_element_type=jnp.float32
    )


def rounded(values):
    return values.astype(jnp.bfloat16)


def norm_rows(values, gain, shift):
    centred = values - jnp.mean(values, axis=-1, keepdims=True)
    inverse = lax.rsqrt(jnp.mean(centred * centred, axis=-1, keepdims=True) + epsilon)
    unit_rows = centred * inverse
    return (unit_rows * gain + shift, unit_rows, inverse)


def norm_back(upstream, unit_rows, inverse, gain):
    scaled = upstream * gain
    centred = scaled - jnp.mean(scaled, axis=-1, keepdims=True)
    return inverse * (centred - unit_rows * jnp.mean(scaled * unit_rows, axis=-1, keepdims=True))


def pick_rows(source, key_picks):
    return jax.vmap(lambda table_in, places: table_in[places])(source, key_picks)


def shards(
    inputs,
    norm1_gain,
    norm1_bias,
    qkv_weight,
    qv_bias,
    score_weight,
    out_weight,
    out_bias,
    norm2_gain,
    norm2_bias,
    fc1_weight,
    fc1_bias,
    fc2_weight,
    fc2_bias,
    prefix,
    selected,
    cotangent,
):
    all_seqs, own_tok, width_full = inputs.shape
    ctx_tok = own_tok * lax.axis_size("tp")
    heads_local = score_weight.shape[1]
    hidden_local = out_weight.shape[1]
    units_local = fc1_bias.shape[0]
    seq_full = ctx_tok * lax.axis_size("ctx")
    blocks_local = ctx_tok // QB
    near_span = QB + 2 * WIN
    chosen_span = SEL * KB
    key_count = chosen_span + near_span
    tokens = SEQ_MB * ctx_tok
    score_scale = HD ** (-0.5)
    own_start = lax.axis_index("tp") * own_tok
    block_ids = lax.axis_index("ctx") * blocks_local + jnp.arange(blocks_local, dtype=jnp.int32)
    query_pos = block_ids[:, None] * QB + jnp.arange(QB, dtype=jnp.int32)[None, :]
    near_picks = block_ids[:, None] * QB + jnp.arange(near_span, dtype=jnp.int32)[None, :]
    is_chosen = jnp.arange(key_count) < chosen_span
    qkv_offsets = jnp.stack([qv_bias[0], jnp.zeros_like(qv_bias[0]), qv_bias[1]])
    key_own = lax.axis_index("ctx") * ctx_tok + jnp.arange(ctx_tok, dtype=jnp.int32)
    every_query = jnp.arange(seq_full, dtype=jnp.int32)
    chosen_every = lax.all_gather(selected, "ctx", axis=1, tiled=True)

    def scores_of(queries, keys_near, gates_near, allowed):
        raw_scores = (
            jnp.einsum("sbqhd,sbkhd->sbhqk", queries, keys_near, preferred_element_type=jnp.float32)
            * score_scale
        )
        logits = raw_scores + jnp.transpose(gates_near, (0, 1, 3, 2))[:, :, :, None, :].astype(
            jnp.float32
        )
        return jnp.where(allowed[:, :, None], logits, negative_fill)

    def micro_step(micro_index, carried):
        big_sums, small_sums, out_buffer, grad_buffer = carried
        qkv_full, score_full, out_full, fc1_full, fc2_full = (
            lax.all_gather(qkv_weight, ("fsdp", "ctx"), axis=0, tiled=True),
            lax.all_gather(score_weight, ("fsdp", "ctx"), axis=0, tiled=True),
            lax.all_gather(out_weight, ("fsdp", "ctx"), axis=0, tiled=True),
            lax.all_gather(fc1_weight, ("fsdp", "ctx"), axis=0, tiled=True),
            lax.all_gather(fc2_weight, ("fsdp", "ctx"), axis=0, tiled=True),
        )
        seq_start = micro_index * SEQ_MB
        local_rows = lax.dynamic_slice_in_dim(inputs, seq_start, SEQ_MB, 0)
        full_rows = (
            lax.all_gather(local_rows, "tp", axis=1, tiled=True)
            .astype(jnp.float32)
            .reshape(tokens, width_full)
        )
        normed, unit_one, inverse_one = norm_rows(full_rows, norm1_gain, norm1_bias)
        normed_low = rounded(normed)
        qkv_flat = qkv_full.reshape(width_full, 3 * hidden_local)
        mixed_rows = contract(normed_low, qkv_flat, 1, 0).reshape(tokens, 3, hidden_local)
        mixed_low = rounded(mixed_rows + qkv_offsets)
        scoring = contract(normed_low, score_full, 1, 0)
        gate_low = rounded(jax.nn.log_sigmoid(scoring))
        kv_local = mixed_low[:, 1:].reshape(SEQ_MB, ctx_tok, 2 * hidden_local)
        kv_all, gate_all = (
            lax.all_gather(kv_local, "ctx", axis=1, tiled=True),
            lax.all_gather(
                gate_low.reshape(SEQ_MB, ctx_tok, heads_local), "ctx", axis=1, tiled=True
            ),
        )
        kv_padded = jnp.pad(kv_all, ((0, 0), (WIN, WIN), (0, 0)))
        gate_padded = jnp.pad(gate_all, ((0, 0), (WIN, WIN), (0, 0)))
        chosen = lax.dynamic_slice_in_dim(selected, seq_start, SEQ_MB, 0)
        chosen_picks = (chosen[..., None] * KB + jnp.arange(KB, dtype=jnp.int32) + WIN).reshape(
            SEQ_MB, blocks_local, chosen_span
        )
        key_picks = jnp.concatenate(
            [chosen_picks, jnp.broadcast_to(near_picks, (SEQ_MB, blocks_local, near_span))], axis=-1
        )
        key_pos = (key_picks - WIN)[:, :, None, :]
        query_at = query_pos[None, :, :, None]
        prefix_now = lax.dynamic_slice_in_dim(prefix, seq_start, SEQ_MB, 0)
        prefix_end = prefix_now[:, None, None, None]
        permitted = (key_pos <= query_at) | (query_at < prefix_end) & (key_pos < prefix_end)
        inside = (key_pos >= 0) & (key_pos < seq_full)
        near_by = jnp.abs(query_at - key_pos) < WIN
        allowed = inside & permitted & jnp.where(is_chosen, jnp.logical_not(near_by), near_by)
        kv_near = pick_rows(kv_padded, key_picks).reshape(
            SEQ_MB, blocks_local, key_count, 2, heads_local, HD
        )
        keys_near = kv_near[:, :, :, 0]
        values_near = kv_near[:, :, :, 1]
        gates_near = pick_rows(gate_padded, key_picks)
        queries = mixed_low[:, 0].reshape(SEQ_MB, blocks_local, QB, heads_local, HD)
        logits = scores_of(queries, keys_near, gates_near, allowed)
        row_max = jnp.max(logits, axis=-1, keepdims=True)
        log_total = row_max + jnp.log(jnp.sum(jnp.exp(logits - row_max), axis=-1, keepdims=True))
        probs_low = rounded(jnp.exp(logits - log_total))
        attended = jnp.einsum(
            "sbhqk,sbkhd->sbqhd", probs_low, values_near, preferred_element_type=jnp.float32
        )
        attended_low = rounded(attended).reshape(tokens, hidden_local)
        branch = contract(attended_low, out_full, 1, 1).reshape(SEQ_MB, ctx_tok, width_full)
        middle = (
            local_rows.astype(jnp.float32)
            + lax.psum_scatter(branch, "tp", scatter_dimension=1, tiled=True)
            + out_bias
        )
        middle_full = lax.all_gather(middle, "tp", axis=1, tiled=True).reshape(tokens, width_full)
        normed_two, unit_two, inverse_two = norm_rows(middle_full, norm2_gain, norm2_bias)
        normed_two_low = rounded(normed_two)
        before = contract(normed_two_low, fc1_full, 1, 0) + fc1_bias
        activated, gelu_back = jax.vjp(partial(jax.nn.gelu, approximate=True), before)
        activated_low = rounded(activated)
        mlp_terms = contract(activated_low, fc2_full, 1, 1).reshape(SEQ_MB, ctx_tok, width_full)
        outcome = (
            middle
            + lax.psum_scatter(
                mlp_terms.astype(jnp.bfloat16), "tp", scatter_dimension=1, tiled=True
            ).astype(jnp.float32)
            + fc2_bias
        )
        out_buffer = lax.dynamic_update_slice_in_dim(out_buffer, rounded(outcome), seq_start, 0)
        grad_local = lax.dynamic_slice_in_dim(cotangent, seq_start, SEQ_MB, 0)
        grad_low = lax.all_gather(grad_local, "tp", axis=1, tiled=True).reshape(tokens, width_full)
        grad_rows = grad_low.astype(jnp.float32)
        d_activated = contract(grad_low, fc2_full, 1, 0)
        d_before_low = rounded(gelu_back(d_activated)[0])
        fc2_step = contract(grad_low, activated_low, 0, 0)
        fc1_step = contract(normed_two_low, d_before_low, 0, 0)
        d_normed_two = lax.psum(contract(d_before_low, fc1_full, 1, 1), "tp")
        d_middle = grad_rows + norm_back(d_normed_two, unit_two, inverse_two, norm2_gain)
        d_middle_low = rounded(d_middle)
        out_step = contract(d_middle_low, attended_low, 0, 0)
        d_attended = rounded(contract(d_middle_low, out_full, 1, 0)).reshape(
            SEQ_MB, blocks_local, QB, heads_local, HD
        )
        probs_again = jnp.exp(scores_of(queries, keys_near, gates_near, allowed) - log_total)
        d_probs = jnp.einsum(
            "sbqhd,sbkhd->sbhqk", d_attended, values_near, preferred_element_type=jnp.float32
        )
        row_delta = jnp.sum(probs_again * d_probs, axis=-1, keepdims=True)
        d_logits = probs_again * (d_probs - row_delta)
        d_logits_low = rounded(d_logits)
        d_queries = (
            jnp.einsum(
                "sbhqk,sbkhd->sbqhd", d_logits_low, keys_near, preferred_element_type=jnp.float32
            )
            * score_scale
        )
        stats_local = (
            jnp.transpose(log_total, (0, 1, 3, 2, 4)).reshape(SEQ_MB, ctx_tok, heads_local),
            jnp.transpose(row_delta, (0, 1, 3, 2, 4)).reshape(SEQ_MB, ctx_tok, heads_local),
        )
        queries_flat = mixed_low[:, 0].reshape(SEQ_MB, ctx_tok, hidden_local)
        d_att_flat = d_attended.reshape(SEQ_MB, ctx_tok, hidden_local)
        queries_every, d_att_every = (
            lax.all_gather(queries_flat, "ctx", axis=1, tiled=True),
            lax.all_gather(d_att_flat, "ctx", axis=1, tiled=True),
        )
        log_every, delta_every = (
            lax.all_gather(stats_local[0], "ctx", axis=1, tiled=True),
            lax.all_gather(stats_local[1], "ctx", axis=1, tiled=True),
        )
        chosen_now = lax.dynamic_slice_in_dim(chosen_every, seq_start, SEQ_MB, 0)
        query_all = every_query[None, :, None]
        key_all = key_own[None, None, :]
        end_all = prefix_now[:, None, None]
        permitted_all = (key_all <= query_all) | (query_all < end_all) & (key_all < end_all)
        near_all = jnp.abs(query_all - key_all) < WIN
        block_hits = jnp.any(
            chosen_now[:, :, :, None] == (key_own // KB)[None, None, None, :], axis=2
        )
        member = jnp.repeat(block_hits, QB, axis=1)
        allowed_all = permitted_all & (near_all | member)
        queries_four = queries_every.reshape(SEQ_MB, seq_full, heads_local, HD)
        d_att_four = d_att_every.reshape(SEQ_MB, seq_full, heads_local, HD)
        keys_own = mixed_low[:, 1].reshape(SEQ_MB, ctx_tok, heads_local, HD)
        values_own = mixed_low[:, 2].reshape(SEQ_MB, ctx_tok, heads_local, HD)
        gates_own = gate_low.reshape(SEQ_MB, ctx_tok, heads_local)
        logits_own = (
            jnp.einsum(
                "sqhd,skhd->shqk", queries_four, keys_own, preferred_element_type=jnp.float32
            )
            * score_scale
        )
        logits_own = logits_own + jnp.transpose(gates_own, (0, 2, 1))[:, :, None, :].astype(
            jnp.float32
        )
        logits_own = jnp.where(allowed_all[:, None], logits_own, negative_fill)
        probs_own = jnp.exp(logits_own - jnp.transpose(log_every, (0, 2, 1))[..., None])
        d_probs_own = jnp.einsum(
            "sqhd,skhd->shqk", d_att_four, values_own, preferred_element_type=jnp.float32
        )
        d_logits_own = probs_own * (d_probs_own - jnp.transpose(delta_every, (0, 2, 1))[..., None])
        d_keys_own = (
            jnp.einsum(
                "shqk,sqhd->skhd",
                rounded(d_logits_own),
                queries_four,
                preferred_element_type=jnp.float32,
            )
            * score_scale
        )
        d_values_own = jnp.einsum(
            "shqk,sqhd->skhd", rounded(probs_own), d_att_four, preferred_element_type=jnp.float32
        )
        d_kv_mine = jnp.stack([d_keys_own, d_values_own], axis=2).reshape(
            SEQ_MB, ctx_tok, 2 * hidden_local
        )
        d_gate_mine = jnp.transpose(jnp.sum(d_logits_own, axis=2), (0, 2, 1))
        d_kv_low = rounded(d_kv_mine).reshape(tokens, 2, hidden_local)
        gate_grad = (
            lax.optimization_barrier(rounded(d_gate_mine))
            .astype(jnp.float32)
            .reshape(tokens, heads_local)
        )
        d_scoring_low = rounded(gate_grad * jax.nn.sigmoid(-scoring))
        d_queries_low = rounded(d_queries).reshape(tokens, 1, hidden_local)
        d_mixed = jnp.concatenate([d_queries_low, d_kv_low], axis=1).reshape(
            tokens, 3 * hidden_local
        )
        qkv_step = contract(normed_low, d_mixed, 0, 0).reshape(width_full, 3, hidden_local)
        score_step = contract(normed_low, d_scoring_low, 0, 0)
        d_normed_part = contract(d_mixed, qkv_flat, 1, 1) + contract(
            d_scoring_low, score_full, 1, 1
        )
        d_normed = lax.psum(d_normed_part.astype(jnp.bfloat16), "tp").astype(jnp.float32)
        d_inputs = (d_middle + norm_back(d_normed, unit_one, inverse_one, norm1_gain)).reshape(
            SEQ_MB, ctx_tok, width_full
        )
        d_inputs_mine = lax.dynamic_slice_in_dim(d_inputs, own_start, own_tok, 1)
        grad_buffer = lax.dynamic_update_slice_in_dim(
            grad_buffer, rounded(d_inputs_mine), seq_start, 0
        )
        small_step = (
            jnp.sum(d_normed * unit_one, axis=0),
            jnp.sum(d_normed, axis=0),
            jnp.stack(
                [
                    jnp.sum(d_queries_low[:, 0], axis=0, dtype=jnp.float32),
                    jnp.sum(d_kv_low[:, 1], axis=0, dtype=jnp.float32),
                ]
            ),
            jnp.sum(d_middle, axis=0),
            jnp.sum(d_normed_two * unit_two, axis=0),
            jnp.sum(d_normed_two, axis=0),
            jnp.sum(d_before_low, axis=0, dtype=jnp.float32),
            jnp.sum(grad_rows, axis=0),
        )
        big_step = (qkv_step, score_step, out_step, fc1_step, fc2_step)
        big_sums = jax.tree.map(jnp.add, big_sums, big_step)
        small_sums = jax.tree.map(jnp.add, small_sums, small_step)
        return (big_sums, small_sums, out_buffer, grad_buffer)

    big_init = (
        jnp.zeros((width_full, 3, hidden_local), jnp.float32),
        jnp.zeros((width_full, heads_local), jnp.float32),
        jnp.zeros((width_full, hidden_local), jnp.float32),
        jnp.zeros((width_full, units_local), jnp.float32),
        jnp.zeros((width_full, units_local), jnp.float32),
    )
    small_init = (
        jnp.zeros((width_full,), jnp.float32),
        jnp.zeros((width_full,), jnp.float32),
        jnp.zeros((2, hidden_local), jnp.float32),
        jnp.zeros((width_full,), jnp.float32),
        jnp.zeros((width_full,), jnp.float32),
        jnp.zeros((width_full,), jnp.float32),
        jnp.zeros((units_local,), jnp.float32),
        jnp.zeros((width_full,), jnp.float32),
    )
    buffer_init = jnp.zeros(inputs.shape, jnp.bfloat16)
    big_sums, small_sums, out_buffer, grad_buffer = lax.fori_loop(
        0, MICRO, micro_step, (big_init, small_init, buffer_init, buffer_init)
    )
    big_grads = (
        lax.psum_scatter(big_sums[0], ("fsdp", "ctx"), scatter_dimension=0, tiled=True),
        lax.psum_scatter(big_sums[1], ("fsdp", "ctx"), scatter_dimension=0, tiled=True),
        lax.psum_scatter(big_sums[2], ("fsdp", "ctx"), scatter_dimension=0, tiled=True),
        lax.psum_scatter(big_sums[3], ("fsdp", "ctx"), scatter_dimension=0, tiled=True),
        lax.psum_scatter(big_sums[4], ("fsdp", "ctx"), scatter_dimension=0, tiled=True),
    )
    small_grads = lax.psum(
        (
            small_sums[0],
            small_sums[1],
            small_sums[2],
            small_sums[3],
            small_sums[4],
            small_sums[5],
            small_sums[6],
            small_sums[7],
        ),
        ("fsdp", "ctx"),
    )
    return (
        out_buffer,
        grad_buffer,
        small_grads[0],
        small_grads[1],
        big_grads[0],
        small_grads[2],
        big_grads[1],
        big_grads[2],
        small_grads[3],
        small_grads[4],
        small_grads[5],
        big_grads[3],
        small_grads[6],
        big_grads[4],
        small_grads[7],
    )


EPS = 1e-05
MASKED = -1e30
MESH_ID = pl.DeviceIdType.MESH
CH_A, CH_B, CH_1, CH_2 = 0, 1, 2, 3
f32 = jnp.float32
bf16 = jnp.bfloat16


def dot(left, right, left_dim, right_dim):
    return lax.dot_general(
        left, right, (((left_dim,), (right_dim,)), ((), ())), preferred_element_type=f32
    )


def ln_parts(rows):
    centred = rows - jnp.mean(rows, axis=-1, keepdims=True)
    inverse = lax.rsqrt(jnp.mean(centred * centred, axis=-1, keepdims=True) + EPS)
    return centred * inverse, inverse


def ln_back(upstream, unit, inverse, gain):
    scaled = upstream * gain
    return inverse * (
        scaled
        - jnp.mean(scaled, axis=-1, keepdims=True)
        - unit * jnp.mean(scaled * unit, axis=-1, keepdims=True)
    )


PLAN = {
    "front": (("p0w", 0), ("za", 0, 0), ("za", 0, 1), ("p0w", 3), ("p0w", 2), ("p0w", 1), ("a2a", "x"), ("s1", 0, 1), ("za", 1, 1), ("s1", 0, 0), ("s2", 0, 1),),
    "x_wait": (("za", 1, 0), ("zr2", 0, 1),),
    "ln1": (("za", 2, 0), ("s2", 0, 0), ("za", 3, 0), ("a2a", "cot"),),
    "nrm_wait": (("zr2", 0, 0), ("s1", 1, 1),),
    "qkv0": (("s1", 1, 0),),
    "qkv2": (("s1", 2, 0),),
    "gat1": (("s2", 1, 0),),
    "fwd3": (("za", 3, 1), ("s2", 1, 1),),
    "fwd5": (("s1", 3, 0),),
    "fwd8": (("zr2", 1, 1),),
    "fwd11": (("s1", 3, 1),),
    "fwd12": (("s2", 3, 0),),
    "fwd13": (("zr2", 3, 0), ("zr2", 1, 0), ("s2", 2, 0),),
    "fwd14": (("za", 2, 1), ("cotw",),),
    "br0": (("zr2", 2, 0),),
    "br1": (("s1", 2, 1),),
    "mlpa2": (("s2", 2, 1), ("s2", 3, 1),),
    "pm0": (("zr2", 2, 1), ("zr2", 3, 1),),
    "datt": (("r2", 2, 0), ("r2", 3, 0),),
    "bwd2": (("r2", 1, 0), ("r3", 3, 0),),
    "bwd5": (("a2a", "res"),),
    "bwd9": (("r3", 2, 0),),
    "bwd11": (("r2", 1, 1),),
    "bwd12": (("r2", 3, 1),),
    "bwd14": (("r2", 2, 1), ("r3b", 3, 0),),
    "ga1": (("r3b", 2, 0), ("r3", 1, 1),),
    "dn0": (("r3", 2, 1),),
    "e0": (("r3b", 1, 1),),
    "e1": (("r3", 1, 0),),
    "e2": (("hs", 0),),
    "e3": (("hw", 0), ("hs", 1),),
    "e4": (("r3b", 1, 0),),
    "e5": (("r2", 0, 0),),
    "e6": (("r2", 0, 1),),
    "e7": (("r3b", 2, 1),),
    "e9": (("hw", 1),),
    "e11": (("hs", 2),),
    "e12": (("r3", 0, 0), ("r4", 2),),
    "e13": (("hw", 2), ("hs", 3),),
    "e14": (("r3b", 0, 0), ("r3", 0, 1), ("hw", 3),),
    "e16": (("r3b", 0, 1),),
    "e17": (("r4", 0),),
    "e18": (("r3", 3, 1),),
    "e19": (("r4", 1), ("r3b", 3, 1), ("hs", 4),),
    "e20": (("r4", 3),),
    "e22": (("hw", 4),),
}
PEER_FIRST, FF_GRADS_LATER, QKV_GRADS_LAST = False, True, False
AG_Z_LAST, RS_Z_FIRST = {(1, 0)}, {(1, 0)}
AG_DIRECT, RS_DIRECT = (), ()
AG_XLIGHT = {(2, 1), (3, 0), (0, 0), (1, 0), (1, 1)}
RS_XLIGHT = {(3, 0), (3, 1), (0, 0), (0, 1), (1, 0)}


def layer_kernel(
    x_hbm, cot_hbm, wq_hbm, ws_hbm, wo_hbm, f1_hbm, f2_hbm, sel_hbm, n1g, n1b, ob, n2g, n2b, f2b, f1b, qvb, pref,
    res_o, ing_o, ga_o, gb_o, g1_o, g2_o, sm_o,
    wa, wb, w1, w2, ga,
    rba, rbb, rb1, rb2, rza, rzb, rz1, rz2, rpa, rpb, rp1, rp2,
    xin, cot, nrm, qb, kb, vb, ksel, vsel, pr, att, mid, n2, act, dbf,
    st, rv, dnr, dml, datt, acc, scr, stage, selraw, selb, wq, ws, wo, pa, pb, v0, v1, v2, v3, v4, v5, fb0, fb1, qvbb, smb, smr,
    ain_s, ain_r, aout_s, aout_r, ag_s, ag_r, rs_s, rs_r, tm_s, tm_r,
    sel_s, sel_r, bias_s, bias_r, sm_s, sm_r, loc, gout,
):
    y = lax.axis_index("fsdp")
    x = lax.axis_index("xo")
    c = lax.axis_index("team")
    z = lax.axis_index("tp")
    zz = z + c * (3 - 2 * z)
    source = zz < 2
    own_tok = x_hbm.shape[1]
    width = x_hbm.shape[2]
    tile = 4 * own_tok
    half = 2 * tile
    seq = 2 * half
    my_seq = x * 4 + z
    hbms = (pa, pb, f1_hbm, f2_hbm)
    weights = (wa, wb, w1, w2)
    grads = (ga, wb, w1, w2)
    rbs = (rba, rbb, rb1, rb2)
    rzs = (rza, rzb, rz1, rz2)
    rps = (rpa, rpb, rp1, rp2)
    g_outs = (ga_o, gb_o, g1_o, g2_o)
    shard = f1_hbm.shape[0]
    pair = 2 * shard
    over_x, over_y, other = {"xo": 1 - x}, {"fsdp": 1 - y}, {"team": 1 - c}

    def block(yy, xx):
        return pl.ds(pl.multiple_of((yy * 4 + xx * 2) * shard, pair), pair)

    mine = block(y, x)
    vecs, fbs = (v0, v1, v2, v3, v4, v5), (fb0, fb1)

    def vec(i):
        return vecs[i][...].reshape(1, width)

    far_x, far_y = block(y, 1 - x), block(1 - y, x)
    far_xy = block(1 - y, 1 - x)

    def at_zz(q):
        return {"tp": q + c * (3 - 2 * q)}

    def own_shard(cc):
        return pl.ds(pl.multiple_of((y * 4 + x * 2 + cc) * shard, shard), shard)

    def rcopy(src, dst, ss, rs, dev):
        return pltpu.make_async_remote_copy(
            src_ref=src, dst_ref=dst, send_sem=ss, recv_sem=rs, device_id=dev, device_id_type=MESH_ID
        )

    bar = pltpu.get_barrier_semaphore()
    peers = []
    for dx in range(2):
        for dz in range(4):
            if dx or dz:
                peers.append({"xo": lax.rem(x + dx, 2), "tp": lax.rem(z + dz, 4)})
    peers += [other, over_y, {"xo": 1 - x, "team": 1 - c}]
    for peer in peers:
        pl.semaphore_signal(bar, 1, device_id=peer, device_id_type=MESH_ID)
    pl.semaphore_wait(bar, len(peers))

    def a2a_in(which, hbm):
        out = []
        for dx in range(2):
            for dz in range(4):
                xx, z2 = lax.rem(x + dx, 2), lax.rem(z + dz, 4)
                if which == 0:
                    at = pl.ds(pl.multiple_of(x * tile + z * own_tok, own_tok), own_tok)
                    dst = xin.at[at]
                else:
                    at = pl.ds(pl.multiple_of(x * half + c * tile + z * own_tok, own_tok), own_tok)
                    dst = cot.at[at]
                idx = dx * 4 + dz
                src = hbm.at[xx * 4 + z2]
                if idx == 0:
                    out.append(pltpu.make_async_copy(src, dst, ain_r.at[which, 0]))
                else:
                    out.append(
                        rcopy(src, dst, ain_s.at[which, idx], ain_r.at[which, idx], {"xo": xx, "tp": z2})
                    )
        return out

    def a2a_in_wait(copies):
        copies[0].wait()
        for cp in copies[1:]:
            cp.wait()

    def p0_local(k):
        return pltpu.make_async_copy(hbms[k], weights[k].at[zz, own_shard(c)], loc.at[k])

    def p0_away(k):
        return rcopy(
            hbms[k], weights[k].at[3 - zz, own_shard(c)], ag_s.at[k, 5], ag_r.at[k, 2], other
        )

    def p0_back(k):
        return rcopy(
            hbms[k], weights[k].at[zz, own_shard(1 - c)], ag_s.at[k, 5], ag_r.at[k, 2], other
        )

    def p0_start(k):
        @pl.when(source)
        def _():
            p0_local(k).start()

        @pl.when(jnp.logical_not(source))
        def _():
            p0_away(k).start()

    def p0_wait(k):
        @pl.when(source)
        def _():
            p0_local(k).wait()
            p0_back(k).wait_recv()

        @pl.when(jnp.logical_not(source))
        def _():
            p0_away(k).wait_send()

    def z_copy(k, s, q, idx):
        ref = weights[k].at[s] if (k, s) in AG_Z_LAST else weights[k].at[s, mine]
        return rcopy(ref, ref, ag_s.at[k, idx], ag_r.at[k, s], at_zz(q))

    def z_sends(k, s):
        out = [z_copy(k, s, 2, 0), z_copy(k, s, 1 - s, 1)]
        if k in AG_DIRECT:
            out.append(z_copy(k, s, 3, 2))
        return out

    def xy_start(k, s):
        for which in (0, 1) if (k, s) in AG_XLIGHT else (1, 0):
            xy(k, s, which).start()

    def z_start(k, s):
        @pl.when(zz == s)
        def _():
            if (k, s) in AG_Z_LAST:
                xy_start(k, s)
            else:
                for cp in z_sends(k, s):
                    cp.start()

    def z_relay(k, s):
        if (k, s) in AG_Z_LAST:
            @pl.when(zz == 2)
            def _():
                z_copy(k, s, 2, 0).wait_recv()
                z_copy(k, s, 3, 3 + s).start()

    def xy(k, s, which):
        light = (k, s) in AG_XLIGHT
        rows, dev = (
            (mine, over_x),
            (mine, over_y),
            (far_x, over_y) if light else (far_y, over_x),
        )[which]
        ref = weights[k].at[s, rows]
        return rcopy(ref, ref, ag_s.at[k, 6 + 3 * s + which], ag_r.at[k, 3 + 3 * s + which], dev)

    def s1(k, s):
        if (k, s) in AG_Z_LAST:
            @pl.when(zz == s)
            def _():
                xy(k, s, 0 if (k, s) in AG_XLIGHT else 1).wait_recv()
                xy(k, s, 2).start()
            return

        @pl.when(zz != s)
        def _():
            z_copy(k, s, 2, 0).wait_recv()

        if k not in AG_DIRECT:
            @pl.when(zz == 2)
            def _():
                z_copy(k, s, 3, 3 + s).start()

        xy_start(k, s)

    def s2(k, s):
        if (k, s) in AG_Z_LAST:
            @pl.when(zz == s)
            def _():
                for which in (1 if (k, s) in AG_XLIGHT else 0, 2):
                    xy(k, s, which).wait_recv()
                for cp in z_sends(k, s):
                    cp.start()
            return

        xy(k, s, 0 if (k, s) in AG_XLIGHT else 1).wait_recv()
        xy(k, s, 2).start()

    def s3(k, s):
        if (k, s) in AG_Z_LAST:
            @pl.when((zz == 1 - s) | (zz == 3))
            def _():
                z_copy(k, s, 2, 0).wait_recv()
            return

        for which in (1 if (k, s) in AG_XLIGHT else 0, 2):
            xy(k, s, which).wait_recv()

    def ag_drain(k, s):
        @pl.when(zz == s)
        def _():
            for cp in z_sends(k, s):
                cp.wait_send()

        if k not in AG_DIRECT:
            @pl.when(zz == 2)
            def _():
                z_copy(k, s, 3, 3 + s).wait_send()

        @pl.when(zz == s if (k, s) in AG_Z_LAST else zz >= 0)
        def _():
            for which in range(3):
                xy(k, s, which).wait_send()

    def rs_copy(k, s, which):
        light = (k, s) in RS_XLIGHT
        rows, dev = (
            (far_xy, over_y if light else over_x),
            (far_y, over_y) if light else (far_x, over_x),
            (far_x, over_x) if light else (far_y, over_y),
        )[which]
        i = 3 * s + which
        return rcopy(grads[k].at[s, rows], rbs[k].at[i], rs_s.at[k, i], rs_r.at[k, i], dev)

    def add_rows(k, slot, rows, bufs):
        g = grads[k]
        total = g[slot, rows, :].astype(f32)
        for buf in bufs:
            total = total + buf[...].astype(f32)
        g[slot, rows, :] = total.astype(bf16)

    def xy_first(k, s):
        for which in range(2):
            rs_copy(k, s, which).start()

    def xy_second(k, s):
        rs_copy(k, s, 0).wait_recv()
        add_rows(k, s, far_x if (k, s) in RS_XLIGHT else far_y, [rbs[k].at[3 * s]])
        rs_copy(k, s, 2).start()

    def xy_sum(k, s):
        for which in range(1, 3):
            rs_copy(k, s, which).wait_recv()
        add_rows(k, s, mine, [rbs[k].at[3 * s + 1], rbs[k].at[3 * s + 2]])

    def z_first(k, s):
        @pl.when(zz == 3)
        def _():
            rz_copy(k, s, 2, s).start()

        @pl.when(zz == 1 - s)
        def _():
            rz_copy(k, s, s, 0).start()

    def z_second(k, s):
        @pl.when(zz == 2)
        def _():
            rz_copy(k, s, 2, s).wait_recv()
            add_rows(k, s, slice(None), [rz_room(k, s, s)])
            rz_copy(k, s, s, 1).start()

    def r1(k, s):
        if (k, s) in RS_Z_FIRST:
            z_first(k, s)
        else:
            xy_first(k, s)

    def r2(k, s):
        if (k, s) in RS_Z_FIRST:
            z_second(k, s)
        else:
            xy_second(k, s)

    def rz_room(k, s, idx):
        ref = rzs[k].at[idx]
        if (k, s) in RS_Z_FIRST or not {(k, 1 - s)} & RS_Z_FIRST:
            return ref
        return rzs[k].at[idx, 0:pair]

    def rz_copy(k, s, q, idx):
        return rcopy(
            grads[k].at[s] if (k, s) in RS_Z_FIRST else grads[k].at[s, mine], rz_room(k, s, idx), rs_s.at[k, 6 + s], rs_r.at[k, 6 + idx], at_zz(q)
        )

    def rz_last(k, s):
        return rz_copy(k, s, s, 2) if k in RS_DIRECT else rz_copy(k, s, 2, s)

    def r3(k, s):
        if (k, s) in RS_Z_FIRST:
            @pl.when(zz == s)
            def _():
                for idx in range(2):
                    rz_copy(k, s, s, idx).wait_recv()
                add_rows(k, s, slice(None), [rz_room(k, s, 0), rz_room(k, s, 1)])
                xy_first(k, s)
            return

        xy_sum(k, s)

        @pl.when(zz == 3)
        def _():
            rz_last(k, s).start()

        @pl.when(zz == 1 - s)
        def _():
            rz_copy(k, s, s, 0).start()

    def r3b(k, s):
        if (k, s) in RS_Z_FIRST:
            @pl.when(zz == s)
            def _():
                xy_second(k, s)
            return

        @pl.when(zz == 2)
        def _():
            if k not in RS_DIRECT:
                rz_copy(k, s, 2, s).wait_recv()
                add_rows(k, s, mine, [rz_room(k, s, s)])
            rz_copy(k, s, s, 1).start()

    def rp_copy(k):
        return rcopy(
            grads[k].at[zz, own_shard(1 - c)], rps[k], rs_s.at[k, 8], rs_r.at[k, 9], other
        )

    def keep_own(k):
        return pltpu.make_async_copy(grads[k].at[zz, own_shard(c)], g_outs[k], gout.at[k])

    def keep_got(k):
        return pltpu.make_async_copy(rps[k], g_outs[k], gout.at[k])

    def r4(k):
        came = range(3) if k in RS_DIRECT else range(2)
        for s in range(2):
            @pl.when(zz == s)
            def _(s=s):
                if (k, s) in RS_Z_FIRST:
                    xy_sum(k, s)
                    return
                for idx in came:
                    rz_copy(k, s, s, idx).wait_recv()
                add_rows(k, s, mine, [rz_room(k, s, idx) for idx in came])

        @pl.when(source)
        def _():
            rp_copy(k).start()
            keep_own(k).start()

    def rp_wait(k):
        @pl.when(jnp.logical_not(source))
        def _():
            rcopy(rps[k], rps[k], rs_s.at[k, 8], rs_r.at[k, 9], other).wait_recv()
            keep_got(k).start()

        @pl.when(source)
        def _():
            rp_copy(k).wait_send()

    def rs_drain(k):
        keep_got(k).wait()
        for s in range(2):
            @pl.when(zz == s if (k, s) in RS_Z_FIRST else zz >= 0)
            def _(s=s):
                for which in range(3):
                    rs_copy(k, s, which).wait_send()

            @pl.when((zz >= 2) | (zz == 1 - s))
            def _(s=s):
                rz_copy(k, s, s, 0).wait_send()

    def chunk(j, cc):
        return pl.ds(pl.multiple_of(j * half + cc * tile, tile), tile)

    def swap(buf, j, idx):
        return rcopy(buf.at[chunk(j, c)], buf.at[chunk(j, c)], tm_s.at[idx + j], tm_r.at[idx + j], other)

    def swap_wait(buf, j, idx):
        rcopy(buf.at[chunk(j, 1 - c)], buf.at[chunk(j, 1 - c)], tm_s.at[idx + j], tm_r.at[idx + j], other).wait_recv()

    def part(which, j, idx):
        return rcopy(st.at[which, j], rv.at[which, j], tm_s.at[idx + j], tm_r.at[idx + j], other)

    T_NRM, T_COT, T_BR, T_N2, T_MLP, T_DN2, T_DML, T_DNR = range(0, 16, 2)

    lane256 = lax.broadcasted_iota(jnp.int32, (1, 256), 1)
    head_rows = [jnp.where(lane256 // 64 == h, 1.0, 0.0).astype(f32) for h in range(3)]
    q_rows = [
        jnp.where((lane256 // 64 == h) | (lane256 == 192 + h), 1.0, 0.0).astype(f32) for h in range(3)
    ]

    def stack3(rows, masks):
        wide = rows.astype(f32)
        return jnp.concatenate([(wide * m).astype(bf16) for m in masks], axis=0)

    def fold3(stacked):
        n = stacked.shape[0] // 3
        return (
            stacked[:n] * head_rows[0] + stacked[n : 2 * n] * head_rows[1] + stacked[2 * n :] * head_rows[2]
        )

    sends = {"x": lambda: a2a_in(0, x_hbm), "cot": lambda: a2a_in(1, cot_hbm), "res": lambda: a2a_out(0, stage)}
    hops = [other, over_x, over_y, {"tp": z + 1 - 2 * lax.rem(z, 2)}, {"tp": lax.rem(z + 2, 4)}]

    def hop(i):
        return rcopy(smb, smr.at[i], sm_s.at[i], sm_r.at[i], hops[i])

    def hop_wait(i):
        hop(i).wait()
        smb[...] += smr[i]

    def a2a_start(name):
        for cp in sends[name]():
            cp.start()

    def cot_here():
        a2a_in_wait(a2a_in(1, cot_hbm))
        for j in range(2):
            swap(cot, j, T_COT).start()

    steps = {
        "p0w": p0_wait, "za": z_start, "s1": s1, "s2": s2, "r2": r2, "r3": r3, "r3b": r3b, "r4": r4, "zr2": z_relay,
        "a2a": a2a_start, "cotw": cot_here, "hs": lambda i: hop(i).start(), "hw": hop_wait,
    }

    def point(name):
        for step in PLAN.get(name, ()):
            steps[step[0]](*step[1:])

    def points(name, i, count):
        for n in range(count):
            if name + str(n) in PLAN:
                @pl.when(i == n)
                def _(n=n):
                    point(name + str(n))

    def a2a_out(which, stage):
        out = []
        for dx in range(2):
            for dz in range(4):
                xx, z2_ = lax.rem(x + dx, 2), lax.rem(z + dz, 4)
                src = stage.at[pl.ds(pl.multiple_of(xx * tile + z2_ * own_tok, own_tok), own_tok)]
                dst = (res_o, ing_o)[which].at[my_seq]
                idx = dx * 4 + dz
                if idx == 0:
                    out.append(pltpu.make_async_copy(src, dst, aout_r.at[which, 0]))
                else:
                    out.append(
                        rcopy(src, dst, aout_s.at[which, idx], aout_r.at[which, idx], {"xo": xx, "tp": z2_})
                    )
        return out

    def weights_in():
        return [
            pltpu.make_async_copy(src, dst, loc.at[4 + i])
            for i, (src, dst) in enumerate(((wq_hbm, wq), (ws_hbm, ws), (wo_hbm, wo)))
        ]

    def vectors_in():
        return [
            pltpu.make_async_copy(src, dst, loc.at[7 + i])
            for i, (src, dst) in enumerate(zip((n1g, n1b, ob, n2g, n2b, f2b), vecs))
        ]

    def bias_copies(s, dz):
        dev = {"tp": lax.rem(z + dz, 4)}
        return [
            rcopy(src, buf, bias_s.at[i, dz], bias_r.at[i, s], dev)
            for i, (src, buf) in enumerate(((f1b, fbs[s]), (qvb, qvbb.at[s])))
        ]

    def bias_own(s):
        return [
            pltpu.make_async_copy(src, buf, bias_s.at[i, 0])
            for i, (src, buf) in enumerate(((f1b, fbs[s]), (qvb, qvbb.at[s])))
        ]

    for cp in weights_in():
        cp.start()
    for cp in vectors_in():
        cp.start()
    for k in (CH_1, CH_2):
        p0_start(k)

    def place(rows, cols, first):
        i = lax.broadcasted_iota(jnp.int32, (rows, cols), 0)
        j = lax.broadcasted_iota(jnp.int32, (rows, cols), 1)
        return jnp.where(j == i + first, 1.0, 0.0).astype(bf16)

    for cp in weights_in():
        cp.wait()
    head_cols = wq.shape[2]
    packed = dot(ws[...], place(ws.shape[0], 640, 3 * head_cols), 0, 0)
    for i in range(3):
        packed = packed + dot(wq[i], place(head_cols, 640, i * head_cols), 1, 0)
    pa[...] = packed.astype(bf16)
    pb[...] = dot(wo[...], place(head_cols, 256, 0), 1, 0).astype(bf16)
    for k in (CH_A, CH_B):
        p0_start(k)
    point("front")
    sel_copies = []
    for dx in range(2):
        for dc in range(2):
            idx = dx * 2 + dc
            xx, cc = lax.rem(x + dx, 2), lax.rem(c + dc, 2)
            src, dst = sel_hbm, selraw.at[x * 2 + c]
            if idx == 0:
                sel_copies.append(pltpu.make_async_copy(src, dst, sel_r.at[0]))
            else:
                sel_copies.append(
                    rcopy(src, dst, sel_s.at[idx], sel_r.at[idx], {"xo": xx, "team": cc})
                )
    for cp in sel_copies:
        cp.start()

    for s in range(2):
        @pl.when(zz == s)
        def _(s=s):
            for dz in range(1, 4):
                for cp in bias_copies(s, dz):
                    cp.start()
            for cp in bias_own(s):
                cp.start()

    zero_k = jnp.zeros((own_tok, 256), bf16)
    for ref in (kb, vb):
        for slot in range(2):
            ref[slot, 0:own_tok, :] = zero_k
            ref[slot, seq + own_tok : seq + 2 * own_tok, :] = zero_k
    smb[...] = jnp.zeros_like(smb)
    for cp in vectors_in():
        cp.wait()
    point("x_wait")
    a2a_in_wait(a2a_in(0, x_hbm))

    def natural(i):
        return pl.multiple_of((i // 4) * half + c * tile + (i % 4) * own_tok, own_tok)

    def ln1_body(i, carry):
        rows = xin[pl.ds(pl.multiple_of(i * own_tok, own_tok), own_tok), :].astype(f32)
        unit, _ = ln_parts(rows)
        nrm[pl.ds(natural(i), own_tok), :] = (unit * vec(0) + vec(1)).astype(bf16)
        return carry

    point("ln1")
    lax.fori_loop(0, 8, ln1_body, 0)
    for j in range(2):
        swap(nrm, j, T_NRM).start()

    for cp in sel_copies:
        cp.wait()
    lane_seq = lax.broadcasted_iota(jnp.int32, selraw.shape[1:], 2)
    sub = lax.broadcasted_iota(jnp.int32, (SEL, 256), 0)
    lane = lax.broadcasted_iota(jnp.int32, (SEL, 256), 1)
    inner = (lane % KB).astype(f32)
    for g in range(4):
        chosen = jnp.sum(jnp.where(lane_seq == my_seq, selraw[g].astype(f32), 0.0), axis=2, keepdims=True)
        every = jnp.zeros((1, 256), f32)
        for b in range(4):
            keys = jnp.broadcast_to(chosen[b], (SEL, 256)) * KB + inner
            here = jnp.sum(jnp.where(lane // KB == sub + 192 // KB, keys, 0.0), axis=0, keepdims=True)
            selb[g, b : b + 1, :] = here.astype(jnp.int32)
            every = every + jnp.sum(
                jnp.where(lane // KB == sub + b * SEL, keys, 0.0), axis=0, keepdims=True
            )
        selb[g, 4:5, :] = every.astype(jnp.int32)

    for s in range(2):
        @pl.when(zz != s)
        def _(s=s):
            for cp in bias_copies(s, 1):
                cp.wait_recv()

        @pl.when(zz == s)
        def _(s=s):
            for cp in bias_own(s):
                cp.wait()

    point("nrm_wait")
    for j in range(2):
        swap_wait(nrm, j, T_NRM)
    for s in range(2):
        s3(CH_A, s)

    gate_lane = (lane256 >= 192) & (lane256 < 195)

    gap = jnp.zeros((1, 640 - 3 * head_cols), f32)
    none = jnp.zeros((1, head_cols), f32)
    mix_bias = [
        jnp.concatenate([qvbb[slot, 0:1, :], none, qvbb[slot, 1:2, :], gap], axis=1) for slot in range(2)
    ]

    def qkv_body(i, carry):
        points("qkv", i, 4)
        at = pl.ds(pl.multiple_of(i * tile, tile), tile)
        padded = pl.ds(pl.multiple_of(i * tile + own_tok, own_tok), tile)
        rows = nrm[at, :]
        for slot in range(2):
            mixed = dot(rows, wa[slot], 1, 0)
            scr[slot, at, :] = mixed[:, 512:640]
            mixed = mixed + mix_bias[slot]
            q = mixed[:, 0:256].astype(bf16).astype(f32) * 0.125
            q = jnp.where(lane256 < 192, q, jnp.where(gate_lane, 1.0, 0.0))
            qb[slot, at, :] = q.astype(bf16)
            keys = pltpu.roll(mixed[:, 128:384], 192, 1)
            score = mixed[:, 512:640]
            gate = -(jnp.maximum(-score, 0.0) + jnp.log(1.0 + jnp.exp(-jnp.abs(score))))
            gate = jnp.concatenate([gate, gate], axis=1)
            keys = jnp.where(lane256 < 192, keys, jnp.where(gate_lane, gate, 0.0))
            kb[slot, padded, :] = keys.astype(bf16)
            vb[slot, padded, :] = jnp.where(lane256 < 192, mixed[:, 384:640], 0.0).astype(bf16)
        return carry

    lax.fori_loop(0, 4, qkv_body, 0)

    key_iota = lax.broadcasted_iota(jnp.int32, (seq, 256), 0)

    def one_hot(g):
        return jnp.where(key_iota == selb[g, 4:5, :], 1.0, 0.0).astype(bf16)

    def gather_body(g, carry):
        points("gat", g, 4)
        hot = one_hot(g)
        at = pl.ds(pl.multiple_of(g * 256, 256), 256)
        for slot in range(2):
            ksel[slot, at, :] = dot(hot, kb[slot, own_tok : own_tok + seq, :], 0, 0).astype(bf16)
            vsel[slot, at, :] = dot(hot, vb[slot, own_tok : own_tok + seq, :], 0, 0).astype(bf16)
        return carry

    lax.fori_loop(0, 4, gather_body, 0)

    prefix_end = pref[my_seq]

    def windows(b, slot):
        near = pl.ds(pl.multiple_of(b * 64, 64), 192)
        at = pl.ds(pl.multiple_of(b * 64, 64), 64)
        keys = jnp.concatenate([kb[slot, near, :], ksel[slot, at, :]], axis=0)
        vals = jnp.concatenate([vb[slot, near, :], vsel[slot, at, :]], axis=0)
        return at, near, keys, vals

    def fwd_body(b, carry):
        points("fwd", b, 16)
        picks = selb[b // 4, pl.ds(b % 4, 1), :]
        key_pos = jnp.where(lane256 < 192, (b - 1) * 64 + lane256, picks)
        query_pos = b * 64 + lax.broadcasted_iota(jnp.int32, (64, 256), 0)
        key_pos = jnp.broadcast_to(key_pos, (64, 256))
        inside = (key_pos >= 0) & (key_pos < seq)
        permitted = (key_pos <= query_pos) | ((query_pos < prefix_end) & (key_pos < prefix_end))
        near_by = jnp.abs(query_pos - key_pos) < 64
        is_near = jnp.broadcast_to(lane256 < 192, (64, 256))
        allowed = inside & permitted & (near_by == is_near)
        fill = jnp.where(allowed, 0.0, MASKED)
        for slot in range(2):
            at, near, keys, vals = windows(b, slot)
            stacked = stack3(qb[slot, at, :], q_rows)
            logits = dot(stacked, keys, 1, 1).reshape(3, 64, 256) + fill[None]
            top = jnp.max(logits, axis=-1, keepdims=True)
            p = jnp.exp(logits - top)
            p = p * (1.0 / jnp.sum(p, axis=-1, keepdims=True))
            p = p.reshape(192, 256).astype(bf16)
            pr[b * 2 + slot] = p
            att[slot, at, :] = fold3(dot(p, vals, 1, 0)).astype(bf16)
        return carry

    lax.fori_loop(0, 16, fwd_body, 0)

    point("brs")
    for s in range(2):
        s3(CH_B, s)

    def branch_tile(rows):
        return dot(att[0, rows, :], wb[0], 1, 1) + dot(att[1, rows, :], wb[1], 1, 1)

    for j in range(2):
        st[0, j] = branch_tile(chunk(j, 1 - c)).astype(bf16)
        part(0, j, T_BR).start()
    for j in range(2):
        point("br" + str(j))
        own = branch_tile(chunk(j, c))
        at = slice(j * tile, (j + 1) * tile)
        part(0, j, T_BR).wait_recv()
        mid[at, :] = (
            xin[at, :].astype(f32) + own + rv[0, j].astype(f32) + vec(2)
        )

        def ln2_body(i, carry, j=j):
            rows = mid[pl.ds(pl.multiple_of(j * tile + i * own_tok, own_tok), own_tok), :]
            unit, _ = ln_parts(rows)
            n2[pl.ds(natural(j * 4 + i), own_tok), :] = (unit * vec(3) + vec(4)).astype(bf16)
            return carry

        lax.fori_loop(0, 4, ln2_body, 0)
        swap(n2, j, T_N2).start()

    point("mlpa0")
    for k in (CH_1, CH_2):
        s3(k, 0)
    for j in range(2):
        swap_wait(cot, j, T_COT)
        part(0, j, T_BR).wait_send()
        swap_wait(n2, j, T_N2)

    def mlp_tile(rows, slot):
        before = dot(n2[rows, :], w1[slot], 1, 0) + fbs[slot][...].reshape(1, width)
        d_act = dot(cot[rows, :], w2[slot], 1, 0)
        square = before * before
        t = jnp.tanh(0.7978845608028654 * before * (1.0 + 0.044715 * square))
        gate = 0.5 * (1.0 + t)
        slope = gate + 0.5 * before * (1.0 - t * t) * (
            0.7978845608028654 * (1.0 + 0.134145 * square)
        )
        low = (before * gate).astype(bf16)
        low_back = (d_act * slope).astype(bf16)
        act[slot, rows, :] = low
        dbf[slot, rows, :] = low_back
        smb[pl.ds(8 + slot + c * (3 - 2 * slot), 1), :] += jnp.sum(
            low_back.astype(f32), axis=0, keepdims=True
        )
        return dot(low, w2[slot], 1, 1), dot(low_back, w1[slot], 1, 1)

    def first_mlp(i, carry):
        @pl.when(i > 0)
        def _():
            points("mlpa", i, 4)

        at = pl.ds(pl.multiple_of(i * tile, tile), tile)
        out, back = mlp_tile(at, 0)
        acc[0, at, :] = out
        acc[1, at, :] = back
        return carry

    lax.fori_loop(0, 4, first_mlp, 0)

    def weight_grad(g, slot, left, right):
        def body(m, carry):
            at = pl.ds(pl.multiple_of(m * 256, 256), 256)
            g[slot, at, :] = dot(left[:, at], right, 0, 0).astype(bf16)
            return carry

        lax.fori_loop(0, 3, body, 0)

    def ff_grads(slot):
        for k, name, left, right in ((CH_2, "g2", cot, act), (CH_1, "g1", n2, dbf)):
            point(name + str(slot))
            ag_drain(k, slot)
            weight_grad(grads[k], slot, left, right[slot])
            r1(k, slot)

    def peer_mlp(j, carry):
        @pl.when(j == 1)
        def _():
            point("pm1")

        rows = chunk(j, 1 - c)
        out, back = mlp_tile(rows, 1)
        st[0, j] = (acc[0, rows, :] + out).astype(bf16)
        st[1, j] = (acc[1, rows, :] + back).astype(bf16)
        part(0, j, T_MLP).start()
        part(1, j, T_DN2).start()
        return carry

    if not PEER_FIRST:
        ff_grads(0)
    point("pm0")
    for k in (CH_1, CH_2):
        s3(k, 1)
    lax.fori_loop(0, 2, peer_mlp, 0)
    if PEER_FIRST:
        ff_grads(0)

    def own_mlp(j, carry):
        points("om", j, 2)
        rows = chunk(j, c)
        out, back = mlp_tile(rows, 1)
        out = acc[0, rows, :] + out
        back = acc[1, rows, :] + back
        at = pl.ds(pl.multiple_of(j * tile, tile), tile)
        part(0, j, T_MLP).wait_recv()
        part(1, j, T_DN2).wait_recv()
        stage[at, :] = (mid[at, :] + out + rv[0, j].astype(f32) + vec(5)).astype(bf16)
        dnr[...] = back + rv[1, j].astype(f32)

        def ln2_back(i, carry):
            here = pl.ds(pl.multiple_of(j * tile + i * own_tok, own_tok), own_tok)
            nat = pl.ds(natural(j * 4 + i), own_tok)
            unit, inverse = ln_parts(mid[here, :])
            up_grad = dnr[pl.ds(pl.multiple_of(i * own_tok, own_tok), own_tok), :]
            grad_rows = cot[nat, :].astype(f32)
            d_mid = grad_rows + ln_back(up_grad, unit, inverse, vec(3))
            mid[here, :] = d_mid
            dml[nat, :] = d_mid.astype(bf16)
            smb[2:3, :] += jnp.sum(d_mid, axis=0, keepdims=True)
            smb[3:4, :] += jnp.sum(up_grad * unit, axis=0, keepdims=True)
            smb[4:5, :] += jnp.sum(up_grad, axis=0, keepdims=True)
            smb[5:6, :] += jnp.sum(grad_rows, axis=0, keepdims=True)
            return carry

        lax.fori_loop(0, 4, ln2_back, 0)
        swap(dml, j, T_DML).start()
        return carry

    lax.fori_loop(0, 2, own_mlp, 0)

    if not FF_GRADS_LATER:
        ff_grads(1)
    point("datt")
    for j in range(2):
        swap_wait(dml, j, T_DML)

    def datt_body(i, carry):
        at = pl.ds(pl.multiple_of(i * tile, tile), tile)
        for slot in range(2):
            datt[slot, at, :] = dot(dml[at, :], wb[slot], 1, 0).astype(bf16)
        return carry

    lax.fori_loop(0, 4, datt_body, 0)
    for slot in range(2):
        point("gb" + str(slot))
        ag_drain(CH_B, slot)
        weight_grad(wb, slot, dml, att[slot])
        r1(CH_B, slot)
    if FF_GRADS_LATER:
        ff_grads(1)
    acc[:, :, 0:512] = jnp.zeros((2, seq + 2 * own_tok, 512), f32)

    def bwd_body(b, carry):
        points("bwd", b, 16)
        for slot in range(2):
            at, near, keys, vals = windows(b, slot)
            q_stack = stack3(qb[slot, at, :], q_rows)
            d_stack = stack3(datt[slot, at, :], head_rows)
            p_low = pr[b * 2 + slot]
            p = p_low.astype(f32)
            pdp = p * dot(d_stack, vals, 1, 1)
            dl = (pdp - p * jnp.sum(pdp, axis=-1, keepdims=True)).astype(bf16)
            dbf[slot, at, 512:768] = (fold3(dot(dl, keys, 1, 0)) * 0.125).astype(bf16)
            dk = dot(dl, q_stack, 0, 0)
            dv = dot(p_low, d_stack, 0, 0)
            side = slice(slot * 256, slot * 256 + 256)
            acc[0, near, side] += dk[0:192]
            acc[1, near, side] += dv[0:192]
            dbf[slot, at, 0:256] = dk[192:256].astype(bf16)
            dbf[slot, at, 256:512] = dv[192:256].astype(bf16)
        return carry

    lax.fori_loop(0, 16, bwd_body, 0)
    point("mix")

    sel_pos = jnp.concatenate([selb[g, 4:5, :] for g in range(4)], axis=1)

    def mix_body(i, carry):
        at = pl.ds(pl.multiple_of(i * tile, tile), tile)
        padded = pl.ds(pl.multiple_of(i * tile + own_tok, own_tok), tile)
        key_at = i * tile + lax.broadcasted_iota(jnp.int32, (tile, seq), 0)
        hot = jnp.where(key_at == sel_pos, 1.0, 0.0).astype(bf16)
        for slot in range(2):
            far = dot(hot, dbf[slot, :, 0:512], 1, 0)
            dk = (acc[0, padded, slot * 256 : slot * 256 + 256] + far[:, 0:256]).astype(bf16).astype(f32)
            dv = (acc[1, padded, slot * 256 : slot * 256 + 256] + far[:, 256:512]).astype(bf16).astype(f32)
            dq = dbf[slot, at, 512:768].astype(f32)
            turned = pltpu.roll(dk, 64, 1)
            d_score = dk[:, 128:256] / (1.0 + jnp.exp(scr[slot, at, :]))
            lane128 = lane256[:, 0:128]
            v1 = jnp.where(lane128 < 64, dq[:, 128:256], turned[:, 0:128])
            v4 = jnp.where(lane128 < 64, dv[:, 128:256], jnp.where(lane128 < 67, d_score, 0.0))
            mix = jnp.concatenate([dq[:, 0:128], v1, turned[:, 128:256], dv[:, 0:128], v4], axis=1)
            mix = mix.astype(bf16)
            act[slot, at, 0:640] = mix
            smb[pl.ds(12 + slot + c * (3 - 2 * slot), 1), 0:640] += jnp.sum(
                mix.astype(f32), axis=0, keepdims=True
            )
        return carry

    lax.fori_loop(0, 4, mix_body, 0)
    def qkv_grads():
        for slot in range(2):
            point("ga" + str(slot))
            weight_grad(ga, slot, nrm, act[slot, :, 0:640])
            r1(CH_A, slot)

    if not QKV_GRADS_LAST:
        qkv_grads()
    point("dn0")
    for j in range(2):
        part(0, j, T_MLP).wait_send()
        part(1, j, T_DN2).wait_send()

    def dnorm_tile(rows):
        return dot(act[0, rows, 0:640], wa[0], 1, 1) + dot(act[1, rows, 0:640], wa[1], 1, 1)

    for j in range(2):
        st[0, j] = dnorm_tile(chunk(j, 1 - c)).astype(bf16)
        part(0, j, T_DNR).start()

    res_copies = a2a_out(0, stage)
    res_copies[0].wait()
    for cp in res_copies[1:]:
        cp.wait_send()

    def own_dnorm(j, carry):
        points("od", j, 2)
        dnr[...] = dnorm_tile(chunk(j, c))
        part(0, j, T_DNR).wait_recv()

        def ln1_back(i, carry):
            here = pl.ds(pl.multiple_of(j * tile + i * own_tok, own_tok), own_tok)
            local = pl.ds(pl.multiple_of(i * own_tok, own_tok), own_tok)
            unit, inverse = ln_parts(xin[here, :].astype(f32))
            up_grad = dnr[local, :] + rv[0, j, local, :].astype(f32)
            grad = mid[here, :] + ln_back(up_grad, unit, inverse, vec(0))
            stage[here, :] = grad.astype(bf16)
            smb[0:1, :] += jnp.sum(up_grad * unit, axis=0, keepdims=True)
            smb[1:2, :] += jnp.sum(up_grad, axis=0, keepdims=True)
            return carry

        lax.fori_loop(0, 4, ln1_back, 0)
        return carry

    lax.fori_loop(0, 2, own_dnorm, 0)
    ing_copies = a2a_out(1, stage)
    for cp in ing_copies:
        cp.start()
    if QKV_GRADS_LAST:
        qkv_grads()
    for i in range(24):
        point("e" + str(i))

    small = pltpu.make_async_copy(smb, sm_o, gout.at[4])
    small.start()
    for k in (CH_2, CH_1, CH_B, CH_A):
        rp_wait(k)
    for s in range(2):
        ag_drain(CH_A, s)
    for k in range(4):
        rs_drain(k)
    small.wait()
    for j in range(2):
        for buf, idx in ((nrm, T_NRM), (cot, T_COT), (n2, T_N2), (dml, T_DML)):
            swap(buf, j, idx).wait_send()
        part(0, j, T_DNR).wait_send()

    for s in range(2):
        @pl.when(zz == s)
        def _(s=s):
            for dz in range(1, 4):
                for cp in bias_copies(s, dz):
                    cp.wait_send()

    for cp in res_copies[1:]:
        cp.wait_recv()
    for cp in ing_copies:
        cp.wait()


def finish_kernel(
    res_i, ing_i, ga_i, gb_i, g1_i, g2_i, sm_i,
    res_o, ing_o, n1g, n1b, wq_o, qvb, ws_o, wo_o, ob, n2g, n2b, g1_o, f1b, g2_o, f2b,
    res, ing, sem,
):
    def moves(way, i):
        return [
            pltpu.make_async_copy(*((a, b) if way == 0 else (b, d)), sem.at[way, n, i])
            for n, (a, b, d) in enumerate(
                (r.at[i] for r in refs) for refs in ((res_i, res, res_o), (ing_i, ing, ing_o))
            )
        ]

    seqs = res.shape[0]
    for i in range(seqs):
        for cp in moves(0, i):
            cp.start()
    for i in range(seqs):
        for come, go in zip(moves(0, i), moves(1, i)):
            come.wait()
            go.start()
    z = lax.axis_index("tp")
    for row, ref in enumerate((n1g, n1b, ob, n2g, n2b, f2b)):
        ref[...] = sm_i[row, :]
    f1b[...] = sm_i[pl.ds(8 + z, 1), :][0]
    cols = wo_o.shape[1]
    mixed = sm_i[pl.ds(12 + z, 1), :]
    qvb[0:1, :] = mixed[:, 0:cols]
    qvb[1:2, :] = mixed[:, 2 * cols : 3 * cols]
    g1_o[...] = g1_i[...].astype(f32)
    g2_o[...] = g2_i[...].astype(f32)
    wo_o[...] = gb_i[:, 0:cols].astype(f32)
    i = lax.broadcasted_iota(jnp.int32, (640, cols), 0)
    j = lax.broadcasted_iota(jnp.int32, (640, cols), 1)
    for part in range(3):
        wq_o[part] = dot(ga_i[...], jnp.where(i == j + part * cols, 1.0, 0.0).astype(bf16), 1, 0)
    heads = ws_o.shape[0]
    i = lax.broadcasted_iota(jnp.int32, (heads, 640), 0)
    j = lax.broadcasted_iota(jnp.int32, (heads, 640), 1)
    ws_o[...] = dot(jnp.where(j == i + 3 * cols, 1.0, 0.0).astype(bf16), ga_i[...], 1, 1)
    for i in range(seqs):
        for cp in moves(1, i):
            cp.wait()


def fast_layer(
    inputs, norm1_gain, norm1_bias, qkv_weight, qv_bias, score_weight, out_weight, out_bias,
    norm2_gain, norm2_bias, fc1_weight, fc1_bias, fc2_weight, fc2_bias, prefix, selected, cotangent,
):
    shard, _, cols = qkv_weight.shape
    heads = score_weight.shape[1]
    width = inputs.shape[2]
    own_tok = inputs.shape[1]
    seqs = inputs.shape[0]
    seq = 16 * own_tok
    vm = pltpu.VMEM
    ncols = (640, 256, 768, 768)
    hbm = pl.BlockSpec(memory_space=pl.ANY)
    vmem = pl.BlockSpec(memory_space=pltpu.VMEM)
    dma = pltpu.SemaphoreType.DMA
    outs = pl.pallas_call(
        layer_kernel,
        out_shape=[
            jax.ShapeDtypeStruct(inputs.shape, bf16),
            jax.ShapeDtypeStruct(inputs.shape, bf16),
        ]
        + [jax.ShapeDtypeStruct((shard, n), bf16) for n in ncols]
        + [jax.ShapeDtypeStruct((16, width), f32)],
        in_specs=[hbm] * 16 + [pl.BlockSpec(memory_space=pltpu.SMEM)],
        out_specs=[hbm] * 7,
        scratch_shapes=[vm((2, 768, n), bf16) for n in ncols]
        + [vm((2, 768, 640), bf16)]
        + [vm((6, 2 * shard, n), bf16) for n in ncols]
        + [vm((2, 768 if {(k, 0), (k, 1)} & RS_Z_FIRST else 2 * shard, n), bf16) for k, n in enumerate(ncols)]
        + [vm((shard, n), bf16) for n in ncols]
        + [
            vm((seq // 2, width), bf16),
            vm((seq, width), bf16),
            vm((seq, width), bf16),
            vm((2, seq, 256), bf16),
            vm((2, seq + 2 * own_tok, 256), bf16),
            vm((2, seq + 2 * own_tok, 256), bf16),
            vm((2, seq, 256), bf16),
            vm((2, seq, 256), bf16),
            vm((32, 192, 256), bf16),
            vm((2, seq, 256), bf16),
            vm((seq // 2, width), f32),
            vm((seq, width), bf16),
            vm((2, seq, 768), bf16),
            vm((2, seq, 768), bf16),
            vm((2, 2, seq // 4, width), bf16),
            vm((2, 2, seq // 4, width), bf16),
            vm((seq // 4, width), f32),
            vm((seq, width), bf16),
            vm((2, seq, 256), bf16),
            vm((2, seq + 2 * own_tok, 768), f32),
            vm((2, seq, 128), f32),
            vm((seq // 2, width), bf16),
            vm((4, 4, 4, seqs), jnp.int32),
            vm((4, 8, 256), jnp.int32),
            vm((3, shard, cols), bf16),
            vm((heads, shard), bf16),
            vm((shard, cols), bf16),
            vm((shard, 640), bf16),
            vm((shard, 256), bf16),
        ]
        + [vm((width,), f32)] * 8
        + [
            vm((2, 2, cols), f32),
            vm((16, 768), f32),
            vm((5, 16, 768), f32),
            dma((2, 8)), dma((2, 8)), dma((2, 8)), dma((2, 8)),
            dma((4, 12)), dma((4, 9)), dma((4, 9)), dma((4, 10)),
            dma((16,)), dma((16,)), dma((4,)), dma((4,)), dma((2, 4)), dma((2, 2)),
            dma((5,)), dma((5,)), dma((13,)), dma((5,)),
        ],
        compiler_params=pltpu.CompilerParams(
            collective_id=0, has_side_effects=True, vmem_limit_bytes=67043328
        ),
    )(
        inputs, cotangent, jnp.transpose(qkv_weight, (1, 0, 2)), jnp.transpose(score_weight), out_weight,
        fc1_weight, fc2_weight, jnp.transpose(selected, (1, 2, 0)), norm1_gain, norm1_bias,
        out_bias, norm2_gain, norm2_bias, fc2_bias, fc1_bias, qv_bias, prefix,
    )
    line = jax.ShapeDtypeStruct((width,), f32)
    square = jax.ShapeDtypeStruct((shard, 768), f32)
    done = pl.pallas_call(
        finish_kernel,
        out_shape=[
            jax.ShapeDtypeStruct(inputs.shape, bf16), jax.ShapeDtypeStruct(inputs.shape, bf16), line, line,
            jax.ShapeDtypeStruct((3, shard, cols), f32), jax.ShapeDtypeStruct((2, cols), f32),
            jax.ShapeDtypeStruct((heads, shard), f32), jax.ShapeDtypeStruct((shard, cols), f32),
            line, line, line, square, line, square, line,
        ],
        in_specs=[hbm, hbm] + [vmem] * 5,
        out_specs=[hbm, hbm] + [vmem] * 13,
        scratch_shapes=[vm(inputs.shape, bf16), vm(inputs.shape, bf16), dma((2, 2, seqs))],
    )(*outs)
    done = list(done)
    done[4] = jnp.transpose(done[4], (1, 0, 2))
    done[6] = jnp.transpose(done[6])
    return tuple(done)


def general(mesh):
    placed = (
        P("fsdp", ("ctx", "tp"), None),
        P(),
        P(),
        P(("fsdp", "ctx"), None, "tp"),
        P(None, "tp"),
        P(("fsdp", "ctx"), "tp"),
        P(("fsdp", "ctx"), "tp"),
        P(),
        P(),
        P(),
        P(("fsdp", "ctx"), "tp"),
        P("tp"),
        P(("fsdp", "ctx"), "tp"),
        P(),
        P("fsdp"),
        P("fsdp", "ctx", None),
        P("fsdp", ("ctx", "tp"), None),
    )
    return jax.shard_map(
        shards,
        mesh=mesh,
        in_specs=placed,
        out_specs=(
            P("fsdp", ("ctx", "tp"), None),
            P("fsdp", ("ctx", "tp"), None),
            P(),
            P(),
            P(("fsdp", "ctx"), None, "tp"),
            P(None, "tp"),
            P(("fsdp", "ctx"), "tp"),
            P(("fsdp", "ctx"), "tp"),
            P(),
            P(),
            P(),
            P(("fsdp", "ctx"), "tp"),
            P("tp"),
            P(("fsdp", "ctx"), "tp"),
            P(),
        ),
        check_vma=False,
    )


def solution(mesh):
    shape = dict(mesh.shape)
    if shape != {"fsdp": 2, "ctx": 4, "tp": 4}:
        return general(mesh)
    split = Mesh(mesh.devices.reshape(2, 2, 2, 4), ("fsdp", "xo", "team", "tp"))
    ctx = ("xo", "team")
    rows = ("fsdp", "xo", "team")
    tokens = P("fsdp", ("xo", "team", "tp"), None)
    placed = (
        tokens, P(), P(), P(rows, None, "tp"), P(None, "tp"), P(rows, "tp"), P(rows, "tp"), P(), P(), P(),
        P(rows, "tp"), P("tp"), P(rows, "tp"), P(), P("fsdp"), P("fsdp", ctx, None), tokens,
    )
    given = (
        tokens, tokens, P(), P(), P(rows, None, "tp"), P(None, "tp"), P(rows, "tp"), P(rows, "tp"),
        P(), P(), P(), P(rows, "tp"), P("tp"), P(rows, "tp"), P(),
    )
    return jax.shard_map(fast_layer, mesh=split, in_specs=placed, out_specs=given, check_vma=False)
```

```python
from functools import partial

import jax
import jax.numpy as jnp
from jax import lax
from jax.experimental import pallas as pl
from jax.experimental.pallas import tpu as pltpu
from jax.sharding import Mesh
from jax.sharding import PartitionSpec as P

HD = 64
QB = 64
KB = 16
SEL = 4
WIN = 64
SEQ_MB = 4
MICRO = 2


epsilon = 1e-05
negative_fill = -1e30


def contract(left, right, left_dim, right_dim):
    return lax.dot_general(
        left, right, (((left_dim,), (right_dim,)), ((), ())), preferred_element_type=jnp.float32
    )


def rounded(values):
    return values.astype(jnp.bfloat16)


def norm_rows(values, gain, shift):
    centred = values - jnp.mean(values, axis=-1, keepdims=True)
    inverse = lax.rsqrt(jnp.mean(centred * centred, axis=-1, keepdims=True) + epsilon)
    unit_rows = centred * inverse
    return (unit_rows * gain + shift, unit_rows, inverse)


def norm_back(upstream, unit_rows, inverse, gain):
    scaled = upstream * gain
    centred = scaled - jnp.mean(scaled, axis=-1, keepdims=True)
    return inverse * (centred - unit_rows * jnp.mean(scaled * unit_rows, axis=-1, keepdims=True))


def pick_rows(source, key_picks):
    return jax.vmap(lambda table_in, places: table_in[places])(source, key_picks)


def shards(
    inputs,
    norm1_gain,
    norm1_bias,
    qkv_weight,
    qv_bias,
    score_weight,
    out_weight,
    out_bias,
    norm2_gain,
    norm2_bias,
    fc1_weight,
    fc1_bias,
    fc2_weight,
    fc2_bias,
    prefix,
    selected,
    cotangent,
):
    all_seqs, own_tok, width_full = inputs.shape
    ctx_tok = own_tok * lax.axis_size("tp")
    heads_local = score_weight.shape[1]
    hidden_local = out_weight.shape[1]
    units_local = fc1_bias.shape[0]
    seq_full = ctx_tok * lax.axis_size("ctx")
    blocks_local = ctx_tok // QB
    near_span = QB + 2 * WIN
    chosen_span = SEL * KB
    key_count = chosen_span + near_span
    tokens = SEQ_MB * ctx_tok
    score_scale = HD ** (-0.5)
    own_start = lax.axis_index("tp") * own_tok
    block_ids = lax.axis_index("ctx") * blocks_local + jnp.arange(blocks_local, dtype=jnp.int32)
    query_pos = block_ids[:, None] * QB + jnp.arange(QB, dtype=jnp.int32)[None, :]
    near_picks = block_ids[:, None] * QB + jnp.arange(near_span, dtype=jnp.int32)[None, :]
    is_chosen = jnp.arange(key_count) < chosen_span
    qkv_offsets = jnp.stack([qv_bias[0], jnp.zeros_like(qv_bias[0]), qv_bias[1]])
    key_own = lax.axis_index("ctx") * ctx_tok + jnp.arange(ctx_tok, dtype=jnp.int32)
    every_query = jnp.arange(seq_full, dtype=jnp.int32)
    chosen_every = lax.all_gather(selected, "ctx", axis=1, tiled=True)

    def scores_of(queries, keys_near, gates_near, allowed):
        raw_scores = (
            jnp.einsum("sbqhd,sbkhd->sbhqk", queries, keys_near, preferred_element_type=jnp.float32)
            * score_scale
        )
        logits = raw_scores + jnp.transpose(gates_near, (0, 1, 3, 2))[:, :, :, None, :].astype(
            jnp.float32
        )
        return jnp.where(allowed[:, :, None], logits, negative_fill)

    def micro_step(micro_index, carried):
        big_sums, small_sums, out_buffer, grad_buffer = carried
        qkv_full, score_full, out_full, fc1_full, fc2_full = (
            lax.all_gather(qkv_weight, ("fsdp", "ctx"), axis=0, tiled=True),
            lax.all_gather(score_weight, ("fsdp", "ctx"), axis=0, tiled=True),
            lax.all_gather(out_weight, ("fsdp", "ctx"), axis=0, tiled=True),
            lax.all_gather(fc1_weight, ("fsdp", "ctx"), axis=0, tiled=True),
            lax.all_gather(fc2_weight, ("fsdp", "ctx"), axis=0, tiled=True),
        )
        seq_start = micro_index * SEQ_MB
        local_rows = lax.dynamic_slice_in_dim(inputs, seq_start, SEQ_MB, 0)
        full_rows = (
            lax.all_gather(local_rows, "tp", axis=1, tiled=True)
            .astype(jnp.float32)
            .reshape(tokens, width_full)
        )
        normed, unit_one, inverse_one = norm_rows(full_rows, norm1_gain, norm1_bias)
        normed_low = rounded(normed)
        qkv_flat = qkv_full.reshape(width_full, 3 * hidden_local)
        mixed_rows = contract(normed_low, qkv_flat, 1, 0).reshape(tokens, 3, hidden_local)
        mixed_low = rounded(mixed_rows + qkv_offsets)
        scoring = contract(normed_low, score_full, 1, 0)
        gate_low = rounded(jax.nn.log_sigmoid(scoring))
        kv_local = mixed_low[:, 1:].reshape(SEQ_MB, ctx_tok, 2 * hidden_local)
        kv_all, gate_all = (
            lax.all_gather(kv_local, "ctx", axis=1, tiled=True),
            lax.all_gather(
                gate_low.reshape(SEQ_MB, ctx_tok, heads_local), "ctx", axis=1, tiled=True
            ),
        )
        kv_padded = jnp.pad(kv_all, ((0, 0), (WIN, WIN), (0, 0)))
        gate_padded = jnp.pad(gate_all, ((0, 0), (WIN, WIN), (0, 0)))
        chosen = lax.dynamic_slice_in_dim(selected, seq_start, SEQ_MB, 0)
        chosen_picks = (chosen[..., None] * KB + jnp.arange(KB, dtype=jnp.int32) + WIN).reshape(
            SEQ_MB, blocks_local, chosen_span
        )
        key_picks = jnp.concatenate(
            [chosen_picks, jnp.broadcast_to(near_picks, (SEQ_MB, blocks_local, near_span))], axis=-1
        )
        key_pos = (key_picks - WIN)[:, :, None, :]
        query_at = query_pos[None, :, :, None]
        prefix_now = lax.dynamic_slice_in_dim(prefix, seq_start, SEQ_MB, 0)
        prefix_end = prefix_now[:, None, None, None]
        permitted = (key_pos <= query_at) | (query_at < prefix_end) & (key_pos < prefix_end)
        inside = (key_pos >= 0) & (key_pos < seq_full)
        near_by = jnp.abs(query_at - key_pos) < WIN
        allowed = inside & permitted & jnp.where(is_chosen, jnp.logical_not(near_by), near_by)
        kv_near = pick_rows(kv_padded, key_picks).reshape(
            SEQ_MB, blocks_local, key_count, 2, heads_local, HD
        )
        keys_near = kv_near[:, :, :, 0]
        values_near = kv_near[:, :, :, 1]
        gates_near = pick_rows(gate_padded, key_picks)
        queries = mixed_low[:, 0].reshape(SEQ_MB, blocks_local, QB, heads_local, HD)
        logits = scores_of(queries, keys_near, gates_near, allowed)
        row_max = jnp.max(logits, axis=-1, keepdims=True)
        log_total = row_max + jnp.log(jnp.sum(jnp.exp(logits - row_max), axis=-1, keepdims=True))
        probs_low = rounded(jnp.exp(logits - log_total))
        attended = jnp.einsum(
            "sbhqk,sbkhd->sbqhd", probs_low, values_near, preferred_element_type=jnp.float32
        )
        attended_low = rounded(attended).reshape(tokens, hidden_local)
        branch = contract(attended_low, out_full, 1, 1).reshape(SEQ_MB, ctx_tok, width_full)
        middle = (
            local_rows.astype(jnp.float32)
            + lax.psum_scatter(branch, "tp", scatter_dimension=1, tiled=True)
            + out_bias
        )
        middle_full = lax.all_gather(middle, "tp", axis=1, tiled=True).reshape(tokens, width_full)
        normed_two, unit_two, inverse_two = norm_rows(middle_full, norm2_gain, norm2_bias)
        normed_two_low = rounded(normed_two)
        before = contract(normed_two_low, fc1_full, 1, 0) + fc1_bias
        activated, gelu_back = jax.vjp(partial(jax.nn.gelu, approximate=True), before)
        activated_low = rounded(activated)
        mlp_terms = contract(activated_low, fc2_full, 1, 1).reshape(SEQ_MB, ctx_tok, width_full)
        outcome = (
            middle
            + lax.psum_scatter(
                mlp_terms.astype(jnp.bfloat16), "tp", scatter_dimension=1, tiled=True
            ).astype(jnp.float32)
            + fc2_bias
        )
        out_buffer = lax.dynamic_update_slice_in_dim(out_buffer, rounded(outcome), seq_start, 0)
        grad_local = lax.dynamic_slice_in_dim(cotangent, seq_start, SEQ_MB, 0)
        grad_low = lax.all_gather(grad_local, "tp", axis=1, tiled=True).reshape(tokens, width_full)
        grad_rows = grad_low.astype(jnp.float32)
        d_activated = contract(grad_low, fc2_full, 1, 0)
        d_before_low = rounded(gelu_back(d_activated)[0])
        fc2_step = contract(grad_low, activated_low, 0, 0)
        fc1_step = contract(normed_two_low, d_before_low, 0, 0)
        d_normed_two = lax.psum(contract(d_before_low, fc1_full, 1, 1), "tp")
        d_middle = grad_rows + norm_back(d_normed_two, unit_two, inverse_two, norm2_gain)
        d_middle_low = rounded(d_middle)
        out_step = contract(d_middle_low, attended_low, 0, 0)
        d_attended = rounded(contract(d_middle_low, out_full, 1, 0)).reshape(
            SEQ_MB, blocks_local, QB, heads_local, HD
        )
        probs_again = jnp.exp(scores_of(queries, keys_near, gates_near, allowed) - log_total)
        d_probs = jnp.einsum(
            "sbqhd,sbkhd->sbhqk", d_attended, values_near, preferred_element_type=jnp.float32
        )
        row_delta = jnp.sum(probs_again * d_probs, axis=-1, keepdims=True)
        d_logits = probs_again * (d_probs - row_delta)
        d_logits_low = rounded(d_logits)
        d_queries = (
            jnp.einsum(
                "sbhqk,sbkhd->sbqhd", d_logits_low, keys_near, preferred_element_type=jnp.float32
            )
            * score_scale
        )
        stats_local = (
            jnp.transpose(log_total, (0, 1, 3, 2, 4)).reshape(SEQ_MB, ctx_tok, heads_local),
            jnp.transpose(row_delta, (0, 1, 3, 2, 4)).reshape(SEQ_MB, ctx_tok, heads_local),
        )
        queries_flat = mixed_low[:, 0].reshape(SEQ_MB, ctx_tok, hidden_local)
        d_att_flat = d_attended.reshape(SEQ_MB, ctx_tok, hidden_local)
        queries_every, d_att_every = (
            lax.all_gather(queries_flat, "ctx", axis=1, tiled=True),
            lax.all_gather(d_att_flat, "ctx", axis=1, tiled=True),
        )
        log_every, delta_every = (
            lax.all_gather(stats_local[0], "ctx", axis=1, tiled=True),
            lax.all_gather(stats_local[1], "ctx", axis=1, tiled=True),
        )
        chosen_now = lax.dynamic_slice_in_dim(chosen_every, seq_start, SEQ_MB, 0)
        query_all = every_query[None, :, None]
        key_all = key_own[None, None, :]
        end_all = prefix_now[:, None, None]
        permitted_all = (key_all <= query_all) | (query_all < end_all) & (key_all < end_all)
        near_all = jnp.abs(query_all - key_all) < WIN
        block_hits = jnp.any(
            chosen_now[:, :, :, None] == (key_own // KB)[None, None, None, :], axis=2
        )
        member = jnp.repeat(block_hits, QB, axis=1)
        allowed_all = permitted_all & (near_all | member)
        queries_four = queries_every.reshape(SEQ_MB, seq_full, heads_local, HD)
        d_att_four = d_att_every.reshape(SEQ_MB, seq_full, heads_local, HD)
        keys_own = mixed_low[:, 1].reshape(SEQ_MB, ctx_tok, heads_local, HD)
        values_own = mixed_low[:, 2].reshape(SEQ_MB, ctx_tok, heads_local, HD)
        gates_own = gate_low.reshape(SEQ_MB, ctx_tok, heads_local)
        logits_own = (
            jnp.einsum(
                "sqhd,skhd->shqk", queries_four, keys_own, preferred_element_type=jnp.float32
            )
            * score_scale
        )
        logits_own = logits_own + jnp.transpose(gates_own, (0, 2, 1))[:, :, None, :].astype(
            jnp.float32
        )
        logits_own = jnp.where(allowed_all[:, None], logits_own, negative_fill)
        probs_own = jnp.exp(logits_own - jnp.transpose(log_every, (0, 2, 1))[..., None])
        d_probs_own = jnp.einsum(
            "sqhd,skhd->shqk", d_att_four, values_own, preferred_element_type=jnp.float32
        )
        d_logits_own = probs_own * (d_probs_own - jnp.transpose(delta_every, (0, 2, 1))[..., None])
        d_keys_own = (
            jnp.einsum(
                "shqk,sqhd->skhd",
                rounded(d_logits_own),
                queries_four,
                preferred_element_type=jnp.float32,
            )
            * score_scale
        )
        d_values_own = jnp.einsum(
            "shqk,sqhd->skhd", rounded(probs_own), d_att_four, preferred_element_type=jnp.float32
        )
        d_kv_mine = jnp.stack([d_keys_own, d_values_own], axis=2).reshape(
            SEQ_MB, ctx_tok, 2 * hidden_local
        )
        d_gate_mine = jnp.transpose(jnp.sum(d_logits_own, axis=2), (0, 2, 1))
        d_kv_low = rounded(d_kv_mine).reshape(tokens, 2, hidden_local)
        gate_grad = (
            lax.optimization_barrier(rounded(d_gate_mine))
            .astype(jnp.float32)
            .reshape(tokens, heads_local)
        )
        d_scoring_low = rounded(gate_grad * jax.nn.sigmoid(-scoring))
        d_queries_low = rounded(d_queries).reshape(tokens, 1, hidden_local)
        d_mixed = jnp.concatenate([d_queries_low, d_kv_low], axis=1).reshape(
            tokens, 3 * hidden_local
        )
        qkv_step = contract(normed_low, d_mixed, 0, 0).reshape(width_full, 3, hidden_local)
        score_step = contract(normed_low, d_scoring_low, 0, 0)
        d_normed_part = contract(d_mixed, qkv_flat, 1, 1) + contract(
            d_scoring_low, score_full, 1, 1
        )
        d_normed = lax.psum(d_normed_part.astype(jnp.bfloat16), "tp").astype(jnp.float32)
        d_inputs = (d_middle + norm_back(d_normed, unit_one, inverse_one, norm1_gain)).reshape(
            SEQ_MB, ctx_tok, width_full
        )
        d_inputs_mine = lax.dynamic_slice_in_dim(d_inputs, own_start, own_tok, 1)
        grad_buffer = lax.dynamic_update_slice_in_dim(
            grad_buffer, rounded(d_inputs_mine), seq_start, 0
        )
        small_step = (
            jnp.sum(d_normed * unit_one, axis=0),
            jnp.sum(d_normed, axis=0),
            jnp.stack(
                [
                    jnp.sum(d_queries_low[:, 0], axis=0, dtype=jnp.float32),
                    jnp.sum(d_kv_low[:, 1], axis=0, dtype=jnp.float32),
                ]
            ),
            jnp.sum(d_middle, axis=0),
            jnp.sum(d_normed_two * unit_two, axis=0),
            jnp.sum(d_normed_two, axis=0),
            jnp.sum(d_before_low, axis=0, dtype=jnp.float32),
            jnp.sum(grad_rows, axis=0),
        )
        big_step = (qkv_step, score_step, out_step, fc1_step, fc2_step)
        big_sums = jax.tree.map(jnp.add, big_sums, big_step)
        small_sums = jax.tree.map(jnp.add, small_sums, small_step)
        return (big_sums, small_sums, out_buffer, grad_buffer)

    big_init = (
        jnp.zeros((width_full, 3, hidden_local), jnp.float32),
        jnp.zeros((width_full, heads_local), jnp.float32),
        jnp.zeros((width_full, hidden_local), jnp.float32),
        jnp.zeros((width_full, units_local), jnp.float32),
        jnp.zeros((width_full, units_local), jnp.float32),
    )
    small_init = (
        jnp.zeros((width_full,), jnp.float32),
        jnp.zeros((width_full,), jnp.float32),
        jnp.zeros((2, hidden_local), jnp.float32),
        jnp.zeros((width_full,), jnp.float32),
        jnp.zeros((width_full,), jnp.float32),
        jnp.zeros((width_full,), jnp.float32),
        jnp.zeros((units_local,), jnp.float32),
        jnp.zeros((width_full,), jnp.float32),
    )
    buffer_init = jnp.zeros(inputs.shape, jnp.bfloat16)
    big_sums, small_sums, out_buffer, grad_buffer = lax.fori_loop(
        0, MICRO, micro_step, (big_init, small_init, buffer_init, buffer_init)
    )
    big_grads = (
        lax.psum_scatter(big_sums[0], ("fsdp", "ctx"), scatter_dimension=0, tiled=True),
        lax.psum_scatter(big_sums[1], ("fsdp", "ctx"), scatter_dimension=0, tiled=True),
        lax.psum_scatter(big_sums[2], ("fsdp", "ctx"), scatter_dimension=0, tiled=True),
        lax.psum_scatter(big_sums[3], ("fsdp", "ctx"), scatter_dimension=0, tiled=True),
        lax.psum_scatter(big_sums[4], ("fsdp", "ctx"), scatter_dimension=0, tiled=True),
    )
    small_grads = lax.psum(
        (
            small_sums[0],
            small_sums[1],
            small_sums[2],
            small_sums[3],
            small_sums[4],
            small_sums[5],
            small_sums[6],
            small_sums[7],
        ),
        ("fsdp", "ctx"),
    )
    return (
        out_buffer,
        grad_buffer,
        small_grads[0],
        small_grads[1],
        big_grads[0],
        small_grads[2],
        big_grads[1],
        big_grads[2],
        small_grads[3],
        small_grads[4],
        small_grads[5],
        big_grads[3],
        small_grads[6],
        big_grads[4],
        small_grads[7],
    )


EPS = 1e-05
MASKED = -1e30
MESH_ID = pl.DeviceIdType.MESH
CH_A, CH_B, CH_1, CH_2 = 0, 1, 2, 3
f32 = jnp.float32
bf16 = jnp.bfloat16


def dot(left, right, left_dim, right_dim):
    return lax.dot_general(
        left, right, (((left_dim,), (right_dim,)), ((), ())), preferred_element_type=f32
    )


def ln_parts(rows):
    centred = rows - jnp.mean(rows, axis=-1, keepdims=True)
    inverse = lax.rsqrt(jnp.mean(centred * centred, axis=-1, keepdims=True) + EPS)
    return centred * inverse, inverse


def ln_back(upstream, unit, inverse, gain):
    scaled = upstream * gain
    return inverse * (
        scaled
        - jnp.mean(scaled, axis=-1, keepdims=True)
        - unit * jnp.mean(scaled * unit, axis=-1, keepdims=True)
    )


PLAN = {
    "front": (("p0w", 0), ("za", 0, 0), ("za", 0, 1), ("p0w", 3), ("p0w", 2), ("p0w", 1), ("a2a", "x"), ("s1", 0, 1), ("za", 1, 1), ("s1", 0, 0), ("s2", 0, 1),),
    "x_wait": (("za", 1, 0), ("zr2", 0, 1),),
    "ln1": (("za", 2, 0), ("s2", 0, 0), ("za", 3, 0), ("a2a", "cot"),),
    "nrm_wait": (("zr2", 0, 0), ("s1", 1, 1),),
    "qkv0": (("s1", 1, 0),),
    "qkv2": (("s1", 2, 0),),
    "gat1": (("s2", 1, 0),),
    "fwd3": (("za", 3, 1), ("s2", 1, 1),),
    "fwd5": (("s1", 3, 0),),
    "fwd8": (("zr2", 1, 1),),
    "fwd11": (("s1", 3, 1),),
    "fwd12": (("s2", 3, 0),),
    "fwd13": (("zr2", 3, 0), ("zr2", 1, 0), ("s2", 2, 0),),
    "fwd14": (("za", 2, 1), ("cotw",),),
    "br0": (("zr2", 2, 0),),
    "br1": (("s1", 2, 1),),
    "mlpa2": (("s2", 2, 1), ("s2", 3, 1),),
    "pm0": (("zr2", 2, 1), ("zr2", 3, 1),),
    "datt": (("r2", 2, 0), ("r2", 3, 0),),
    "bwd2": (("r2", 1, 0), ("r3", 3, 0),),
    "bwd5": (("a2a", "res"),),
    "bwd9": (("r3", 2, 0),),
    "bwd11": (("r2", 1, 1),),
    "bwd12": (("r2", 3, 1),),
    "bwd14": (("r2", 2, 1), ("r3b", 3, 0),),
    "ga1": (("r3b", 2, 0), ("r3", 1, 1),),
    "dn0": (("r3", 2, 1),),
    "e0": (("r3b", 1, 1),),
    "e1": (("r3", 1, 0),),
    "e2": (("hs", 0),),
    "e3": (("hw", 0), ("hs", 1),),
    "e4": (("r3b", 1, 0),),
    "e5": (("r2", 0, 0),),
    "e6": (("r2", 0, 1),),
    "e7": (("r3b", 2, 1),),
    "e9": (("hw", 1),),
    "e11": (("hs", 2),),
    "e12": (("r3", 0, 0), ("r4", 2),),
    "e13": (("hw", 2), ("hs", 3),),
    "e14": (("r3b", 0, 0), ("r3", 0, 1), ("hw", 3),),
    "e16": (("r3b", 0, 1),),
    "e17": (("r4", 0),),
    "e18": (("r3", 3, 1),),
    "e19": (("r4", 1), ("r3b", 3, 1), ("hs", 4),),
    "e20": (("r4", 3),),
    "e22": (("hw", 4),),
}
PEER_FIRST, FF_GRADS_LATER, QKV_GRADS_LAST = False, True, False
AG_Z_LAST, RS_Z_FIRST = {(1, 0)}, {(1, 0)}
AG_DIRECT, RS_DIRECT = (), ()
AG_XLIGHT = {(2, 1), (3, 0), (0, 0), (1, 0), (1, 1)}
RS_XLIGHT = {(3, 0), (3, 1), (0, 0), (0, 1), (1, 0), (1, 1)}


def layer_kernel(
    x_hbm, cot_hbm, wq_hbm, ws_hbm, wo_hbm, f1_hbm, f2_hbm, sel_hbm, n1g, n1b, ob, n2g, n2b, f2b, f1b, qvb, pref,
    res_o, ing_o, ga_o, gb_o, g1_o, g2_o, sm_o,
    wa, wb, w1, w2, ga,
    rba, rbb, rb1, rb2, rza, rzb, rz1, rz2, rpa, rpb, rp1, rp2,
    xin, cot, nrm, qb, kb, vb, ksel, vsel, pr, att, mid, n2, act, dbf,
    st, rv, dnr, dml, datt, acc, scr, stage, selraw, selb, wq, ws, wo, pa, pb, v0, v1, v2, v3, v4, v5, fb0, fb1, qvbb, smb, smr,
    ain_s, ain_r, aout_s, aout_r, ag_s, ag_r, rs_s, rs_r, tm_s, tm_r,
    sel_s, sel_r, bias_s, bias_r, sm_s, sm_r, loc, gout,
):
    y = lax.axis_index("fsdp")
    x = lax.axis_index("xo")
    c = lax.axis_index("team")
    z = lax.axis_index("tp")
    zz = z + c * (3 - 2 * z)
    source = zz < 2
    own_tok = x_hbm.shape[1]
    width = x_hbm.shape[2]
    tile = 4 * own_tok
    half = 2 * tile
    seq = 2 * half
    my_seq = x * 4 + z
    hbms = (pa, pb, f1_hbm, f2_hbm)
    weights = (wa, wb, w1, w2)
    grads = (ga, wb, w1, w2)
    rbs = (rba, rbb, rb1, rb2)
    rzs = (rza, rzb, rz1, rz2)
    rps = (rpa, rpb, rp1, rp2)
    g_outs = (ga_o, gb_o, g1_o, g2_o)
    shard = f1_hbm.shape[0]
    pair = 2 * shard
    over_x, over_y, other = {"xo": 1 - x}, {"fsdp": 1 - y}, {"team": 1 - c}

    def block(yy, xx):
        return pl.ds(pl.multiple_of((yy * 4 + xx * 2) * shard, pair), pair)

    mine = block(y, x)
    vecs, fbs = (v0, v1, v2, v3, v4, v5), (fb0, fb1)

    def vec(i):
        return vecs[i][...].reshape(1, width)

    far_x, far_y = block(y, 1 - x), block(1 - y, x)
    far_xy = block(1 - y, 1 - x)

    def at_zz(q):
        return {"tp": q + c * (3 - 2 * q)}

    def own_shard(cc):
        return pl.ds(pl.multiple_of((y * 4 + x * 2 + cc) * shard, shard), shard)

    def rcopy(src, dst, ss, rs, dev):
        return pltpu.make_async_remote_copy(
            src_ref=src, dst_ref=dst, send_sem=ss, recv_sem=rs, device_id=dev, device_id_type=MESH_ID
        )

    bar = pltpu.get_barrier_semaphore()
    peers = []
    for dx in range(2):
        for dz in range(4):
            if dx or dz:
                peers.append({"xo": lax.rem(x + dx, 2), "tp": lax.rem(z + dz, 4)})
    peers += [other, over_y, {"xo": 1 - x, "team": 1 - c}]
    for peer in peers:
        pl.semaphore_signal(bar, 1, device_id=peer, device_id_type=MESH_ID)
    pl.semaphore_wait(bar, len(peers))

    def a2a_in(which, hbm):
        out = []
        for dx in range(2):
            for dz in range(4):
                xx, z2 = lax.rem(x + dx, 2), lax.rem(z + dz, 4)
                if which == 0:
                    at = pl.ds(pl.multiple_of(x * tile + z * own_tok, own_tok), own_tok)
                    dst = xin.at[at]
                else:
                    at = pl.ds(pl.multiple_of(x * half + c * tile + z * own_tok, own_tok), own_tok)
                    dst = cot.at[at]
                idx = dx * 4 + dz
                src = hbm.at[xx * 4 + z2]
                if idx == 0:
                    out.append(pltpu.make_async_copy(src, dst, ain_r.at[which, 0]))
                else:
                    out.append(
                        rcopy(src, dst, ain_s.at[which, idx], ain_r.at[which, idx], {"xo": xx, "tp": z2})
                    )
        return out

    def a2a_in_wait(copies):
        copies[0].wait()
        for cp in copies[1:]:
            cp.wait()

    def p0_local(k):
        return pltpu.make_async_copy(hbms[k], weights[k].at[zz, own_shard(c)], loc.at[k])

    def p0_away(k):
        return rcopy(
            hbms[k], weights[k].at[3 - zz, own_shard(c)], ag_s.at[k, 5], ag_r.at[k, 2], other
        )

    def p0_back(k):
        return rcopy(
            hbms[k], weights[k].at[zz, own_shard(1 - c)], ag_s.at[k, 5], ag_r.at[k, 2], other
        )

    def p0_start(k):
        @pl.when(source)
        def _():
            p0_local(k).start()

        @pl.when(jnp.logical_not(source))
        def _():
            p0_away(k).start()

    def p0_wait(k):
        @pl.when(source)
        def _():
            p0_local(k).wait()
            p0_back(k).wait_recv()

        @pl.when(jnp.logical_not(source))
        def _():
            p0_away(k).wait_send()

    def z_copy(k, s, q, idx):
        ref = weights[k].at[s] if (k, s) in AG_Z_LAST else weights[k].at[s, mine]
        return rcopy(ref, ref, ag_s.at[k, idx], ag_r.at[k, s], at_zz(q))

    def z_sends(k, s):
        out = [z_copy(k, s, 2, 0), z_copy(k, s, 1 - s, 1)]
        if k in AG_DIRECT:
            out.append(z_copy(k, s, 3, 2))
        return out

    def xy_start(k, s):
        for which in (0, 1) if (k, s) in AG_XLIGHT else (1, 0):
            xy(k, s, which).start()

    def z_start(k, s):
        @pl.when(zz == s)
        def _():
            if (k, s) in AG_Z_LAST:
                xy_start(k, s)
            else:
                for cp in z_sends(k, s):
                    cp.start()

    def z_relay(k, s):
        if (k, s) in AG_Z_LAST:
            @pl.when(zz == 2)
            def _():
                z_copy(k, s, 2, 0).wait_recv()
                z_copy(k, s, 3, 3 + s).start()

    def xy(k, s, which):
        light = (k, s) in AG_XLIGHT
        rows, dev = (
            (mine, over_x),
            (mine, over_y),
            (far_x, over_y) if light else (far_y, over_x),
        )[which]
        ref = weights[k].at[s, rows]
        return rcopy(ref, ref, ag_s.at[k, 6 + 3 * s + which], ag_r.at[k, 3 + 3 * s + which], dev)

    def s1(k, s):
        if (k, s) in AG_Z_LAST:
            @pl.when(zz == s)
            def _():
                xy(k, s, 0 if (k, s) in AG_XLIGHT else 1).wait_recv()
                xy(k, s, 2).start()
            return

        @pl.when(zz != s)
        def _():
            z_copy(k, s, 2, 0).wait_recv()

        if k not in AG_DIRECT:
            @pl.when(zz == 2)
            def _():
                z_copy(k, s, 3, 3 + s).start()

        xy_start(k, s)

    def s2(k, s):
        if (k, s) in AG_Z_LAST:
            @pl.when(zz == s)
            def _():
                for which in (1 if (k, s) in AG_XLIGHT else 0, 2):
                    xy(k, s, which).wait_recv()
                for cp in z_sends(k, s):
                    cp.start()
            return

        xy(k, s, 0 if (k, s) in AG_XLIGHT else 1).wait_recv()
        xy(k, s, 2).start()

    def s3(k, s):
        if (k, s) in AG_Z_LAST:
            @pl.when((zz == 1 - s) | (zz == 3))
            def _():
                z_copy(k, s, 2, 0).wait_recv()
            return

        for which in (1 if (k, s) in AG_XLIGHT else 0, 2):
            xy(k, s, which).wait_recv()

    def ag_drain(k, s):
        @pl.when(zz == s)
        def _():
            for cp in z_sends(k, s):
                cp.wait_send()

        if k not in AG_DIRECT:
            @pl.when(zz == 2)
            def _():
                z_copy(k, s, 3, 3 + s).wait_send()

        @pl.when(zz == s if (k, s) in AG_Z_LAST else zz >= 0)
        def _():
            for which in range(3):
                xy(k, s, which).wait_send()

    def rs_copy(k, s, which):
        light = (k, s) in RS_XLIGHT
        rows, dev = (
            (far_xy, over_y if light else over_x),
            (far_y, over_y) if light else (far_x, over_x),
            (far_x, over_x) if light else (far_y, over_y),
        )[which]
        i = 3 * s + which
        return rcopy(grads[k].at[s, rows], rbs[k].at[i], rs_s.at[k, i], rs_r.at[k, i], dev)

    def add_rows(k, slot, rows, bufs):
        g = grads[k]
        total = g[slot, rows, :].astype(f32)
        for buf in bufs:
            total = total + buf[...].astype(f32)
        g[slot, rows, :] = total.astype(bf16)

    def xy_first(k, s):
        for which in range(2):
            rs_copy(k, s, which).start()

    def xy_second(k, s):
        rs_copy(k, s, 0).wait_recv()
        add_rows(k, s, far_x if (k, s) in RS_XLIGHT else far_y, [rbs[k].at[3 * s]])
        rs_copy(k, s, 2).start()

    def xy_sum(k, s):
        for which in range(1, 3):
            rs_copy(k, s, which).wait_recv()
        add_rows(k, s, mine, [rbs[k].at[3 * s + 1], rbs[k].at[3 * s + 2]])

    def z_first(k, s):
        @pl.when(zz == 3)
        def _():
            rz_copy(k, s, 2, s).start()

        @pl.when(zz == 1 - s)
        def _():
            rz_copy(k, s, s, 0).start()

    def z_second(k, s):
        @pl.when(zz == 2)
        def _():
            rz_copy(k, s, 2, s).wait_recv()
            add_rows(k, s, slice(None), [rz_room(k, s, s)])
            rz_copy(k, s, s, 1).start()

    def r1(k, s):
        if (k, s) in RS_Z_FIRST:
            z_first(k, s)
        else:
            xy_first(k, s)

    def r2(k, s):
        if (k, s) in RS_Z_FIRST:
            z_second(k, s)
        else:
            xy_second(k, s)

    def rz_room(k, s, idx):
        ref = rzs[k].at[idx]
        if (k, s) in RS_Z_FIRST or not {(k, 1 - s)} & RS_Z_FIRST:
            return ref
        return rzs[k].at[idx, 0:pair]

    def rz_copy(k, s, q, idx):
        return rcopy(
            grads[k].at[s] if (k, s) in RS_Z_FIRST else grads[k].at[s, mine], rz_room(k, s, idx), rs_s.at[k, 6 + s], rs_r.at[k, 6 + idx], at_zz(q)
        )

    def rz_last(k, s):
        return rz_copy(k, s, s, 2) if k in RS_DIRECT else rz_copy(k, s, 2, s)

    def r3(k, s):
        if (k, s) in RS_Z_FIRST:
            @pl.when(zz == s)
            def _():
                for idx in range(2):
                    rz_copy(k, s, s, idx).wait_recv()
                add_rows(k, s, slice(None), [rz_room(k, s, 0), rz_room(k, s, 1)])
                xy_first(k, s)
            return

        xy_sum(k, s)

        @pl.when(zz == 3)
        def _():
            rz_last(k, s).start()

        @pl.when(zz == 1 - s)
        def _():
            rz_copy(k, s, s, 0).start()

    def r3b(k, s):
        if (k, s) in RS_Z_FIRST:
            @pl.when(zz == s)
            def _():
                xy_second(k, s)
            return

        @pl.when(zz == 2)
        def _():
            if k not in RS_DIRECT:
                rz_copy(k, s, 2, s).wait_recv()
                add_rows(k, s, mine, [rz_room(k, s, s)])
            rz_copy(k, s, s, 1).start()

    def rp_copy(k):
        return rcopy(
            grads[k].at[zz, own_shard(1 - c)], rps[k], rs_s.at[k, 8], rs_r.at[k, 9], other
        )

    def keep_own(k):
        return pltpu.make_async_copy(grads[k].at[zz, own_shard(c)], g_outs[k], gout.at[k])

    def keep_got(k):
        return pltpu.make_async_copy(rps[k], g_outs[k], gout.at[k])

    def r4(k):
        came = range(3) if k in RS_DIRECT else range(2)
        for s in range(2):
            @pl.when(zz == s)
            def _(s=s):
                if (k, s) in RS_Z_FIRST:
                    xy_sum(k, s)
                    return
                for idx in came:
                    rz_copy(k, s, s, idx).wait_recv()
                add_rows(k, s, mine, [rz_room(k, s, idx) for idx in came])

        @pl.when(source)
        def _():
            rp_copy(k).start()
            keep_own(k).start()

    def rp_wait(k):
        @pl.when(jnp.logical_not(source))
        def _():
            rcopy(rps[k], rps[k], rs_s.at[k, 8], rs_r.at[k, 9], other).wait_recv()
            keep_got(k).start()

        @pl.when(source)
        def _():
            rp_copy(k).wait_send()

    def rs_drain(k):
        keep_got(k).wait()
        for s in range(2):
            @pl.when(zz == s if (k, s) in RS_Z_FIRST else zz >= 0)
            def _(s=s):
                for which in range(3):
                    rs_copy(k, s, which).wait_send()

            @pl.when((zz >= 2) | (zz == 1 - s))
            def _(s=s):
                rz_copy(k, s, s, 0).wait_send()

    def chunk(j, cc):
        return pl.ds(pl.multiple_of(j * half + cc * tile, tile), tile)

    def swap(buf, j, idx):
        return rcopy(buf.at[chunk(j, c)], buf.at[chunk(j, c)], tm_s.at[idx + j], tm_r.at[idx + j], other)

    def swap_wait(buf, j, idx):
        rcopy(buf.at[chunk(j, 1 - c)], buf.at[chunk(j, 1 - c)], tm_s.at[idx + j], tm_r.at[idx + j], other).wait_recv()

    def part(which, j, idx):
        return rcopy(st.at[which, j], rv.at[which, j], tm_s.at[idx + j], tm_r.at[idx + j], other)

    T_NRM, T_COT, T_BR, T_N2, T_MLP, T_DN2, T_DML, T_DNR = range(0, 16, 2)

    lane256 = lax.broadcasted_iota(jnp.int32, (1, 256), 1)
    head_rows = [jnp.where(lane256 // 64 == h, 1.0, 0.0).astype(f32) for h in range(3)]
    q_rows = [
        jnp.where((lane256 // 64 == h) | (lane256 == 192 + h), 1.0, 0.0).astype(f32) for h in range(3)
    ]

    def stack3(rows, masks):
        wide = rows.astype(f32)
        return jnp.concatenate([(wide * m).astype(bf16) for m in masks], axis=0)

    def fold3(stacked):
        n = stacked.shape[0] // 3
        return (
            stacked[:n] * head_rows[0] + stacked[n : 2 * n] * head_rows[1] + stacked[2 * n :] * head_rows[2]
        )

    sends = {"x": lambda: a2a_in(0, x_hbm), "cot": lambda: a2a_in(1, cot_hbm), "res": lambda: a2a_out(0, stage)}
    hops = [other, over_x, over_y, {"tp": z + 1 - 2 * lax.rem(z, 2)}, {"tp": lax.rem(z + 2, 4)}]

    def hop(i):
        return rcopy(smb, smr.at[i], sm_s.at[i], sm_r.at[i], hops[i])

    def hop_wait(i):
        hop(i).wait()
        smb[...] += smr[i]

    def a2a_start(name):
        for cp in sends[name]():
            cp.start()

    def cot_here():
        a2a_in_wait(a2a_in(1, cot_hbm))
        for j in range(2):
            swap(cot, j, T_COT).start()

    steps = {
        "p0w": p0_wait, "za": z_start, "s1": s1, "s2": s2, "r2": r2, "r3": r3, "r3b": r3b, "r4": r4, "zr2": z_relay,
        "a2a": a2a_start, "cotw": cot_here, "hs": lambda i: hop(i).start(), "hw": hop_wait,
    }

    def point(name):
        for step in PLAN.get(name, ()):
            steps[step[0]](*step[1:])

    def points(name, i, count, first=0, step=1):
        for n in range(first, count, step):
            if name + str(n) in PLAN:
                @pl.when(i == n)
                def _(n=n):
                    point(name + str(n))

    def a2a_out(which, stage):
        out = []
        for dx in range(2):
            for dz in range(4):
                xx, z2_ = lax.rem(x + dx, 2), lax.rem(z + dz, 4)
                src = stage.at[pl.ds(pl.multiple_of(xx * tile + z2_ * own_tok, own_tok), own_tok)]
                dst = (res_o, ing_o)[which].at[my_seq]
                idx = dx * 4 + dz
                if idx == 0:
                    out.append(pltpu.make_async_copy(src, dst, aout_r.at[which, 0]))
                else:
                    out.append(
                        rcopy(src, dst, aout_s.at[which, idx], aout_r.at[which, idx], {"xo": xx, "tp": z2_})
                    )
        return out

    def weights_in():
        return [
            pltpu.make_async_copy(src, dst, loc.at[4 + i])
            for i, (src, dst) in enumerate(((wq_hbm, wq), (ws_hbm, ws), (wo_hbm, wo)))
        ]

    def vectors_in():
        return [
            pltpu.make_async_copy(src, dst, loc.at[7 + i])
            for i, (src, dst) in enumerate(zip((n1g, n1b, ob, n2g, n2b, f2b), vecs))
        ]

    def bias_copies(s, dz):
        dev = {"tp": lax.rem(z + dz, 4)}
        return [
            rcopy(src, buf, bias_s.at[i, dz], bias_r.at[i, s], dev)
            for i, (src, buf) in enumerate(((f1b, fbs[s]), (qvb, qvbb.at[s])))
        ]

    def bias_own(s):
        return [
            pltpu.make_async_copy(src, buf, bias_s.at[i, 0])
            for i, (src, buf) in enumerate(((f1b, fbs[s]), (qvb, qvbb.at[s])))
        ]

    for cp in weights_in():
        cp.start()
    for cp in vectors_in():
        cp.start()
    for k in (CH_1, CH_2):
        p0_start(k)

    def place(rows, cols, first):
        i = lax.broadcasted_iota(jnp.int32, (rows, cols), 0)
        j = lax.broadcasted_iota(jnp.int32, (rows, cols), 1)
        return jnp.where(j == i + first, 1.0, 0.0).astype(bf16)

    for cp in weights_in():
        cp.wait()
    head_cols = wq.shape[2]
    packed = dot(ws[...], place(ws.shape[0], 640, 3 * head_cols), 0, 0)
    for i in range(3):
        packed = packed + dot(wq[i], place(head_cols, 640, i * head_cols), 1, 0)
    pa[...] = packed.astype(bf16)
    pb[...] = dot(wo[...], place(head_cols, 256, 0), 1, 0).astype(bf16)
    for k in (CH_A, CH_B):
        p0_start(k)
    point("front")
    sel_copies = []
    for dx in range(2):
        for dc in range(2):
            idx = dx * 2 + dc
            xx, cc = lax.rem(x + dx, 2), lax.rem(c + dc, 2)
            src, dst = sel_hbm, selraw.at[x * 2 + c]
            if idx == 0:
                sel_copies.append(pltpu.make_async_copy(src, dst, sel_r.at[0]))
            else:
                sel_copies.append(
                    rcopy(src, dst, sel_s.at[idx], sel_r.at[idx], {"xo": xx, "team": cc})
                )
    for cp in sel_copies:
        cp.start()

    for s in range(2):
        @pl.when(zz == s)
        def _(s=s):
            for dz in range(1, 4):
                for cp in bias_copies(s, dz):
                    cp.start()
            for cp in bias_own(s):
                cp.start()

    zero_k = jnp.zeros((own_tok, 256), bf16)
    for ref in (kb, vb):
        for slot in range(2):
            ref[slot, 0:own_tok, :] = zero_k
            ref[slot, seq + own_tok : seq + 2 * own_tok, :] = zero_k
    smb[...] = jnp.zeros_like(smb)
    for cp in vectors_in():
        cp.wait()
    point("x_wait")
    a2a_in_wait(a2a_in(0, x_hbm))

    def natural(i):
        return pl.multiple_of((i // 4) * half + c * tile + (i % 4) * own_tok, own_tok)

    def ln1_body(i, carry):
        rows = xin[pl.ds(pl.multiple_of(i * own_tok, own_tok), own_tok), :].astype(f32)
        unit, _ = ln_parts(rows)
        nrm[pl.ds(natural(i), own_tok), :] = (unit * vec(0) + vec(1)).astype(bf16)
        return carry

    point("ln1")
    lax.fori_loop(0, 8, ln1_body, 0)
    for j in range(2):
        swap(nrm, j, T_NRM).start()

    for cp in sel_copies:
        cp.wait()
    lane_seq = lax.broadcasted_iota(jnp.int32, selraw.shape[1:], 2)
    sub = lax.broadcasted_iota(jnp.int32, (SEL, 256), 0)
    lane = lax.broadcasted_iota(jnp.int32, (SEL, 256), 1)
    inner = (lane % KB).astype(f32)
    for g in range(4):
        chosen = jnp.sum(jnp.where(lane_seq == my_seq, selraw[g].astype(f32), 0.0), axis=2, keepdims=True)
        every = jnp.zeros((1, 256), f32)
        for b in range(4):
            keys = jnp.broadcast_to(chosen[b], (SEL, 256)) * KB + inner
            here = jnp.sum(jnp.where(lane // KB == sub + 192 // KB, keys, 0.0), axis=0, keepdims=True)
            selb[g, b : b + 1, :] = here.astype(jnp.int32)
            every = every + jnp.sum(
                jnp.where(lane // KB == sub + b * SEL, keys, 0.0), axis=0, keepdims=True
            )
        selb[g, 4:5, :] = every.astype(jnp.int32)

    for s in range(2):
        @pl.when(zz != s)
        def _(s=s):
            for cp in bias_copies(s, 1):
                cp.wait_recv()

        @pl.when(zz == s)
        def _(s=s):
            for cp in bias_own(s):
                cp.wait()

    point("nrm_wait")
    for j in range(2):
        swap_wait(nrm, j, T_NRM)
    for s in range(2):
        s3(CH_A, s)

    gate_lane = (lane256 >= 192) & (lane256 < 195)

    gap = jnp.zeros((1, 640 - 3 * head_cols), f32)
    none = jnp.zeros((1, head_cols), f32)
    mix_bias = [
        jnp.concatenate([qvbb[slot, 0:1, :], none, qvbb[slot, 1:2, :], gap], axis=1) for slot in range(2)
    ]

    def qkv_body(i, carry):
        points("qkv", i, 4)
        at = pl.ds(pl.multiple_of(i * tile, tile), tile)
        padded = pl.ds(pl.multiple_of(i * tile + own_tok, own_tok), tile)
        rows = nrm[at, :]
        for slot in range(2):
            mixed = dot(rows, wa[slot], 1, 0)
            scr[slot, at, :] = mixed[:, 512:640]
            mixed = mixed + mix_bias[slot]
            q = mixed[:, 0:256].astype(bf16).astype(f32) * 0.125
            q = jnp.where(lane256 < 192, q, jnp.where(gate_lane, 1.0, 0.0))
            qb[slot, at, :] = q.astype(bf16)
            keys = pltpu.roll(mixed[:, 128:384], 192, 1)
            score = mixed[:, 512:640]
            gate = -(jnp.maximum(-score, 0.0) + jnp.log(1.0 + jnp.exp(-jnp.abs(score))))
            gate = jnp.concatenate([gate, gate], axis=1)
            keys = jnp.where(lane256 < 192, keys, jnp.where(gate_lane, gate, 0.0))
            kb[slot, padded, :] = keys.astype(bf16)
            vb[slot, padded, :] = jnp.where(lane256 < 192, mixed[:, 384:640], 0.0).astype(bf16)
        return carry

    lax.fori_loop(0, 4, qkv_body, 0)

    key_iota = lax.broadcasted_iota(jnp.int32, (seq, 256), 0)

    def one_hot(g):
        return jnp.where(key_iota == selb[g, 4:5, :], 1.0, 0.0).astype(bf16)

    def gather_body(g, carry):
        points("gat", g, 4)
        hot = one_hot(g)
        at = pl.ds(pl.multiple_of(g * 256, 256), 256)
        for slot in range(2):
            ksel[slot, at, :] = dot(hot, kb[slot, own_tok : own_tok + seq, :], 0, 0).astype(bf16)
            vsel[slot, at, :] = dot(hot, vb[slot, own_tok : own_tok + seq, :], 0, 0).astype(bf16)
        return carry

    lax.fori_loop(0, 4, gather_body, 0)

    prefix_end = pref[my_seq]

    def windows(b, slot):
        near = pl.ds(pl.multiple_of(b * 64, 64), 192)
        at = pl.ds(pl.multiple_of(b * 64, 64), 64)
        keys = jnp.concatenate([kb[slot, near, :], ksel[slot, at, :]], axis=0)
        vals = jnp.concatenate([vb[slot, near, :], vsel[slot, at, :]], axis=0)
        return at, near, keys, vals

    def fwd_body(i, carry):
        for n in range(2):
            points("fwd", 2 * i + n, 16, n, 2)
        for b in (i, i + 8):
            picks = selb[b // 4, pl.ds(b % 4, 1), :]
            key_pos = jnp.where(lane256 < 192, (b - 1) * 64 + lane256, picks)
            query_pos = b * 64 + lax.broadcasted_iota(jnp.int32, (64, 256), 0)
            key_pos = jnp.broadcast_to(key_pos, (64, 256))
            inside = (key_pos >= 0) & (key_pos < seq)
            permitted = (key_pos <= query_pos) | ((query_pos < prefix_end) & (key_pos < prefix_end))
            near_by = jnp.abs(query_pos - key_pos) < 64
            is_near = jnp.broadcast_to(lane256 < 192, (64, 256))
            allowed = inside & permitted & (near_by == is_near)
            fill = jnp.where(allowed, 0.0, MASKED)
            for slot in range(2):
                at, near, keys, vals = windows(b, slot)
                stacked = stack3(qb[slot, at, :], q_rows)
                logits = dot(stacked, keys, 1, 1).reshape(3, 64, 256) + fill[None]
                top = jnp.max(logits, axis=-1, keepdims=True)
                p = jnp.exp(logits - top)
                p = p * (1.0 / jnp.sum(p, axis=-1, keepdims=True))
                p = p.reshape(192, 256).astype(bf16)
                pr[b * 2 + slot] = p
                att[slot, at, :] = fold3(dot(p, vals, 1, 0)).astype(bf16)
        return carry

    lax.fori_loop(0, 8, fwd_body, 0)

    point("brs")
    for s in range(2):
        s3(CH_B, s)

    def branch_tile(rows):
        return dot(att[0, rows, :], wb[0], 1, 1) + dot(att[1, rows, :], wb[1], 1, 1)

    for j in range(2):
        st[0, j] = branch_tile(chunk(j, 1 - c)).astype(bf16)
        part(0, j, T_BR).start()
    for j in range(2):
        point("br" + str(j))
        own = branch_tile(chunk(j, c))
        at = slice(j * tile, (j + 1) * tile)
        part(0, j, T_BR).wait_recv()
        mid[at, :] = (
            xin[at, :].astype(f32) + own + rv[0, j].astype(f32) + vec(2)
        )

        def ln2_body(i, carry, j=j):
            rows = mid[pl.ds(pl.multiple_of(j * tile + i * own_tok, own_tok), own_tok), :]
            unit, _ = ln_parts(rows)
            n2[pl.ds(natural(j * 4 + i), own_tok), :] = (unit * vec(3) + vec(4)).astype(bf16)
            return carry

        lax.fori_loop(0, 4, ln2_body, 0)
        swap(n2, j, T_N2).start()

    point("mlpa0")
    for k in (CH_1, CH_2):
        s3(k, 0)
    for j in range(2):
        swap_wait(cot, j, T_COT)
        part(0, j, T_BR).wait_send()
        swap_wait(n2, j, T_N2)

    def mlp_tile(rows, slot):
        before = dot(n2[rows, :], w1[slot], 1, 0) + fbs[slot][...].reshape(1, width)
        d_act = dot(cot[rows, :], w2[slot], 1, 0)
        square = before * before
        t = jnp.tanh(0.7978845608028654 * before * (1.0 + 0.044715 * square))
        gate = 0.5 * (1.0 + t)
        slope = gate + 0.5 * before * (1.0 - t * t) * (
            0.7978845608028654 * (1.0 + 0.134145 * square)
        )
        low = (before * gate).astype(bf16)
        low_back = (d_act * slope).astype(bf16)
        act[slot, rows, :] = low
        dbf[slot, rows, :] = low_back
        smb[pl.ds(8 + slot + c * (3 - 2 * slot), 1), :] += jnp.sum(
            low_back.astype(f32), axis=0, keepdims=True
        )
        return dot(low, w2[slot], 1, 1), dot(low_back, w1[slot], 1, 1)

    def first_mlp(i, carry):
        @pl.when(i > 0)
        def _():
            points("mlpa", i, 4)

        at = pl.ds(pl.multiple_of(i * tile, tile), tile)
        out, back = mlp_tile(at, 0)
        acc[0, at, :] = out
        acc[1, at, :] = back
        return carry

    lax.fori_loop(0, 4, first_mlp, 0)

    def weight_grad(g, slot, left, right):
        def body(m, carry):
            at = pl.ds(pl.multiple_of(m * 256, 256), 256)
            g[slot, at, :] = dot(left[:, at], right, 0, 0).astype(bf16)
            return carry

        lax.fori_loop(0, 3, body, 0)

    def ff_grads(slot):
        for k, name, left, right in ((CH_2, "g2", cot, act), (CH_1, "g1", n2, dbf)):
            point(name + str(slot))
            ag_drain(k, slot)
            weight_grad(grads[k], slot, left, right[slot])
            r1(k, slot)

    def peer_mlp(j, carry):
        @pl.when(j == 1)
        def _():
            point("pm1")

        rows = chunk(j, 1 - c)
        out, back = mlp_tile(rows, 1)
        st[0, j] = (acc[0, rows, :] + out).astype(bf16)
        st[1, j] = (acc[1, rows, :] + back).astype(bf16)
        part(0, j, T_MLP).start()
        part(1, j, T_DN2).start()
        return carry

    if not PEER_FIRST:
        ff_grads(0)
    point("pm0")
    for k in (CH_1, CH_2):
        s3(k, 1)
    lax.fori_loop(0, 2, peer_mlp, 0)
    if PEER_FIRST:
        ff_grads(0)

    def own_mlp(j, carry):
        points("om", j, 2)
        rows = chunk(j, c)
        out, back = mlp_tile(rows, 1)
        out = acc[0, rows, :] + out
        back = acc[1, rows, :] + back
        at = pl.ds(pl.multiple_of(j * tile, tile), tile)
        part(0, j, T_MLP).wait_recv()
        part(1, j, T_DN2).wait_recv()
        stage[at, :] = (mid[at, :] + out + rv[0, j].astype(f32) + vec(5)).astype(bf16)
        dnr[...] = back + rv[1, j].astype(f32)

        def ln2_back(i, carry):
            here = pl.ds(pl.multiple_of(j * tile + i * own_tok, own_tok), own_tok)
            nat = pl.ds(natural(j * 4 + i), own_tok)
            unit, inverse = ln_parts(mid[here, :])
            up_grad = dnr[pl.ds(pl.multiple_of(i * own_tok, own_tok), own_tok), :]
            grad_rows = cot[nat, :].astype(f32)
            d_mid = grad_rows + ln_back(up_grad, unit, inverse, vec(3))
            mid[here, :] = d_mid
            dml[nat, :] = d_mid.astype(bf16)
            smb[2:3, :] += jnp.sum(d_mid, axis=0, keepdims=True)
            smb[3:4, :] += jnp.sum(up_grad * unit, axis=0, keepdims=True)
            smb[4:5, :] += jnp.sum(up_grad, axis=0, keepdims=True)
            smb[5:6, :] += jnp.sum(grad_rows, axis=0, keepdims=True)
            return carry

        lax.fori_loop(0, 4, ln2_back, 0)
        swap(dml, j, T_DML).start()
        return carry

    lax.fori_loop(0, 2, own_mlp, 0)

    if not FF_GRADS_LATER:
        ff_grads(1)
    point("datt")
    for j in range(2):
        swap_wait(dml, j, T_DML)

    def datt_body(i, carry):
        at = pl.ds(pl.multiple_of(i * tile, tile), tile)
        for slot in range(2):
            datt[slot, at, :] = dot(dml[at, :], wb[slot], 1, 0).astype(bf16)
        return carry

    lax.fori_loop(0, 4, datt_body, 0)
    for slot in range(2):
        point("gb" + str(slot))
        ag_drain(CH_B, slot)
        weight_grad(wb, slot, dml, att[slot])
        r1(CH_B, slot)
    if FF_GRADS_LATER:
        ff_grads(1)
    acc[:, :, 0:512] = jnp.zeros((2, seq + 2 * own_tok, 512), f32)

    def bwd_body(b, carry):
        points("bwd", b, 16)
        for slot in range(2):
            at, near, keys, vals = windows(b, slot)
            q_stack = stack3(qb[slot, at, :], q_rows)
            d_stack = stack3(datt[slot, at, :], head_rows)
            p_low = pr[b * 2 + slot]
            p = p_low.astype(f32)
            pdp = p * dot(d_stack, vals, 1, 1)
            dl = (pdp - p * jnp.sum(pdp, axis=-1, keepdims=True)).astype(bf16)
            dbf[slot, at, 512:768] = (fold3(dot(dl, keys, 1, 0)) * 0.125).astype(bf16)
            dk = dot(dl, q_stack, 0, 0)
            dv = dot(p_low, d_stack, 0, 0)
            side = slice(slot * 256, slot * 256 + 256)
            acc[0, near, side] += dk[0:192]
            acc[1, near, side] += dv[0:192]
            dbf[slot, at, 0:256] = dk[192:256].astype(bf16)
            dbf[slot, at, 256:512] = dv[192:256].astype(bf16)
        return carry

    lax.fori_loop(0, 16, bwd_body, 0)
    point("mix")

    sel_pos = jnp.concatenate([selb[g, 4:5, :] for g in range(4)], axis=1)

    def mix_body(i, carry):
        at = pl.ds(pl.multiple_of(i * tile, tile), tile)
        padded = pl.ds(pl.multiple_of(i * tile + own_tok, own_tok), tile)
        key_at = i * tile + lax.broadcasted_iota(jnp.int32, (tile, seq), 0)
        hot = jnp.where(key_at == sel_pos, 1.0, 0.0).astype(bf16)
        for slot in range(2):
            far = dot(hot, dbf[slot, :, 0:512], 1, 0)
            dk = (acc[0, padded, slot * 256 : slot * 256 + 256] + far[:, 0:256]).astype(bf16).astype(f32)
            dv = (acc[1, padded, slot * 256 : slot * 256 + 256] + far[:, 256:512]).astype(bf16).astype(f32)
            dq = dbf[slot, at, 512:768].astype(f32)
            turned = pltpu.roll(dk, 64, 1)
            d_score = dk[:, 128:256] / (1.0 + jnp.exp(scr[slot, at, :]))
            lane128 = lane256[:, 0:128]
            v1 = jnp.where(lane128 < 64, dq[:, 128:256], turned[:, 0:128])
            v4 = jnp.where(lane128 < 64, dv[:, 128:256], jnp.where(lane128 < 67, d_score, 0.0))
            mix = jnp.concatenate([dq[:, 0:128], v1, turned[:, 128:256], dv[:, 0:128], v4], axis=1)
            mix = mix.astype(bf16)
            act[slot, at, 0:640] = mix
            smb[pl.ds(12 + slot + c * (3 - 2 * slot), 1), 0:640] += jnp.sum(
                mix.astype(f32), axis=0, keepdims=True
            )
        return carry

    lax.fori_loop(0, 4, mix_body, 0)
    def qkv_grads():
        for slot in range(2):
            point("ga" + str(slot))
            weight_grad(ga, slot, nrm, act[slot, :, 0:640])
            r1(CH_A, slot)

    if not QKV_GRADS_LAST:
        qkv_grads()
    point("dn0")
    for j in range(2):
        part(0, j, T_MLP).wait_send()
        part(1, j, T_DN2).wait_send()

    def dnorm_tile(rows):
        return dot(act[0, rows, 0:640], wa[0], 1, 1) + dot(act[1, rows, 0:640], wa[1], 1, 1)

    for j in range(2):
        st[0, j] = dnorm_tile(chunk(j, 1 - c)).astype(bf16)
        part(0, j, T_DNR).start()

    res_copies = a2a_out(0, stage)
    res_copies[0].wait()
    for cp in res_copies[1:]:
        cp.wait_send()

    def own_dnorm(j, carry):
        points("od", j, 2)
        dnr[...] = dnorm_tile(chunk(j, c))
        part(0, j, T_DNR).wait_recv()

        def ln1_back(i, carry):
            here = pl.ds(pl.multiple_of(j * tile + i * own_tok, own_tok), own_tok)
            local = pl.ds(pl.multiple_of(i * own_tok, own_tok), own_tok)
            unit, inverse = ln_parts(xin[here, :].astype(f32))
            up_grad = dnr[local, :] + rv[0, j, local, :].astype(f32)
            grad = mid[here, :] + ln_back(up_grad, unit, inverse, vec(0))
            stage[here, :] = grad.astype(bf16)
            smb[0:1, :] += jnp.sum(up_grad * unit, axis=0, keepdims=True)
            smb[1:2, :] += jnp.sum(up_grad, axis=0, keepdims=True)
            return carry

        lax.fori_loop(0, 4, ln1_back, 0)
        return carry

    lax.fori_loop(0, 2, own_dnorm, 0)
    ing_copies = a2a_out(1, stage)
    for cp in ing_copies:
        cp.start()
    if QKV_GRADS_LAST:
        qkv_grads()
    for i in range(24):
        point("e" + str(i))

    small = pltpu.make_async_copy(smb, sm_o, gout.at[4])
    small.start()
    for k in (CH_2, CH_1, CH_B, CH_A):
        rp_wait(k)
    for s in range(2):
        ag_drain(CH_A, s)
    for k in range(4):
        rs_drain(k)
    small.wait()
    for j in range(2):
        for buf, idx in ((nrm, T_NRM), (cot, T_COT), (n2, T_N2), (dml, T_DML)):
            swap(buf, j, idx).wait_send()
        part(0, j, T_DNR).wait_send()

    for s in range(2):
        @pl.when(zz == s)
        def _(s=s):
            for dz in range(1, 4):
                for cp in bias_copies(s, dz):
                    cp.wait_send()

    for cp in res_copies[1:]:
        cp.wait_recv()
    for cp in ing_copies:
        cp.wait()


def finish_kernel(
    res_i, ing_i, ga_i, gb_i, g1_i, g2_i, sm_i,
    res_o, ing_o, n1g, n1b, wq_o, qvb, ws_o, wo_o, ob, n2g, n2b, g1_o, f1b, g2_o, f2b,
    res, ing, sem,
):
    def moves(way, i):
        return [
            pltpu.make_async_copy(*((a, b) if way == 0 else (b, d)), sem.at[way, n, i])
            for n, (a, b, d) in enumerate(
                (r.at[i] for r in refs) for refs in ((res_i, res, res_o), (ing_i, ing, ing_o))
            )
        ]

    seqs = res.shape[0]
    for i in range(seqs):
        for cp in moves(0, i):
            cp.start()
    for i in range(seqs):
        for come, go in zip(moves(0, i), moves(1, i)):
            come.wait()
            go.start()
    z = lax.axis_index("tp")
    for row, ref in enumerate((n1g, n1b, ob, n2g, n2b, f2b)):
        ref[...] = sm_i[row, :]
    f1b[...] = sm_i[pl.ds(8 + z, 1), :][0]
    cols = wo_o.shape[1]
    mixed = sm_i[pl.ds(12 + z, 1), :]
    qvb[0:1, :] = mixed[:, 0:cols]
    qvb[1:2, :] = mixed[:, 2 * cols : 3 * cols]
    g1_o[...] = g1_i[...].astype(f32)
    g2_o[...] = g2_i[...].astype(f32)
    wo_o[...] = gb_i[:, 0:cols].astype(f32)
    i = lax.broadcasted_iota(jnp.int32, (640, cols), 0)
    j = lax.broadcasted_iota(jnp.int32, (640, cols), 1)
    for part in range(3):
        wq_o[part] = dot(ga_i[...], jnp.where(i == j + part * cols, 1.0, 0.0).astype(bf16), 1, 0)
    heads = ws_o.shape[0]
    i = lax.broadcasted_iota(jnp.int32, (heads, 640), 0)
    j = lax.broadcasted_iota(jnp.int32, (heads, 640), 1)
    ws_o[...] = dot(jnp.where(j == i + 3 * cols, 1.0, 0.0).astype(bf16), ga_i[...], 1, 1)
    for i in range(seqs):
        for cp in moves(1, i):
            cp.wait()


def fast_layer(
    inputs, norm1_gain, norm1_bias, qkv_weight, qv_bias, score_weight, out_weight, out_bias,
    norm2_gain, norm2_bias, fc1_weight, fc1_bias, fc2_weight, fc2_bias, prefix, selected, cotangent,
):
    shard, _, cols = qkv_weight.shape
    heads = score_weight.shape[1]
    width = inputs.shape[2]
    own_tok = inputs.shape[1]
    seqs = inputs.shape[0]
    seq = 16 * own_tok
    vm = pltpu.VMEM
    ncols = (640, 256, 768, 768)
    hbm = pl.BlockSpec(memory_space=pl.ANY)
    vmem = pl.BlockSpec(memory_space=pltpu.VMEM)
    dma = pltpu.SemaphoreType.DMA
    outs = pl.pallas_call(
        layer_kernel,
        out_shape=[
            jax.ShapeDtypeStruct(inputs.shape, bf16),
            jax.ShapeDtypeStruct(inputs.shape, bf16),
        ]
        + [jax.ShapeDtypeStruct((shard, n), bf16) for n in ncols]
        + [jax.ShapeDtypeStruct((16, width), f32)],
        in_specs=[hbm] * 16 + [pl.BlockSpec(memory_space=pltpu.SMEM)],
        out_specs=[hbm] * 7,
        scratch_shapes=[vm((2, 768, n), bf16) for n in ncols]
        + [vm((2, 768, 640), bf16)]
        + [vm((6, 2 * shard, n), bf16) for n in ncols]
        + [vm((2, 768 if {(k, 0), (k, 1)} & RS_Z_FIRST else 2 * shard, n), bf16) for k, n in enumerate(ncols)]
        + [vm((shard, n), bf16) for n in ncols]
        + [
            vm((seq // 2, width), bf16),
            vm((seq, width), bf16),
            vm((seq, width), bf16),
            vm((2, seq, 256), bf16),
            vm((2, seq + 2 * own_tok, 256), bf16),
            vm((2, seq + 2 * own_tok, 256), bf16),
            vm((2, seq, 256), bf16),
            vm((2, seq, 256), bf16),
            vm((32, 192, 256), bf16),
            vm((2, seq, 256), bf16),
            vm((seq // 2, width), f32),
            vm((seq, width), bf16),
            vm((2, seq, 768), bf16),
            vm((2, seq, 768), bf16),
            vm((2, 2, seq // 4, width), bf16),
            vm((2, 2, seq // 4, width), bf16),
            vm((seq // 4, width), f32),
            vm((seq, width), bf16),
            vm((2, seq, 256), bf16),
            vm((2, seq + 2 * own_tok, 768), f32),
            vm((2, seq, 128), f32),
            vm((seq // 2, width), bf16),
            vm((4, 4, 4, seqs), jnp.int32),
            vm((4, 8, 256), jnp.int32),
            vm((3, shard, cols), bf16),
            vm((heads, shard), bf16),
            vm((shard, cols), bf16),
            vm((shard, 640), bf16),
            vm((shard, 256), bf16),
        ]
        + [vm((width,), f32)] * 8
        + [
            vm((2, 2, cols), f32),
            vm((16, 768), f32),
            vm((5, 16, 768), f32),
            dma((2, 8)), dma((2, 8)), dma((2, 8)), dma((2, 8)),
            dma((4, 12)), dma((4, 9)), dma((4, 9)), dma((4, 10)),
            dma((16,)), dma((16,)), dma((4,)), dma((4,)), dma((2, 4)), dma((2, 2)),
            dma((5,)), dma((5,)), dma((13,)), dma((5,)),
        ],
        compiler_params=pltpu.CompilerParams(
            collective_id=0, has_side_effects=True, vmem_limit_bytes=67043328
        ),
    )(
        inputs, cotangent, jnp.transpose(qkv_weight, (1, 0, 2)), jnp.transpose(score_weight), out_weight,
        fc1_weight, fc2_weight, jnp.transpose(selected, (1, 2, 0)), norm1_gain, norm1_bias,
        out_bias, norm2_gain, norm2_bias, fc2_bias, fc1_bias, qv_bias, prefix,
    )
    line = jax.ShapeDtypeStruct((width,), f32)
    square = jax.ShapeDtypeStruct((shard, 768), f32)
    done = pl.pallas_call(
        finish_kernel,
        out_shape=[
            jax.ShapeDtypeStruct(inputs.shape, bf16), jax.ShapeDtypeStruct(inputs.shape, bf16), line, line,
            jax.ShapeDtypeStruct((3, shard, cols), f32), jax.ShapeDtypeStruct((2, cols), f32),
            jax.ShapeDtypeStruct((heads, shard), f32), jax.ShapeDtypeStruct((shard, cols), f32),
            line, line, line, square, line, square, line,
        ],
        in_specs=[hbm, hbm] + [vmem] * 5,
        out_specs=[hbm, hbm] + [vmem] * 13,
        scratch_shapes=[vm(inputs.shape, bf16), vm(inputs.shape, bf16), dma((2, 2, seqs))],
    )(*outs)
    done = list(done)
    done[4] = jnp.transpose(done[4], (1, 0, 2))
    done[6] = jnp.transpose(done[6])
    return tuple(done)


def general(mesh):
    placed = (
        P("fsdp", ("ctx", "tp"), None),
        P(),
        P(),
        P(("fsdp", "ctx"), None, "tp"),
        P(None, "tp"),
        P(("fsdp", "ctx"), "tp"),
        P(("fsdp", "ctx"), "tp"),
        P(),
        P(),
        P(),
        P(("fsdp", "ctx"), "tp"),
        P("tp"),
        P(("fsdp", "ctx"), "tp"),
        P(),
        P("fsdp"),
        P("fsdp", "ctx", None),
        P("fsdp", ("ctx", "tp"), None),
    )
    return jax.shard_map(
        shards,
        mesh=mesh,
        in_specs=placed,
        out_specs=(
            P("fsdp", ("ctx", "tp"), None),
            P("fsdp", ("ctx", "tp"), None),
            P(),
            P(),
            P(("fsdp", "ctx"), None, "tp"),
            P(None, "tp"),
            P(("fsdp", "ctx"), "tp"),
            P(("fsdp", "ctx"), "tp"),
            P(),
            P(),
            P(),
            P(("fsdp", "ctx"), "tp"),
            P("tp"),
            P(("fsdp", "ctx"), "tp"),
            P(),
        ),
        check_vma=False,
    )


def solution(mesh):
    shape = dict(mesh.shape)
    if shape != {"fsdp": 2, "ctx": 4, "tp": 4}:
        return general(mesh)
    split = Mesh(mesh.devices.reshape(2, 2, 2, 4), ("fsdp", "xo", "team", "tp"))
    ctx = ("xo", "team")
    rows = ("fsdp", "xo", "team")
    tokens = P("fsdp", ("xo", "team", "tp"), None)
    placed = (
        tokens, P(), P(), P(rows, None, "tp"), P(None, "tp"), P(rows, "tp"), P(rows, "tp"), P(), P(), P(),
        P(rows, "tp"), P("tp"), P(rows, "tp"), P(), P("fsdp"), P("fsdp", ctx, None), tokens,
    )
    given = (
        tokens, tokens, P(), P(), P(rows, None, "tp"), P(None, "tp"), P(rows, "tp"), P(rows, "tp"),
        P(), P(), P(), P(rows, "tp"), P("tp"), P(rows, "tp"), P(),
    )
    return jax.shard_map(fast_layer, mesh=split, in_specs=placed, out_specs=given, check_vma=False)
```
